32 devices in a mesh: row: 8 (over z, y), col: 4 (over x, core).
Axes of the slice: x: 2, y: 2, z: 4, core: 2. Of those that a mesh axis runs over, the one named last changes fastest.
Arguments:
- tokens: bfloat16 [4096, 2560], P('row', 'col'), may hold values from -6 to 6
- document_ids: int32 [4096], replicated, may hold values from 0 to 3, never falling along the last dimension, each value on 1 to 2000 neighbouring positions
- gain_first: float32 [2560], P('row'), may hold values from 0.5 to 1.5
- query_down: float32 [2560, 768], P('row'), may hold values from -0.125 to 0.125
- query_gain: float32 [768], P('row'), may hold values from 0.5 to 1.5
- latent_down: float32 [2560, 288], P('row'), may hold values from -0.125 to 0.125
- latent_gain: float32 [256], P('row'), may hold values from 0.5 to 1.5
- query_up: float32 [768, 3840], P('row', 'col'), may hold values from -0.21875 to 0.21875
- latent_up: float32 [256, 5120], P('row', 'col'), may hold values from -0.375 to 0.375
- output_weight: float32 [2560, 2560], P('col', 'row'), may hold values from -3 to 3
- gain_second: float32 [2560], P('row'), may hold values from 0.5 to 1.5
- gate_weight: float32 [2560, 6400], P('row', 'col'), may hold values from -0.125 to 0.125
- up_weight: float32 [2560, 6400], P('row', 'col'), may hold values from -0.125 to 0.125
- down_weight: float32 [6400, 2560], P('col', 'row'), may hold values from -1 to 1
- cotangent: float32 [4096, 2560], P('row', 'col'), may hold values from -6 to 6
Outputs:
- result: float32 [4096, 2560], P('row', 'col')
- back_tokens: float32 [4096, 2560], P('row', 'col')
- slope_gain_first: float32 [2560], P('row')
- slope_query_down: float32 [2560, 768], P('row')
- slope_query_gain: float32 [768], P('row')
- slope_latent_down: float32 [2560, 288], P('row')
- slope_latent_gain: float32 [256], P('row')
- slope_query_up: float32 [768, 3840], P('row', 'col')
- slope_latent_up: float32 [256, 5120], P('row', 'col')
- slope_output: float32 [2560, 2560], P('col', 'row')
- slope_gain_second: float32 [2560], P('row')
- slope_gate: float32 [2560, 6400], P('row', 'col')
- slope_up: float32 [2560, 6400], P('row', 'col')
- slope_down: float32 [6400, 2560], P('col', 'row')
The draws below stay inside these ranges and needn't reach their ends.
Inputs may be any that keep to these rules, and one draw needn't show every extreme that they name: `document_ids`: never falls along the tokens; each document has 1 to 2000 tokens and one has exactly 2000.
All inputs are finite; a program needn't handle non-finite values.
Results may differ from the reference program's by a relative error of at most 0.018.
The reference program's roundings to bfloat16 on the way count: a program that leaves them out, or rounds other values in their place, can miss the bound.
Values may be sent and summed in bfloat16 or wider, within the bound.
A program may use at most 384 MiB of HBM per device.

```python
import math
import jax
import jax.numpy as jnp
import numpy as np
from jax import lax

D = 2560
H = 40
DN = 64
DR = 32
DV = 64
QR = 768
KR = 256
FF = 6400
SEQ_LEN = 4096
DOC_MOST = 2000
TOKENS = 4096
DOCS = 4


def level_of(own_key, dims, split, smallest, largest):
    factor_of, own = 1.0, jax.random.fold_in(own_key, 6)
    for position, blocks in split:
        steps = jnp.exp(jax.random.uniform(jax.random.fold_in(own, position), (blocks,), jnp.float32, smallest / len(split), largest / len(split)))
        factor_of = factor_of * jnp.repeat(steps, dims[position] // blocks).reshape([-1 if axis == position else 1 for axis in range(len(dims))])
    return factor_of


def split_up(number_of, total, reach, slope):
    portions = [(1 << 20) // math.isqrt(grade ** slope) + 1 for grade in range(2, number_of + 1)]
    surplus, counts = total - reach - (number_of - 1), [1] * (number_of - 1)
    while surplus > 0:
        free = [i for i in range(number_of - 1) if counts[i] < reach]
        pool, left = sum([portions[i] for i in free]), surplus
        for i in free:
            addition = min(reach - counts[i], max(1, left * portions[i] // pool), surplus)
            counts[i] = counts[i] + addition
            surplus = surplus - addition
    return np.array([reach] + counts)


def uneven(key, amount, total, reach, lean):
    if amount == 2:
        one = jax.random.randint(key, (), max(1, total - reach), min(reach, total - 1) + 1)
        return jnp.stack([one, total - one])
    lengths = jnp.asarray(split_up(amount, total, reach, lean), jnp.int32)
    pairs = (amount - 1) // 2
    donor, taker = lengths[1:1 + 2 * pairs:2], lengths[2:2 + 2 * pairs:2]
    slack = jnp.minimum(donor - 1, reach - taker)
    passed = jax.random.randint(jax.random.fold_in(key, 1), (pairs,), 0, 1 << 20) % (slack + 1)
    lengths = lengths.at[1:1 + 2 * pairs:2].set(donor - passed).at[2:2 + 2 * pairs:2].set(taker + passed)
    return lengths[jax.random.permutation(jax.random.fold_in(key, 2), amount)]


def scatter_about(own_key, shape, spread, reach, cuts=(), kind=jnp.bfloat16):
    array = spread * jax.random.normal(own_key, shape, jnp.float32)
    if cuts:
        array = array * level_of(own_key, shape, cuts, -0.22, 0.18)
    return jnp.clip(array, -reach, reach).astype(kind)


def setup_inputs(seed: int = 0) -> dict:
    splits = jax.random.split(jax.random.key(seed), 16)
    tokens = scatter_about(splits[0], (TOKENS, D), 1.0, 6.0, ((0, 8), (1, 4)))
    document_ids = jnp.searchsorted(jnp.cumsum(uneven(splits[1], DOCS, TOKENS, DOC_MOST, 2)), jnp.arange(TOKENS), side="right").astype(jnp.int32)
    gain_first = jnp.clip(1.0 + 0.1 * jax.random.normal(splits[2], (D,), jnp.float32), 0.5, 1.5)
    query_down = scatter_about(splits[3], (D, QR), D ** -0.5, 0.125, ((0, 8),), jnp.float32)
    query_gain = jnp.clip(1.0 + 0.1 * jax.random.normal(splits[4], (QR,), jnp.float32), 0.5, 1.5)
    latent_down = scatter_about(splits[5], (D, KR + DR), D ** -0.5, 0.125, ((0, 8),), jnp.float32)
    latent_gain = jnp.clip(1.0 + 0.1 * jax.random.normal(splits[6], (KR,), jnp.float32), 0.5, 1.5)
    query_up = scatter_about(splits[7], (QR, H * (DN + DR)), QR ** -0.5, 0.21875, ((0, 8), (1, 4)), jnp.float32)
    latent_up = scatter_about(splits[8], (KR, H * (DN + DV)), KR ** -0.5, 0.375, ((0, 8), (1, 4)), jnp.float32)
    output_weight = scatter_about(splits[9], (H * DV, D), 4 ** -0.5, 3.0, ((0, 4), (1, 8)), jnp.float32)
    gain_second = jnp.clip(1.0 + 0.1 * jax.random.normal(splits[10], (D,), jnp.float32), 0.5, 1.5)
    gate_weight = scatter_about(splits[11], (D, FF), D ** -0.5, 0.125, ((0, 8), (1, 4)), jnp.float32)
    up_weight = scatter_about(splits[12], (D, FF), D ** -0.5, 0.125, ((0, 8), (1, 4)), jnp.float32)
    down_weight = scatter_about(splits[13], (FF, D), (max(FF // 200, 1)) ** -0.5, 1.0, ((0, 4), (1, 8)), jnp.float32)
    cotangent = scatter_about(splits[14], (TOKENS, D), 1.0, 6.0, ((0, 8), (1, 4)), jnp.float32)
    return dict(tokens=tokens, document_ids=document_ids, gain_first=gain_first, query_down=query_down, query_gain=query_gain, latent_down=latent_down, latent_gain=latent_gain, query_up=query_up, latent_up=latent_up, output_weight=output_weight, gain_second=gain_second, gate_weight=gate_weight, up_weight=up_weight, down_weight=down_weight, cotangent=cotangent)


EPS = 1e-05
RES = 1.4 / math.sqrt(62.0)
THETA = 10000.0
NEG = -1e+30
HIGH = lax.Precision.HIGHEST

@jax.custom_vjp
def low(v):
    return lax.optimization_barrier(v.astype(jnp.bfloat16)).astype(jnp.float32)

@jax.custom_vjp
def low_back(v):
    return v

def low_keep(v):
    return (low(v), None)

def low_pass(kept, grad):
    return (grad,)

def back_keep(v):
    return (v, None)

def back_low(kept, grad):
    return (low(grad),)
low.defvjp(low_keep, low_pass)
low_back.defvjp(back_keep, back_low)

def normalize(value, gain):
    return value * lax.rsqrt(lax.optimization_barrier(jnp.mean(value * value, axis=-1, keepdims=True)) + EPS) * gain

def angles(count):
    place = (jnp.arange(count, dtype=jnp.int32) % SEQ_LEN).astype(jnp.float32)
    half = DR // 2
    freq = jnp.exp(jnp.arange(half, dtype=jnp.float32) * (-math.log(THETA) / half))
    turn = place[:, None] * freq[None, :]
    return (jnp.cos(turn), jnp.sin(turn))

def rotate(value, cosine, sine):
    half = value.shape[-1] // 2
    front, behind = (value[..., :half], value[..., half:])
    return jnp.concatenate([front * cosine - behind * sine, behind * cosine + front * sine], axis=-1)

def product(left, right):
    return jnp.dot(left, right, precision=HIGH)

def attention(queries, keys, values, document_ids):
    seqs = TOKENS // SEQ_LEN
    block = min(512, SEQ_LEN)
    blocks = SEQ_LEN // block
    scale = (DN + DR) ** (-0.5)
    query_seq = queries.reshape(seqs, blocks, block, H, DN + DR)
    key_seq = keys.reshape(seqs, SEQ_LEN, H, DN + DR)
    value_seq = values.reshape(seqs, SEQ_LEN, H, DV)
    doc_seq = document_ids.reshape(seqs, SEQ_LEN)

    def one_sequence(carry, item):
        query_blocks, key_all, value_all, doc_all = item
        doc_blocks = doc_all.reshape(blocks, block)
        firsts = jnp.arange(blocks, dtype=jnp.int32) * block

        def one_block(piece):
            query_block, doc_block, start = piece
            scores = low_back(jnp.einsum('qhd,khd->hqk', query_block, key_all, precision=HIGH) * scale)
            query_place = start + jnp.arange(block, dtype=jnp.int32)
            key_place = jnp.arange(SEQ_LEN, dtype=jnp.int32)
            allowed = (doc_block[:, None] == doc_all[None, :]) & (key_place[None, :] <= query_place[:, None])
            scores = jnp.where(allowed[None], scores, NEG)
            chance = jax.nn.softmax(scores, axis=-1)
            return jnp.einsum('hqk,khd->qhd', low(chance), value_all, precision=HIGH)
        outputs = lax.map(jax.checkpoint(one_block), (query_blocks, doc_blocks, firsts))
        return (carry, outputs.reshape(SEQ_LEN, H, DV))
    _, outputs = lax.scan(one_sequence, jnp.float32(0.0), (query_seq, key_seq, value_seq, doc_seq))
    return outputs.reshape(TOKENS, H * DV)

def forward(residual, gain_first, query_down, query_gain, latent_down, latent_gain, query_up, latent_up, output_weight, gain_second, gate_weight, up_weight, down_weight, document_ids):
    cosine, sine = angles(TOKENS)
    first_in = low(normalize(residual, low(gain_first)))
    query_latent = low_back(product(first_in, low(query_down)))
    query_in = low(normalize(query_latent, low(query_gain)))
    latent_all = low_back(product(first_in, low(latent_down)))
    latent_in = low(normalize(latent_all[:, :KR], low(latent_gain)))
    key_rot = low(rotate(latent_all[:, KR:], cosine, sine))
    expanded = low(low_back(product(latent_in, low(latent_up)))).reshape(TOKENS, H, DN + DV)
    raw_query = low_back(product(query_in, low(query_up))).reshape(TOKENS, H, DN + DR)
    queries = low(jnp.concatenate([raw_query[..., :DN], rotate(raw_query[..., DN:], cosine[:, None, :], sine[:, None, :])], axis=-1))
    keys = jnp.concatenate([expanded[..., :DN], jnp.broadcast_to(key_rot[:, None, :], (TOKENS, H, DR))], axis=-1)
    attended = low(low_back(attention(queries, keys, expanded[..., DN:], document_ids)))
    branch = low_back(product(attended, low(output_weight)))
    middle = residual + RES * branch
    second_in = low(normalize(middle, low(gain_second)))
    gate = low_back(product(second_in, low(gate_weight)))
    upward = low_back(product(second_in, low(up_weight)))
    hidden = low(jax.nn.silu(gate) * upward)
    return middle + RES * low_back(product(hidden, low(down_weight)))

def reference(tokens, document_ids, gain_first, query_down, query_gain, latent_down, latent_gain, query_up, latent_up, output_weight, gain_second, gate_weight, up_weight, down_weight, cotangent):

    def apply(*weights):
        return forward(*weights, document_ids)
    result, pull = jax.vjp(apply, tokens.astype(jnp.float32), gain_first, query_down, query_gain, latent_down, latent_gain, query_up, latent_up, output_weight, gain_second, gate_weight, up_weight, down_weight)
    slopes = pull(cotangent)
    return (result, slopes[0], slopes[1], slopes[2], slopes[3], slopes[4], slopes[5], slopes[6], slopes[7], slopes[8], slopes[9], slopes[10], slopes[11], slopes[12])
```

```python
import functools
import math

import jax
import jax.numpy as jnp
from jax import lax
from jax.experimental import pallas as pl
from jax.experimental.pallas import tpu as pltpu
from jax.sharding import PartitionSpec as P

DN = 64
DR = 32
DV = 64
QR = 768
KR = 256
SEQ_LEN = 4096
DOC_MOST = 2000
EPS = 1e-05
RES = 1.4 / math.sqrt(62.0)
THETA = 10000.0
NEG = -1e30
LOG2E = math.log2(math.e)
SCALE = (DN + DR) ** (-0.5)
VMEM_LIMIT = 56 << 20
bf = jnp.bfloat16
f32 = jnp.float32


def ring_place(row, rows):
    return row // 2 + (row % 2) * (rows - 1 - 2 * (row // 2))


def ring_row(place, rows):
    side = place // (rows // 2)
    return 2 * (place + side * (rows - 1 - 2 * place)) + side


def ring_links(rows):
    order = [ring_row(p, rows) for p in range(rows)]
    ahead = [(order[p], order[(p + 1) % rows]) for p in range(rows)]
    return (ahead, [(b, a) for a, b in ahead])


class Gather:
    def __init__(self, block):
        self.rows = lax.axis_size("row")
        self.place = ring_place(lax.axis_index("row"), self.rows)
        self.shape = block.shape
        half = block.shape[0] // 2
        self.links = ring_links(self.rows)
        self.moving = [block[:half], block[half:]]
        self.whole = jnp.zeros((self.rows, 2, half, block.shape[1]), block.dtype)
        self.put(0)
        self.step = 0

    def put(self, step):
        for side in (0, 1):
            origin = ring_row((self.place + (step if side else self.rows - step)) % self.rows, self.rows)
            self.whole = lax.dynamic_update_slice(
                self.whole, self.moving[side][None, None], (origin, side, 0, 0)
            )

    def advance(self):
        self.moving = [lax.ppermute(self.moving[side], "row", self.links[side]) for side in (0, 1)]
        self.step += 1
        self.put(self.step)

    def result(self):
        return self.whole.reshape(self.rows * self.shape[0], self.shape[1])


def gather_rows(*blocks):
    flows = [Gather(block) for block in blocks]
    for _ in range(flows[0].rows - 1):
        for flow in flows:
            flow.advance()
    return [flow.result() for flow in flows]


class Scatter:
    def __init__(self, left, right, transposed=False):
        self.rows = lax.axis_size("row")
        self.place = ring_place(lax.axis_index("row"), self.rows)
        half = left.shape[0] // self.rows // 2
        self.left = left.reshape(self.rows, 2, half, left.shape[1])
        self.right = right
        self.transposed = transposed
        self.links = ring_links(self.rows)
        self.moving = [self.part(0, side).astype(bf) for side in (0, 1)]
        self.step = 0

    def part(self, step, side):
        place = self.place + 1 + step if side else self.place + 2 * self.rows - 1 - step
        target = ring_row(place % self.rows, self.rows)
        piece = lax.dynamic_slice(self.left, (target, side, 0, 0), (1, 1) + self.left.shape[2:])[0, 0]
        contract = ((1,), (1,)) if self.transposed else ((1,), (0,))
        return lax.dot_general(piece, self.right, (contract, ((), ())), preferred_element_type=f32)

    def advance(self):
        self.step += 1
        last = self.step == self.rows - 1
        for side in (0, 1):
            arrived = lax.ppermute(self.moving[side], "row", self.links[side])
            total = arrived.astype(f32) + self.part(self.step, side)
            self.moving[side] = total if last else total.astype(bf)

    def result(self):
        return jnp.concatenate(self.moving, axis=0)


def scatter_rows(*flows):
    for _ in range(flows[0].rows - 1):
        for flow in flows:
            flow.advance()
    return [flow.result() for flow in flows]


def from_behind(value, steps):
    count = lax.axis_size("row")
    initial, last = (max(0, -steps), min(count, count - steps))
    return lax.ppermute(value, "row", [(source, source + steps) for source in range(initial, last)])


def swap_col(value, bit):
    return lax.ppermute(value, "col", [(c, c ^ bit) for c in range(lax.axis_size("col"))])


def by_owner(pieces):
    column = lax.axis_index("col")
    bit = 1
    pieces = list(pieces)
    while bit < len(pieces):
        odd = (column // bit) % 2 == 1
        pieces = [jnp.where(odd, pieces[k ^ bit], pieces[k]) for k in range(len(pieces))]
        bit *= 2
    return pieces


def pick(pieces):
    return by_owner(pieces)[0]


def col_gather(own):
    across = swap_col(own, 2)
    beside = swap_col(own, 1)
    return by_owner([own, beside, across, swap_col(across, 1)])


def col_scatter(pieces):
    mine = by_owner(pieces)
    low = [piece.astype(bf) for piece in mine]
    across = mine[2].astype(f32) + swap_col(low[3], 1).astype(f32)
    beside = mine[0].astype(f32) + swap_col(low[1], 1).astype(f32)
    return beside + swap_col(across.astype(bf), 2).astype(f32)


def col_exchange(pieces):
    mine = by_owner(pieces)
    return by_owner([mine[0]] + [swap_col(mine[k], k) for k in range(1, len(mine))])


def quarters(value, axis):
    return jnp.split(value, lax.axis_size("col"), axis=axis)


def dot(left, right, dims):
    return lax.dot_general(left, right, (dims, ((), ())), preferred_element_type=f32)


def multiply(left, right):
    return dot(left, right, ((1,), (0,)))


def against(left, right):
    return dot(left, right, ((1,), (1,)))


def over_rows(left, right):
    return dot(left, right, ((0,), (0,)))


def inverse_of(value, axis):
    return lax.rsqrt(jnp.mean(value * value, axis=axis, keepdims=True) + EPS)


def norm_back(value, inverse, gain, upstream, axis):
    unit = value * inverse
    scaled = upstream * gain
    inward = inverse * (scaled - unit * jnp.mean(scaled * unit, axis=axis, keepdims=True))
    return (inward, jnp.sum(upstream * unit, axis=1 - axis))


def angles(start, count):
    place = ((start + jnp.arange(count, dtype=jnp.int32)) % SEQ_LEN).astype(f32)
    half = DR // 2
    freq = jnp.exp(jnp.arange(half, dtype=f32) * (-math.log(THETA) / half))
    turn = freq[:, None] * place[None, :]
    return (jnp.cos(turn), jnp.sin(turn))


def rotate(front, behind, cosine, sine):
    return (front * cosine - behind * sine, behind * cosine + front * sine)


def query_columns(heads):
    tiles = -(-heads // 4)
    column = lax.iota(jnp.int32, heads * DN + tiles * 128)
    plain = (column // DN) * (DN + DR) + column % DN
    rest = column - heads * DN
    head = (rest // 128) * 4 + (rest % 64) // 16
    turned = head * (DN + DR) + DN + ((rest % 128) // 64) * 16 + rest % 16
    turned = jnp.where(head < heads, turned, -1)
    return jnp.where(column < heads * DN, plain, turned)


def latent_columns(heads):
    column = lax.iota(jnp.int32, heads * (DN + DV))
    rest = column % (heads * DN)
    return (rest // DN) * (DN + DV) + rest % DN + (column // (heads * DN)) * DN


def chosen(origin, width):
    return lax.broadcasted_iota(jnp.int32, (width, origin.shape[0]), 0) == origin[None, :]


BLOCK = 512


def head_rows(step, side, shape, axis):
    place = lax.broadcasted_iota(jnp.int32, shape, axis)
    plain = (place // DN == side).astype(f32).astype(bf)
    turned = ((place % 64) // 16 == 2 * (step % 2) + side).astype(f32).astype(bf)
    return (plain, turned)


def attend_kernel(blocks, first_ref, qn_ref, qr_ref, k_ref, kr_ref, vt_ref, bias_ref, o_ref, lse_ref, s_ref):
    step = pl.program_id(0)
    first = first_ref[0]
    count = qn_ref.shape[1]
    for side in (0, 1):
        plain, turned = head_rows(step, side, qn_ref.shape, 0)
        right = jnp.concatenate([qn_ref[...] * plain, qr_ref[...] * turned], axis=0)

        def score(j, top):
            rows = pl.ds(pl.multiple_of(j * BLOCK, BLOCK), BLOCK)
            left = jnp.concatenate([k_ref[rows, :], kr_ref[rows, :]], axis=1)
            s = multiply(left, right) * (SCALE * LOG2E) + bias_ref[rows, :]
            s_ref[rows, :] = s
            return jnp.maximum(top, jnp.max(s, axis=0, keepdims=True))

        top = lax.fori_loop(first, blocks, score, jnp.full((1, count), NEG, f32))

        def gather(j, carry):
            total, out = carry
            rows = pl.ds(pl.multiple_of(j * BLOCK, BLOCK), BLOCK)
            chance = jnp.exp2(s_ref[rows, :] - top)
            total = total + jnp.sum(chance, axis=0, keepdims=True)
            out = out + multiply(vt_ref[side * DV : (side + 1) * DV, rows], chance.astype(bf))
            return (total, out)

        total, out = lax.fori_loop(
            first, blocks, gather, (jnp.zeros((1, count), f32), jnp.zeros((DV, count), f32))
        )
        o_ref[side * DV : (side + 1) * DV, :] = (out / total).astype(bf)
        lse_ref[0, side : side + 1, :] = top + jnp.log2(total)


def attend(first, query, keys, turned_keys, values_t, bias, heads):
    count, kl = query.shape[1], keys.shape[0]
    pairs, base = heads // 2, heads * DN // 128
    grid = pltpu.PrefetchScalarGridSpec(
        num_scalar_prefetch=1,
        grid=(pairs,),
        in_specs=[
            pl.BlockSpec((128, count), lambda p, s: (p, 0)),
            pl.BlockSpec((128, count), lambda p, s: (base + p // 2, 0)),
            pl.BlockSpec((kl, 128), lambda p, s: (0, p)),
            pl.BlockSpec((kl, 128), lambda p, s: (0, 0)),
            pl.BlockSpec((128, kl), lambda p, s: (p, 0)),
            pl.BlockSpec((kl, count), lambda p, s: (0, 0)),
        ],
        out_specs=[
            pl.BlockSpec((128, count), lambda p, s: (p, 0)),
            pl.BlockSpec((1, 2, count), lambda p, s: (p, 0, 0)),
        ],
        scratch_shapes=[pltpu.VMEM((kl, count), f32)],
    )
    return pl.pallas_call(
        functools.partial(attend_kernel, kl // BLOCK),
        grid_spec=grid,
        out_shape=[
            jax.ShapeDtypeStruct((heads * DV, count), bf),
            jax.ShapeDtypeStruct((pairs, 2, count), f32),
        ],
        compiler_params=pltpu.CompilerParams(vmem_limit_bytes=VMEM_LIMIT),
        cost_estimate=pl.CostEstimate(
            flops=heads * kl * count * 2 * 512, bytes_accessed=16 << 20, transcendentals=heads * kl * count
        ),
        name="attend",
    )(first, query, query, keys, turned_keys, values_t, bias)


def attend_back_kernel(
    blocks, first_ref, qn_ref, qr_ref, qnn_ref, qrn_ref, k_ref, kr_ref, kt_ref, krt_ref, v_ref, dot_ref, do_ref,
    bias_ref, lse_ref, dqn_ref, dqr_ref, dk_ref, dv_ref, dkr_ref, p_ref, dp_ref,
):
    step = pl.program_id(0)
    first = first_ref[0]
    count = qn_ref.shape[1]

    @pl.when(step == 0)
    def _():
        dkr_ref[...] = jnp.zeros_like(dkr_ref)

    @pl.when(step % 2 == 0)
    def _():
        dqr_ref[...] = jnp.zeros_like(dqr_ref)

    dk_ref[...] = jnp.zeros_like(dk_ref)
    dv_ref[...] = jnp.zeros_like(dv_ref)
    for side in (0, 1):
        plain, turned = head_rows(step, side, qn_ref.shape, 0)
        right = jnp.concatenate([qn_ref[...] * plain, qr_ref[...] * turned], axis=0)
        out_right = dot_ref[...] * plain
        lse = lse_ref[0, side : side + 1, :]

        def score(j, delta):
            rows = pl.ds(pl.multiple_of(j * BLOCK, BLOCK), BLOCK)
            left = jnp.concatenate([k_ref[rows, :], kr_ref[rows, :]], axis=1)
            s = multiply(left, right) * (SCALE * LOG2E) + bias_ref[rows, :]
            chance = jnp.exp2(s - lse)
            p_ref[rows, :] = chance
            back = multiply(v_ref[rows, :], out_right)
            dp_ref[rows, :] = back
            return delta + jnp.sum(chance * back, axis=0, keepdims=True)

        delta = lax.fori_loop(first, blocks, score, jnp.zeros((1, count), f32))
        plain_l, turned_l = head_rows(step, side, qnn_ref.shape, 1)
        query_right = jnp.concatenate([qnn_ref[...] * plain_l, qrn_ref[...] * turned_l], axis=1)
        value_right = do_ref[...] * plain_l

        def spread(j, dq):
            rows = pl.ds(pl.multiple_of(j * BLOCK, BLOCK), BLOCK)
            chance = p_ref[rows, :]
            ds = (chance * (dp_ref[rows, :] - delta)).astype(bf)
            left = jnp.concatenate([kt_ref[:, rows], krt_ref[:, rows]], axis=0)
            dq = dq + multiply(left, ds)
            dk = multiply(ds, query_right)
            dk_ref[rows, :] += (dk[:, :128] * SCALE).astype(bf)
            dkr_ref[rows, :] += dk[:, 128:] * SCALE
            dv_ref[rows, :] += multiply(chance.astype(bf), value_right).astype(bf)
            return dq

        dq = lax.fori_loop(first, blocks, spread, jnp.zeros((256, count), f32)) * SCALE
        dqn_ref[side * DN : (side + 1) * DN, :] = dq[side * DN : (side + 1) * DN]
        place = lax.broadcasted_iota(jnp.int32, (128, count), 0)
        dqr_ref[...] += jnp.where((place % 64) // 16 == 2 * (step % 2) + side, dq[128:], 0.0)


def attend_back(first, query, query_n, keys, turned_keys, keys_t, turned_keys_t, values, do_t, do, bias, lse, heads):
    count, kl = query.shape[1], keys.shape[0]
    pairs, base, tiles = heads // 2, heads * DN // 128, -(-heads // 4)
    across = lambda p, s: (0, p)
    along = lambda p, s: (p, 0)
    fixed = lambda p, s: (0, 0)
    grid = pltpu.PrefetchScalarGridSpec(
        num_scalar_prefetch=1,
        grid=(pairs,),
        in_specs=[
            pl.BlockSpec((128, count), along),
            pl.BlockSpec((128, count), lambda p, s: (base + p // 2, 0)),
            pl.BlockSpec((count, 128), across),
            pl.BlockSpec((count, 128), lambda p, s: (0, base + p // 2)),
            pl.BlockSpec((kl, 128), across),
            pl.BlockSpec((kl, 128), fixed),
            pl.BlockSpec((128, kl), along),
            pl.BlockSpec((128, kl), fixed),
            pl.BlockSpec((kl, 128), across),
            pl.BlockSpec((128, count), along),
            pl.BlockSpec((count, 128), across),
            pl.BlockSpec((kl, count), fixed),
            pl.BlockSpec((1, 2, count), lambda p, s: (p, 0, 0)),
        ],
        out_specs=[
            pl.BlockSpec((128, count), along),
            pl.BlockSpec((128, count), lambda p, s: (p // 2, 0)),
            pl.BlockSpec((kl, 128), across),
            pl.BlockSpec((kl, 128), across),
            pl.BlockSpec((kl, 128), fixed),
        ],
        scratch_shapes=[pltpu.VMEM((kl, count), f32), pltpu.VMEM((kl, count), f32)],
    )
    return pl.pallas_call(
        functools.partial(attend_back_kernel, kl // BLOCK),
        grid_spec=grid,
        out_shape=[
            jax.ShapeDtypeStruct((heads * DN, count), f32),
            jax.ShapeDtypeStruct((tiles * 128, count), f32),
            jax.ShapeDtypeStruct((kl, heads * DN), bf),
            jax.ShapeDtypeStruct((kl, heads * DV), bf),
            jax.ShapeDtypeStruct((kl, 128), f32),
        ],
        compiler_params=pltpu.CompilerParams(vmem_limit_bytes=VMEM_LIMIT),
        cost_estimate=pl.CostEstimate(
            flops=heads * kl * count * 2 * 1280, bytes_accessed=32 << 20, transcendentals=heads * kl * count
        ),
        name="attend_back",
    )(first, query, query, query_n, query_n, keys, turned_keys, keys_t, turned_keys_t, values, do_t, do, bias, lse)


def shards(
    tokens, document_ids, gain_first, query_down, query_gain, latent_down, latent_gain, query_up, latent_up,
    output_weight, gain_second, gate_weight, up_weight, down_weight, cotangent,
):
    count, own_width = tokens.shape
    rows, cols = lax.axis_size("row"), lax.axis_size("col")
    row, column = lax.axis_index("row"), lax.axis_index("col")
    start = row * count
    heads = query_up.shape[1] // (DN + DR)
    reach = -(-(DOC_MOST - 1) // count)
    blocks = reach + 1
    wide = heads * DN
    quarter = count // cols
    cosine, sine = angles(start, count)

    both_down = jnp.concatenate([query_down, latent_down], axis=1).astype(bf)
    down_slice = pick(quarters(both_down, 1))
    slice_width = down_slice.shape[1]
    small = jnp.concatenate([query_gain, latent_gain]).astype(bf)
    small = jnp.pad(small, (0, gain_first.shape[0] - small.shape[0]))
    gains = jnp.stack([gain_first.astype(bf), gain_second.astype(bf), small], axis=1)
    query_one = chosen(query_columns(heads), heads * (DN + DR))
    latent_one = chosen(latent_columns(heads), heads * (DN + DV))
    query_up_low = multiply(query_up.astype(bf), query_one.astype(bf)).astype(bf)
    latent_up_low = multiply(latent_up.astype(bf), latent_one.astype(bf)).astype(bf)
    (wide_down,) = gather_rows(jnp.concatenate([down_slice, gains], axis=1))
    wide_query_up, wide_latent_up = gather_rows(query_up_low, latent_up_low)
    (wide_output,) = gather_rows(output_weight.astype(bf).T)
    wide_gate, wide_up, wide_back = gather_rows(
        gate_weight.astype(bf), up_weight.astype(bf), down_weight.astype(bf).T
    )
    gain_one = wide_down[:, slice_width].astype(f32)
    gain_two = wide_down[:, slice_width + 1].astype(f32)
    small_gains = wide_down[:, slice_width + 2].reshape(rows, -1).astype(f32)
    own_q = query_gain.shape[0]
    query_scale = small_gains[:, :own_q].reshape(-1)[:, None]
    latent_scale = small_gains[:, own_q : own_q + latent_gain.shape[0]].reshape(-1)[:, None]
    wide_down = wide_down[:, :slice_width]

    features = jnp.concatenate(col_gather(tokens), axis=1)
    own_up = jnp.concatenate(col_exchange(quarters(cotangent, 0)), axis=1)
    back_down = jnp.concatenate(col_gather((RES * cotangent).astype(bf)), axis=1)
    residual = features.astype(f32)
    first_in = (residual * inverse_of(residual, 1) * gain_one).astype(bf)
    own_residual = pick(quarters(features, 0)).astype(f32)

    latents = jnp.concatenate(col_gather(dot(wide_down, first_in, ((0,), (1,)))), axis=0)
    query_latent, latent_part = latents[:QR], latents[QR : QR + KR]
    inverse_query, inverse_latent = inverse_of(query_latent, 0), inverse_of(latent_part, 0)
    query_in = (query_latent * inverse_query * query_scale).astype(bf)
    latent_in = (latent_part * inverse_latent * latent_scale).astype(bf)
    half = DR // 2
    key_front, key_back = rotate(latents[QR + KR : QR + KR + half], latents[QR + KR + half :], cosine, sine)
    key_part = jnp.concatenate([latent_in, key_front.astype(bf), key_back.astype(bf)], axis=0)
    key_parts = jnp.concatenate([from_behind(key_part, step) for step in range(reach, 0, -1)] + [key_part], axis=1)
    latent_all = key_parts[:KR]
    turned_t = jnp.concatenate([key_parts[KR : KR + half]] * 4 + [key_parts[KR + half :]] * 4, axis=0)
    turned = turned_t.T

    key_place = start - reach * count + jnp.arange(blocks * count, dtype=jnp.int32)
    place = start + jnp.arange(count, dtype=jnp.int32)
    key_doc = lax.dynamic_slice_in_dim(jnp.pad(document_ids, (reach * count, 0)), start, blocks * count)
    doc = lax.dynamic_slice_in_dim(document_ids, start, count)
    allowed = (key_doc[:, None] == doc[None, :]) & (key_place[:, None] <= place[None, :])
    allowed = allowed & (key_place[:, None] >= (place // SEQ_LEN * SEQ_LEN)[None, :])
    bias = jnp.where(allowed, 0.0, NEG).astype(f32)
    doc_start = jnp.sum((document_ids < doc[0]).astype(jnp.int32))
    first = jnp.clip((doc_start - (start - reach * count)) // BLOCK, 0, reach).reshape(1)

    raw = over_rows(wide_query_up, query_in)
    tiles = raw[wide:].reshape(-1, 2, 64, count)
    cos_tile, sin_tile = jnp.tile(cosine, (4, 1)), jnp.tile(sine, (4, 1))
    query_turned = jnp.stack(rotate(tiles[:, 0], tiles[:, 1], cos_tile, sin_tile), axis=1).reshape(-1, count)
    query = jnp.concatenate([raw[:wide], query_turned], axis=0).astype(bf)
    up_keys, up_values = wide_latent_up[:, :wide], wide_latent_up[:, wide:]
    keys = over_rows(latent_all, up_keys).astype(bf)
    values_t = over_rows(up_values, latent_all).astype(bf)
    out_t, lse = attend(first, query, keys, turned, values_t, bias, heads)

    branch = dot(out_t, wide_output, ((0,), (1,)))
    middle = own_residual + RES * col_scatter(quarters(branch, 0))
    inverse_second = inverse_of(middle, 1)
    second_in = jnp.concatenate(col_gather((middle * inverse_second * gain_two).astype(bf)), axis=0)

    gate = multiply(second_in, wide_gate)
    upward = multiply(second_in, wide_up)
    sigma = jax.nn.sigmoid(gate)
    hidden = (gate * sigma * upward).astype(bf)
    middle_own = jnp.concatenate(col_exchange(quarters(middle, 1)), axis=0)
    result = middle_own + RES * col_scatter(quarters(against(hidden, wide_back), 1))
    back_hidden = multiply(back_down, wide_back)
    back_gate = (back_hidden * upward * sigma * (1.0 + gate * (1.0 - sigma))).astype(bf)
    back_upward = (back_hidden * gate * sigma).astype(bf)
    ffn = (
        Scatter(second_in.T, back_gate),
        Scatter(second_in.T, back_upward),
        Scatter(back_down.T, hidden),
    )
    slope_gate, slope_up, slope_down = scatter_rows(*ffn)

    back_second = col_scatter(quarters(against(back_gate, wide_gate) + against(back_upward, wide_up), 0))
    back_norm, gain_second_part = norm_back(middle, inverse_second, gain_two, back_second, 1)
    back_middle = own_up + back_norm
    back_branch = jnp.concatenate(col_gather((RES * back_middle).astype(bf)), axis=0)

    out = out_t.T
    back_out = multiply(back_branch, wide_output).astype(bf)
    keys_t = over_rows(up_keys, latent_all).astype(bf)
    values = over_rows(latent_all, up_values).astype(bf)
    back_query_n, back_query_r, back_keys, back_values, back_turned = attend_back(
        first, query, query.T, keys, turned, keys_t, turned_t, values, back_out.T, back_out, bias, lse, heads
    )
    tiles = back_query_r.reshape(-1, 2, 64, count)
    back_turn = jnp.stack(rotate(tiles[:, 0], tiles[:, 1], cos_tile, -sin_tile), axis=1).reshape(-1, count)
    back_raw = jnp.concatenate([back_query_n, back_turn], axis=0).astype(bf)
    query_part = multiply(wide_query_up, back_raw)
    latent_back = against(up_keys, back_keys) + against(up_values, back_values)
    turned_back = jnp.sum(back_turned.T.reshape(2, 4, half, blocks * count), axis=1).reshape(DR, blocks * count)
    far = jnp.concatenate([latent_back, turned_back], axis=0)
    to_send = jnp.concatenate(
        [query_part] + [far[:, b * count : (b + 1) * count] for b in range(blocks)], axis=0
    )
    summed = col_scatter(quarters(to_send, 1))
    back_query_in = summed[:QR]
    wide_far = KR + DR
    parts = [summed[QR + b * wide_far : QR + (b + 1) * wide_far] for b in range(blocks)]
    back_key = parts[reach]
    for step in range(1, reach + 1):
        back_key = back_key + from_behind(parts[reach - step], -step)

    own_latents = pick(quarters(latents, 1))
    own_query, own_latent = own_latents[:QR], own_latents[QR : QR + KR]
    back_query_latent, query_gain_part = norm_back(
        own_query, inverse_of(own_query, 0), query_scale, back_query_in, 0
    )
    back_latent, latent_gain_part = norm_back(
        own_latent, inverse_of(own_latent, 0), latent_scale, back_key[:KR], 0
    )
    own_cosine, own_sine = pick(quarters(cosine, 1)), pick(quarters(sine, 1))
    back_front, back_behind = rotate(back_key[KR : KR + half], back_key[KR + half :], own_cosine, -own_sine)
    back_latents = jnp.concatenate([back_query_latent, back_latent, back_front, back_behind], axis=0).astype(bf)
    back_latents = jnp.concatenate(col_gather(back_latents), axis=1)
    back_slice = lax.dynamic_slice_in_dim(back_latents, column * slice_width, slice_width, 0)
    back_first = col_scatter(quarters(dot(back_slice, wide_down, ((0,), (1,))), 0))
    back_norm_first, gain_first_part = norm_back(own_residual, inverse_of(own_residual, 1), gain_one, back_first, 1)
    back_tokens = jnp.concatenate(col_exchange(quarters(back_middle + back_norm_first, 1)), axis=0)

    attention = (
        Scatter(back_branch.T, out),
        Scatter(query_in, back_raw, True),
        Scatter(latent_all, jnp.concatenate([back_keys, back_values], axis=1)),
        Scatter(first_in.T, back_slice, True),
    )
    slope_output, slope_query_up, slope_latent_up, slope_down_slice = scatter_rows(*attention)
    slope_both = jnp.concatenate(col_gather(slope_down_slice), axis=1)

    packed = jnp.concatenate(
        [part.reshape(rows, -1) for part in (gain_first_part, gain_second_part, query_gain_part, latent_gain_part)],
        axis=1,
    )
    bit = rows // 2
    while bit >= 1:
        upper = (row // bit) % 2 == 1
        low_half, high_half = packed[:bit], packed[bit:]
        away = jnp.where(upper, low_half, high_half)
        stay = jnp.where(upper, high_half, low_half)
        packed = stay + lax.ppermute(away, "row", [(r, r ^ bit) for r in range(rows)])
        bit //= 2
    packed = packed[0]
    bit = 1
    while bit < cols:
        packed = packed + swap_col(packed, bit)
        bit *= 2
    n = gain_first.shape[0]
    m = query_gain.shape[0]

    exact = functools.partial(
        lax.dot_general,
        dimension_numbers=(((1,), (1,)), ((), ())),
        precision=lax.Precision.HIGHEST,
        preferred_element_type=f32,
    )
    return (
        result,
        back_tokens,
        packed[:n],
        slope_both[:, :QR],
        packed[2 * n : 2 * n + m],
        slope_both[:, QR:],
        packed[2 * n + m :],
        exact(slope_query_up, query_one.astype(f32)),
        exact(slope_latent_up, latent_one.astype(f32)),
        slope_output.T,
        packed[n : 2 * n],
        slope_gate,
        slope_up,
        slope_down.T,
    )


def solution(mesh):
    placed = (
        P("row", "col"), P(), P("row"), P("row", None), P("row"), P("row", None), P("row"), P("row", "col"),
        P("row", "col"), P("col", "row"), P("row"), P("row", "col"), P("row", "col"), P("col", "row"),
        P("row", "col"),
    )
    outs = (
        P("row", "col"), P("row", "col"), P("row"), P("row", None), P("row"), P("row", None), P("row"),
        P("row", "col"), P("row", "col"), P("col", "row"), P("row"), P("row", "col"), P("row", "col"),
        P("col", "row"),
    )
    return jax.shard_map(shards, mesh=mesh, in_specs=placed, out_specs=outs, check_vma=False)
```

```python
import functools
import math

import jax
import jax.numpy as jnp
from jax import lax
from jax.experimental import pallas as pl
from jax.experimental.pallas import tpu as pltpu
from jax.sharding import PartitionSpec as P

DN = 64
DR = 32
DV = 64
QR = 768
KR = 256
SEQ_LEN = 4096
DOC_MOST = 2000
EPS = 1e-05
RES = 1.4 / math.sqrt(62.0)
THETA = 10000.0
NEG = -1e30
LOG2E = math.log2(math.e)
SCALE = (DN + DR) ** (-0.5)
VMEM_LIMIT = 56 << 20
MESH = pl.DeviceIdType.MESH
bf = jnp.bfloat16
f32 = jnp.float32


def ring_place(row, rows):
    return row // 2 + (row % 2) * (rows - 1 - 2 * (row // 2))


def ring_row(place, rows):
    side = place // (rows // 2)
    return 2 * (place + side * (rows - 1 - 2 * place)) + side


def ring_barrier(ahead, behind, column):
    barrier = pltpu.get_barrier_semaphore()
    for other in (ahead, behind):
        pl.semaphore_signal(barrier, inc=1, device_id=(other, column), device_id_type=MESH)
    pl.semaphore_wait(barrier, 2)


def ring_gather_kernel(rows, n, *refs):
    blocks, wholes, (own_sem, send_sem, recv_sem) = refs[:n], refs[n : 2 * n], refs[2 * n :]
    row, column = lax.axis_index("row"), lax.axis_index("col")
    place = ring_place(row, rows)
    ends = (ring_row((place + 1) % rows, rows), ring_row((place + rows - 1) % rows, rows))
    ring_barrier(ends[0], ends[1], column)

    def own(k):
        return pltpu.make_async_copy(blocks[k], wholes[k].at[row], own_sem.at[k])

    def hop(step, side, k):
        origin = ring_row((place + (step if side else rows - step)) % rows, rows)
        return pltpu.make_async_remote_copy(
            src_ref=wholes[k].at[origin, side],
            dst_ref=wholes[k].at[origin, side],
            send_sem=send_sem.at[step, side, k],
            recv_sem=recv_sem.at[step, side, k],
            device_id=(ends[side], column),
            device_id_type=MESH,
        )

    for k in range(n):
        own(k).start()
    for k in range(n):
        own(k).wait()
        for side in (0, 1):
            hop(0, side, k).start()

    def advance(step, carry):
        for k in range(n):
            for side in (0, 1):
                hop(step - 1, side, k).wait_recv()
                hop(step, side, k).start()
        return carry

    lax.fori_loop(1, rows - 1, advance, 0)
    for k in range(n):
        for side in (0, 1):
            hop(rows - 2, side, k).wait_recv()

    def drain(step, carry):
        for k in range(n):
            for side in (0, 1):
                hop(step, side, k).wait_send()
        return carry

    lax.fori_loop(0, rows - 1, drain, 0)


def ring_gather(*blocks):
    rows, n = lax.axis_size("row"), len(blocks)
    halves = [block.reshape(2, block.shape[0] // 2, block.shape[1]) for block in blocks]
    wholes = pl.pallas_call(
        functools.partial(ring_gather_kernel, rows, n),
        out_shape=[jax.ShapeDtypeStruct((rows,) + half.shape, half.dtype) for half in halves],
        in_specs=[pl.BlockSpec(memory_space=pl.ANY)] * n,
        out_specs=[pl.BlockSpec(memory_space=pl.ANY)] * n,
        scratch_shapes=[
            pltpu.SemaphoreType.DMA((n,)),
            pltpu.SemaphoreType.DMA((rows - 1, 2, n)),
            pltpu.SemaphoreType.DMA((rows - 1, 2, n)),
        ],
        compiler_params=pltpu.CompilerParams(collective_id=0, has_side_effects=True),
        name="ring_gather",
    )(*halves)
    return [whole.reshape(rows * block.shape[0], block.shape[1]) for whole, block in zip(wholes, blocks)]


def ring_scatter_kernel(rows, n, *refs):
    terms, sums, slots, (send_sem, recv_sem) = refs[:n], refs[n : 2 * n], refs[2 * n : 3 * n], refs[3 * n :]
    row, column = lax.axis_index("row"), lax.axis_index("col")
    place = ring_place(row, rows)
    ends = (ring_row((place + 1) % rows, rows), ring_row((place + rows - 1) % rows, rows))
    ring_barrier(ends[0], ends[1], column)

    def target(step, side):
        return ring_row((place + (1 + step if side else 2 * rows - 1 - step)) % rows, rows)

    def hop(step, side, k, source):
        return pltpu.make_async_remote_copy(
            src_ref=source,
            dst_ref=slots[k].at[step, side],
            send_sem=send_sem.at[step, side, k],
            recv_sem=recv_sem.at[step, side, k],
            device_id=(ends[side], column),
            device_id_type=MESH,
        )

    def first(side, k):
        return hop(0, side, k, terms[k].at[target(0, side), side])

    def later(step, side, k):
        return hop(step, side, k, slots[k].at[step - 1, side])

    for k in range(n):
        for side in (0, 1):
            first(side, k).start()

    def arrive(step, side, k):
        return hop(step, side, k, slots[k].at[step, side])

    def advance(step, carry):
        for k in range(n):
            for side in (0, 1):
                arrive(step - 1, side, k).wait_recv()
                total = slots[k][step - 1, side].astype(f32) + terms[k][target(step, side), side].astype(f32)
                slots[k][step - 1, side] = total.astype(bf)
                later(step, side, k).start()
        return carry

    lax.fori_loop(1, rows - 1, advance, 0)
    for k in range(n):
        for side in (0, 1):
            arrive(rows - 2, side, k).wait_recv()
            sums[k][side] = slots[k][rows - 2, side].astype(f32) + terms[k][row, side].astype(f32)

    def drain(step, carry):
        for k in range(n):
            for side in (0, 1):
                arrive(step, side, k).wait_send()
        return carry

    lax.fori_loop(0, rows - 1, drain, 0)


def ring_scatter(*terms):
    rows, n = lax.axis_size("row"), len(terms)
    split = [term.reshape(rows, 2, term.shape[0] // rows // 2, term.shape[1]) for term in terms]
    sums = pl.pallas_call(
        functools.partial(ring_scatter_kernel, rows, n),
        out_shape=[jax.ShapeDtypeStruct(term.shape[1:], f32) for term in split],
        in_specs=[pl.BlockSpec(memory_space=pltpu.VMEM)] * n,
        out_specs=[pl.BlockSpec(memory_space=pltpu.VMEM)] * n,
        scratch_shapes=[pltpu.VMEM((rows - 1,) + term.shape[1:], bf) for term in split]
        + [pltpu.SemaphoreType.DMA((rows - 1, 2, n)), pltpu.SemaphoreType.DMA((rows - 1, 2, n))],
        compiler_params=pltpu.CompilerParams(
            collective_id=1, has_side_effects=True, vmem_limit_bytes=VMEM_LIMIT
        ),
        name="ring_scatter",
    )(*split)
    return [total.reshape(total.shape[0] * total.shape[1], total.shape[2]) for total in sums]


def from_behind(value, steps):
    count = lax.axis_size("row")
    initial, last = (max(0, -steps), min(count, count - steps))
    return lax.ppermute(value, "row", [(source, source + steps) for source in range(initial, last)])


def swap_col(value, bit):
    return lax.ppermute(value, "col", [(c, c ^ bit) for c in range(lax.axis_size("col"))])


def by_owner(pieces, own=None):
    own = lax.axis_index("col") if own is None else own
    bit = 1
    pieces = list(pieces)
    while bit < len(pieces):
        odd = (own // bit) % 2 == 1
        pieces = [jnp.where(odd, pieces[k ^ bit], pieces[k]) for k in range(len(pieces))]
        bit *= 2
    return pieces


def pick(pieces):
    return by_owner(pieces)[0]


def col_gather(own):
    across = swap_col(own, 2)
    beside = swap_col(own, 1)
    return by_owner([own, beside, across, swap_col(across, 1)])


def col_scatter(pieces):
    mine = by_owner(pieces)
    low = [piece.astype(bf) for piece in mine]
    across = mine[2].astype(f32) + swap_col(low[3], 1).astype(f32)
    beside = mine[0].astype(f32) + swap_col(low[1], 1).astype(f32)
    return beside + swap_col(across.astype(bf), 2).astype(f32)


def col_exchange(pieces):
    mine = by_owner(pieces)
    return by_owner([mine[0]] + [swap_col(mine[k], k) for k in range(1, len(mine))])


def quarters(value, axis):
    return jnp.split(value, lax.axis_size("col"), axis=axis)


PAIR = 2


def group_row(group, side):
    return (group // 2) * 4 + side * PAIR + group % 2


def own_group():
    row = lax.axis_index("row")
    return ((row // 4) * 2 + row % 2, (row // PAIR) % 2)


def swap_row(value, mask):
    return lax.ppermute(value, "row", [(r, r ^ mask) for r in range(lax.axis_size("row"))])


def group_masks():
    bits = (lax.axis_size("row") // 2).bit_length() - 1
    return [(1 << b, group_row(1 << b, 0)) for b in reversed(range(bits))]


def after(value, other):
    return lax.optimization_barrier((value, other))[0]


def features_by_group(value):
    rows = lax.axis_size("row")
    chunks = jnp.split(value, rows, axis=1)
    groups = [
        jnp.concatenate([chunks[group_row(g, side)] for side in (0, 1)], axis=1) for g in range(rows // 2)
    ]
    return jnp.concatenate(by_owner(groups, own_group()[0]), axis=1)


def features_in_order(value):
    rows = lax.axis_size("row")
    groups = by_owner(jnp.split(value, rows // 2, axis=1), own_group()[0])
    chunks = [None] * rows
    for g, group in enumerate(groups):
        for side, chunk in enumerate(jnp.split(group, 2, axis=1)):
            chunks[group_row(g, side)] = chunk
    return jnp.concatenate(chunks, axis=1)


def group_gather(own):
    pieces = []
    for piece in (own, swap_row(own, PAIR)):
        across = swap_col(piece, 2)
        pieces += [piece, swap_col(piece, 1), across, swap_col(across, 1)]
    return jnp.concatenate(pieces, axis=0)


def group_scatter(value):
    x = jnp.split(value, 2 * lax.axis_size("col"), axis=0)
    beside = swap_col(jnp.concatenate([x[1], x[3], x[5], x[7]], axis=0).astype(bf), 1).astype(f32)
    y = [term + got for term, got in zip((x[0], x[2], x[4], x[6]), jnp.split(beside, 4, axis=0))]
    across = swap_col(jnp.concatenate([y[1], y[3]], axis=0).astype(bf), 2).astype(f32)
    z = [term + got for term, got in zip((y[0], y[2]), jnp.split(across, 2, axis=0))]
    return z[0] + swap_row(z[1].astype(bf), PAIR).astype(f32)


def gather_hidden(block, turn):
    low, high = jnp.split(block, 2, axis=0)
    upper = own_group()[1] == 1
    mine = jnp.where(upper, high, low)
    came = swap_row(jnp.where(upper, low, high), PAIR)
    pieces = {0: jnp.concatenate([jnp.where(upper, came, mine), jnp.where(upper, mine, came)], axis=1)}
    if turn is not None:
        pieces[0] = after(pieces[0], turn)
    first = None
    for bit, mask in group_masks():
        for k in list(pieces):
            pieces[k ^ bit] = swap_row(pieces[k], mask)
            first = pieces[k ^ bit] if first is None else first
    return (jnp.concatenate([pieces[k] for k in range(len(pieces))], axis=1), first)


def scatter_hidden(left, right, turn):
    groups = lax.axis_size("row") // 2
    chunks = jnp.split(right, groups, axis=1)
    pieces = {}
    kept = list(range(groups))
    first = None
    for bit, mask in reversed(group_masks()):
        away, stay = [k for k in kept if k & bit], [k for k in kept if not k & bit]
        for k in kept:
            if k not in pieces:
                pieces[k] = None
        if first is None:
            wide = lambda ks: jnp.concatenate([chunks[k] for k in ks], axis=1)
            leaving = over_rows(left, wide(away)).astype(bf)
            staying = over_rows(left, wide(stay))
            if turn is not None:
                leaving = after(leaving, turn)
        else:
            leaving = jnp.concatenate([pieces[k] for k in away], axis=1).astype(bf)
            staying = jnp.concatenate([pieces[k] for k in stay], axis=1)
        came = swap_row(leaving, mask)
        first = came if first is None else first
        total = staying + came.astype(f32)
        pieces = dict(zip(stay, jnp.split(total, len(stay), axis=1)))
        kept = stay
    low, high = jnp.split(pieces[0], 2, axis=1)
    upper = own_group()[1] == 1
    mine = jnp.where(upper, high, low)
    came = swap_row(jnp.where(upper, low, high).astype(bf), PAIR).astype(f32)
    return (jnp.concatenate([jnp.where(upper, came, mine), jnp.where(upper, mine, came)], axis=0), first)


def dot(left, right, dims):
    return lax.dot_general(left, right, (dims, ((), ())), preferred_element_type=f32)


def multiply(left, right):
    return dot(left, right, ((1,), (0,)))


def against(left, right):
    return dot(left, right, ((1,), (1,)))


def over_rows(left, right):
    return dot(left, right, ((0,), (0,)))


def inverse_of(value, axis):
    return lax.rsqrt(jnp.mean(value * value, axis=axis, keepdims=True) + EPS)


def norm_back(value, inverse, gain, upstream, axis):
    unit = value * inverse
    scaled = upstream * gain
    inward = inverse * (scaled - unit * jnp.mean(scaled * unit, axis=axis, keepdims=True))
    return (inward, jnp.sum(upstream * unit, axis=1 - axis))


def angles(start, count):
    place = ((start + jnp.arange(count, dtype=jnp.int32)) % SEQ_LEN).astype(f32)
    half = DR // 2
    freq = jnp.exp(jnp.arange(half, dtype=f32) * (-math.log(THETA) / half))
    turn = freq[:, None] * place[None, :]
    return (jnp.cos(turn), jnp.sin(turn))


def rotate(front, behind, cosine, sine):
    return (front * cosine - behind * sine, behind * cosine + front * sine)


def query_columns(heads):
    tiles = -(-heads // 4)
    column = lax.iota(jnp.int32, heads * DN + tiles * 128)
    plain = (column // DN) * (DN + DR) + column % DN
    rest = column - heads * DN
    head = (rest // 128) * 4 + (rest % 64) // 16
    turned = head * (DN + DR) + DN + ((rest % 128) // 64) * 16 + rest % 16
    turned = jnp.where(head < heads, turned, -1)
    return jnp.where(column < heads * DN, plain, turned)


def latent_columns(heads):
    column = lax.iota(jnp.int32, heads * (DN + DV))
    rest = column % (heads * DN)
    return (rest // DN) * (DN + DV) + rest % DN + (column // (heads * DN)) * DN


def chosen(origin, width):
    return lax.broadcasted_iota(jnp.int32, (width, origin.shape[0]), 0) == origin[None, :]


BLOCK = 512


def head_rows(step, side, shape, axis):
    place = lax.broadcasted_iota(jnp.int32, shape, axis)
    plain = (place // DN == side).astype(f32).astype(bf)
    turned = ((place % 64) // 16 == 2 * (step % 2) + side).astype(f32).astype(bf)
    return (plain, turned)


def attend_kernel(blocks, first_ref, qn_ref, qr_ref, k_ref, kr_ref, vt_ref, bias_ref, o_ref, lse_ref, s_ref):
    step = pl.program_id(0)
    first = first_ref[0]
    count = qn_ref.shape[1]
    for side in (0, 1):
        plain, turned = head_rows(step, side, qn_ref.shape, 0)
        right = jnp.concatenate([qn_ref[...] * plain, qr_ref[...] * turned], axis=0)

        def score(j, top):
            rows = pl.ds(pl.multiple_of(j * BLOCK, BLOCK), BLOCK)
            left = jnp.concatenate([k_ref[rows, :], kr_ref[rows, :]], axis=1)
            s = multiply(left, right) * (SCALE * LOG2E) + bias_ref[rows, :]
            s_ref[rows, :] = s
            return jnp.maximum(top, jnp.max(s, axis=0, keepdims=True))

        top = lax.fori_loop(first, blocks, score, jnp.full((1, count), NEG, f32))

        def gather(j, carry):
            total, out = carry
            rows = pl.ds(pl.multiple_of(j * BLOCK, BLOCK), BLOCK)
            chance = jnp.exp2(s_ref[rows, :] - top)
            total = total + jnp.sum(chance, axis=0, keepdims=True)
            out = out + multiply(vt_ref[side * DV : (side + 1) * DV, rows], chance.astype(bf))
            return (total, out)

        total, out = lax.fori_loop(
            first, blocks, gather, (jnp.zeros((1, count), f32), jnp.zeros((DV, count), f32))
        )
        o_ref[side * DV : (side + 1) * DV, :] = (out / total).astype(bf)
        lse_ref[0, side : side + 1, :] = top + jnp.log2(total)


def attend(first, query, keys, turned_keys, values_t, bias, heads):
    count, kl = query.shape[1], keys.shape[0]
    pairs, base = heads // 2, heads * DN // 128
    grid = pltpu.PrefetchScalarGridSpec(
        num_scalar_prefetch=1,
        grid=(pairs,),
        in_specs=[
            pl.BlockSpec((128, count), lambda p, s: (p, 0)),
            pl.BlockSpec((128, count), lambda p, s: (base + p // 2, 0)),
            pl.BlockSpec((kl, 128), lambda p, s: (0, p)),
            pl.BlockSpec((kl, 128), lambda p, s: (0, 0)),
            pl.BlockSpec((128, kl), lambda p, s: (p, 0)),
            pl.BlockSpec((kl, count), lambda p, s: (0, 0)),
        ],
        out_specs=[
            pl.BlockSpec((128, count), lambda p, s: (p, 0)),
            pl.BlockSpec((1, 2, count), lambda p, s: (p, 0, 0)),
        ],
        scratch_shapes=[pltpu.VMEM((kl, count), f32)],
    )
    return pl.pallas_call(
        functools.partial(attend_kernel, kl // BLOCK),
        grid_spec=grid,
        out_shape=[
            jax.ShapeDtypeStruct((heads * DV, count), bf),
            jax.ShapeDtypeStruct((pairs, 2, count), f32),
        ],
        compiler_params=pltpu.CompilerParams(vmem_limit_bytes=VMEM_LIMIT),
        cost_estimate=pl.CostEstimate(
            flops=heads * kl * count * 2 * 512, bytes_accessed=16 << 20, transcendentals=heads * kl * count
        ),
        name="attend",
    )(first, query, query, keys, turned_keys, values_t, bias)


def attend_back_kernel(
    blocks, first_ref, qn_ref, qr_ref, qnn_ref, qrn_ref, k_ref, kr_ref, kt_ref, krt_ref, v_ref, dot_ref, do_ref,
    bias_ref, lse_ref, dqn_ref, dqr_ref, dk_ref, dv_ref, dkr_ref, p_ref, dp_ref,
):
    step = pl.program_id(0)
    first = first_ref[0]
    count = qn_ref.shape[1]

    @pl.when(step == 0)
    def _():
        dkr_ref[...] = jnp.zeros_like(dkr_ref)

    @pl.when(step % 2 == 0)
    def _():
        dqr_ref[...] = jnp.zeros_like(dqr_ref)

    dk_ref[...] = jnp.zeros_like(dk_ref)
    dv_ref[...] = jnp.zeros_like(dv_ref)
    for side in (0, 1):
        plain, turned = head_rows(step, side, qn_ref.shape, 0)
        right = jnp.concatenate([qn_ref[...] * plain, qr_ref[...] * turned], axis=0)
        out_right = dot_ref[...] * plain
        lse = lse_ref[0, side : side + 1, :]

        def score(j, delta):
            rows = pl.ds(pl.multiple_of(j * BLOCK, BLOCK), BLOCK)
            left = jnp.concatenate([k_ref[rows, :], kr_ref[rows, :]], axis=1)
            s = multiply(left, right) * (SCALE * LOG2E) + bias_ref[rows, :]
            chance = jnp.exp2(s - lse)
            p_ref[rows, :] = chance
            back = multiply(v_ref[rows, :], out_right)
            dp_ref[rows, :] = back
            return delta + jnp.sum(chance * back, axis=0, keepdims=True)

        delta = lax.fori_loop(first, blocks, score, jnp.zeros((1, count), f32))
        plain_l, turned_l = head_rows(step, side, qnn_ref.shape, 1)
        query_right = jnp.concatenate([qnn_ref[...] * plain_l, qrn_ref[...] * turned_l], axis=1)
        value_right = do_ref[...] * plain_l

        def spread(j, dq):
            rows = pl.ds(pl.multiple_of(j * BLOCK, BLOCK), BLOCK)
            chance = p_ref[rows, :]
            ds = (chance * (dp_ref[rows, :] - delta)).astype(bf)
            left = jnp.concatenate([kt_ref[:, rows], krt_ref[:, rows]], axis=0)
            dq = dq + multiply(left, ds)
            dk = multiply(ds, query_right)
            dk_ref[rows, :] += (dk[:, :128] * SCALE).astype(bf)
            dkr_ref[rows, :] += dk[:, 128:] * SCALE
            dv_ref[rows, :] += multiply(chance.astype(bf), value_right).astype(bf)
            return dq

        dq = lax.fori_loop(first, blocks, spread, jnp.zeros((256, count), f32)) * SCALE
        dqn_ref[side * DN : (side + 1) * DN, :] = dq[side * DN : (side + 1) * DN]
        place = lax.broadcasted_iota(jnp.int32, (128, count), 0)
        dqr_ref[...] += jnp.where((place % 64) // 16 == 2 * (step % 2) + side, dq[128:], 0.0)


def attend_back(first, query, query_n, keys, turned_keys, keys_t, turned_keys_t, values, do_t, do, bias, lse, heads):
    count, kl = query.shape[1], keys.shape[0]
    pairs, base, tiles = heads // 2, heads * DN // 128, -(-heads // 4)
    across = lambda p, s: (0, p)
    along = lambda p, s: (p, 0)
    fixed = lambda p, s: (0, 0)
    grid = pltpu.PrefetchScalarGridSpec(
        num_scalar_prefetch=1,
        grid=(pairs,),
        in_specs=[
            pl.BlockSpec((128, count), along),
            pl.BlockSpec((128, count), lambda p, s: (base + p // 2, 0)),
            pl.BlockSpec((count, 128), across),
            pl.BlockSpec((count, 128), lambda p, s: (0, base + p // 2)),
            pl.BlockSpec((kl, 128), across),
            pl.BlockSpec((kl, 128), fixed),
            pl.BlockSpec((128, kl), along),
            pl.BlockSpec((128, kl), fixed),
            pl.BlockSpec((kl, 128), across),
            pl.BlockSpec((128, count), along),
            pl.BlockSpec((count, 128), across),
            pl.BlockSpec((kl, count), fixed),
            pl.BlockSpec((1, 2, count), lambda p, s: (p, 0, 0)),
        ],
        out_specs=[
            pl.BlockSpec((128, count), along),
            pl.BlockSpec((128, count), lambda p, s: (p // 2, 0)),
            pl.BlockSpec((kl, 128), across),
            pl.BlockSpec((kl, 128), across),
            pl.BlockSpec((kl, 128), fixed),
        ],
        scratch_shapes=[pltpu.VMEM((kl, count), f32), pltpu.VMEM((kl, count), f32)],
    )
    return pl.pallas_call(
        functools.partial(attend_back_kernel, kl // BLOCK),
        grid_spec=grid,
        out_shape=[
            jax.ShapeDtypeStruct((heads * DN, count), f32),
            jax.ShapeDtypeStruct((tiles * 128, count), f32),
            jax.ShapeDtypeStruct((kl, heads * DN), bf),
            jax.ShapeDtypeStruct((kl, heads * DV), bf),
            jax.ShapeDtypeStruct((kl, 128), f32),
        ],
        compiler_params=pltpu.CompilerParams(vmem_limit_bytes=VMEM_LIMIT),
        cost_estimate=pl.CostEstimate(
            flops=heads * kl * count * 2 * 1280, bytes_accessed=32 << 20, transcendentals=heads * kl * count
        ),
        name="attend_back",
    )(first, query, query, query_n, query_n, keys, turned_keys, keys_t, turned_keys_t, values, do_t, do, bias, lse)


def shards(
    tokens, document_ids, gain_first, query_down, query_gain, latent_down, latent_gain, query_up, latent_up,
    output_weight, gain_second, gate_weight, up_weight, down_weight, cotangent,
):
    count, own_width = tokens.shape
    rows, cols = lax.axis_size("row"), lax.axis_size("col")
    row, column = lax.axis_index("row"), lax.axis_index("col")
    start = row * count
    heads = query_up.shape[1] // (DN + DR)
    reach = -(-(DOC_MOST - 1) // count)
    blocks = reach + 1
    wide = heads * DN
    quarter = count // cols
    cosine, sine = angles(start, count)

    both_down = jnp.concatenate([query_down, latent_down], axis=1).astype(bf)
    down_slice = pick(quarters(both_down, 1))
    slice_width = down_slice.shape[1]
    small = jnp.concatenate([query_gain, latent_gain]).astype(bf)
    small = jnp.pad(small, (0, gain_first.shape[0] - small.shape[0]))
    gains = jnp.stack([gain_first.astype(bf), gain_second.astype(bf), small], axis=1)
    query_one = chosen(query_columns(heads), heads * (DN + DR))
    latent_one = chosen(latent_columns(heads), heads * (DN + DV))
    query_up_low = multiply(query_up.astype(bf), query_one.astype(bf)).astype(bf)
    latent_up_low = multiply(latent_up.astype(bf), latent_one.astype(bf)).astype(bf)
    down_block = jnp.concatenate([down_slice, gains], axis=1)
    down_block = jnp.pad(down_block, ((0, 0), (0, -down_block.shape[1] % 128)))
    wide_down, wide_query_up, wide_latent_up, wide_output = ring_gather(
        down_block, query_up_low, latent_up_low, output_weight.astype(bf).T
    )
    gate_t, turn = gather_hidden(after(gate_weight.astype(bf).T, wide_down), None)
    up_t, turn = gather_hidden(up_weight.astype(bf).T, turn)
    wide_back, turn = gather_hidden(down_weight.astype(bf), turn)
    gain_one = wide_down[:, slice_width].astype(f32)
    gain_two = wide_down[:, slice_width + 1].astype(f32)
    small_gains = wide_down[:, slice_width + 2].reshape(rows, -1).astype(f32)
    own_q = query_gain.shape[0]
    query_scale = small_gains[:, :own_q].reshape(-1)[:, None]
    latent_scale = small_gains[:, own_q : own_q + latent_gain.shape[0]].reshape(-1)[:, None]
    wide_down = wide_down[:, :slice_width]

    features = jnp.concatenate(col_gather(tokens), axis=1)
    own_up = jnp.concatenate(col_exchange(quarters(cotangent, 0)), axis=1)
    back_down = group_gather(features_by_group((RES * own_up).astype(bf)))
    residual = features.astype(f32)
    first_in = (residual * inverse_of(residual, 1) * gain_one).astype(bf)
    own_residual = pick(quarters(features, 0)).astype(f32)

    latents = jnp.concatenate(col_gather(dot(wide_down, first_in, ((0,), (1,)))), axis=0)
    query_latent, latent_part = latents[:QR], latents[QR : QR + KR]
    inverse_query, inverse_latent = inverse_of(query_latent, 0), inverse_of(latent_part, 0)
    query_in = (query_latent * inverse_query * query_scale).astype(bf)
    latent_in = (latent_part * inverse_latent * latent_scale).astype(bf)
    half = DR // 2
    key_front, key_back = rotate(latents[QR + KR : QR + KR + half], latents[QR + KR + half :], cosine, sine)
    key_part = jnp.concatenate([latent_in, key_front.astype(bf), key_back.astype(bf)], axis=0)
    key_parts = jnp.concatenate([from_behind(key_part, step) for step in range(reach, 0, -1)] + [key_part], axis=1)
    latent_all = key_parts[:KR]
    turned_t = jnp.concatenate([key_parts[KR : KR + half]] * 4 + [key_parts[KR + half :]] * 4, axis=0)
    turned = turned_t.T

    key_place = start - reach * count + jnp.arange(blocks * count, dtype=jnp.int32)
    place = start + jnp.arange(count, dtype=jnp.int32)
    key_doc = lax.dynamic_slice_in_dim(jnp.pad(document_ids, (reach * count, 0)), start, blocks * count)
    doc = lax.dynamic_slice_in_dim(document_ids, start, count)
    allowed = (key_doc[:, None] == doc[None, :]) & (key_place[:, None] <= place[None, :])
    allowed = allowed & (key_place[:, None] >= (place // SEQ_LEN * SEQ_LEN)[None, :])
    bias = jnp.where(allowed, 0.0, NEG).astype(f32)
    doc_start = jnp.sum((document_ids < doc[0]).astype(jnp.int32))
    first = jnp.clip((doc_start - (start - reach * count)) // BLOCK, 0, reach).reshape(1)

    raw = over_rows(wide_query_up, query_in)
    tiles = raw[wide:].reshape(-1, 2, 64, count)
    cos_tile, sin_tile = jnp.tile(cosine, (4, 1)), jnp.tile(sine, (4, 1))
    query_turned = jnp.stack(rotate(tiles[:, 0], tiles[:, 1], cos_tile, sin_tile), axis=1).reshape(-1, count)
    query = jnp.concatenate([raw[:wide], query_turned], axis=0).astype(bf)
    up_keys, up_values = wide_latent_up[:, :wide], wide_latent_up[:, wide:]
    keys = over_rows(latent_all, up_keys).astype(bf)
    values_t = over_rows(up_values, latent_all).astype(bf)
    out_t, lse = attend(first, query, keys, turned, values_t, bias, heads)

    branch = dot(out_t, wide_output, ((0,), (1,)))
    middle = own_residual + RES * col_scatter(quarters(branch, 0))
    inverse_second = inverse_of(middle, 1)
    second_in = group_gather(features_by_group((middle * inverse_second * gain_two).astype(bf)))

    gate = against(second_in, gate_t)
    upward = against(second_in, up_t)
    sigma = jax.nn.sigmoid(gate)
    hidden = (gate * sigma * upward).astype(bf)
    own_result = middle + RES * features_in_order(group_scatter(multiply(hidden, wide_back)))
    result = jnp.concatenate(col_exchange(quarters(own_result, 1)), axis=0)
    slope_down, turn = scatter_hidden(hidden, back_down, None)
    back_hidden = against(back_down, wide_back)
    back_gate = (back_hidden * upward * sigma * (1.0 + gate * (1.0 - sigma))).astype(bf)
    back_upward = (back_hidden * gate * sigma).astype(bf)
    slope_gate, turn = scatter_hidden(back_gate, second_in, turn)
    slope_up, turn = scatter_hidden(back_upward, second_in, turn)
    back_second = features_in_order(group_scatter(multiply(back_gate, gate_t) + multiply(back_upward, up_t)))
    back_norm, gain_second_part = norm_back(middle, inverse_second, gain_two, back_second, 1)
    back_middle = own_up + back_norm
    back_branch = jnp.concatenate(col_gather((RES * back_middle).astype(bf)), axis=0)

    out = out_t.T
    back_out = multiply(back_branch, wide_output).astype(bf)
    keys_t = over_rows(up_keys, latent_all).astype(bf)
    values = over_rows(latent_all, up_values).astype(bf)
    back_query_n, back_query_r, back_keys, back_values, back_turned = attend_back(
        first, query, query.T, keys, turned, keys_t, turned_t, values, back_out.T, back_out, bias, lse, heads
    )
    tiles = back_query_r.reshape(-1, 2, 64, count)
    back_turn = jnp.stack(rotate(tiles[:, 0], tiles[:, 1], cos_tile, -sin_tile), axis=1).reshape(-1, count)
    back_raw = jnp.concatenate([back_query_n, back_turn], axis=0).astype(bf)
    query_part = multiply(wide_query_up, back_raw)
    latent_back = against(up_keys, back_keys) + against(up_values, back_values)
    turned_back = jnp.sum(back_turned.T.reshape(2, 4, half, blocks * count), axis=1).reshape(DR, blocks * count)
    far = jnp.concatenate([latent_back, turned_back], axis=0)
    to_send = jnp.concatenate(
        [query_part] + [far[:, b * count : (b + 1) * count] for b in range(blocks)], axis=0
    )
    summed = col_scatter(quarters(to_send, 1))
    back_query_in = summed[:QR]
    wide_far = KR + DR
    parts = [summed[QR + b * wide_far : QR + (b + 1) * wide_far] for b in range(blocks)]
    back_key = parts[reach]
    for step in range(1, reach + 1):
        back_key = back_key + from_behind(parts[reach - step], -step)

    own_latents = pick(quarters(latents, 1))
    own_query, own_latent = own_latents[:QR], own_latents[QR : QR + KR]
    back_query_latent, query_gain_part = norm_back(
        own_query, inverse_of(own_query, 0), query_scale, back_query_in, 0
    )
    back_latent, latent_gain_part = norm_back(
        own_latent, inverse_of(own_latent, 0), latent_scale, back_key[:KR], 0
    )
    own_cosine, own_sine = pick(quarters(cosine, 1)), pick(quarters(sine, 1))
    back_front, back_behind = rotate(back_key[KR : KR + half], back_key[KR + half :], own_cosine, -own_sine)
    back_latents = jnp.concatenate([back_query_latent, back_latent, back_front, back_behind], axis=0).astype(bf)
    back_latents = jnp.concatenate(col_gather(back_latents), axis=1)
    back_slice = lax.dynamic_slice_in_dim(back_latents, column * slice_width, slice_width, 0)
    back_first = col_scatter(quarters(dot(back_slice, wide_down, ((0,), (1,))), 0))
    back_norm_first, gain_first_part = norm_back(own_residual, inverse_of(own_residual, 1), gain_one, back_first, 1)
    back_tokens = jnp.concatenate(col_exchange(quarters(back_middle + back_norm_first, 1)), axis=0)

    back_slice_n = jnp.pad(back_slice.T, ((0, 0), (0, -slice_width % 128)))
    slope_output, slope_query_up, slope_latent_up, slope_down_slice = ring_scatter(
        over_rows(back_branch, out).astype(bf),
        against(query_in, back_raw).astype(bf),
        multiply(latent_all, jnp.concatenate([back_keys, back_values], axis=1)).astype(bf),
        over_rows(first_in, back_slice_n).astype(bf),
    )
    slope_down_slice = slope_down_slice[:, :slice_width]
    slope_both = jnp.concatenate(col_gather(slope_down_slice), axis=1)

    packed = jnp.concatenate(
        [part.reshape(rows, -1) for part in (gain_first_part, gain_second_part, query_gain_part, latent_gain_part)],
        axis=1,
    )
    bit = rows // 2
    while bit >= 1:
        upper = (row // bit) % 2 == 1
        low_half, high_half = packed[:bit], packed[bit:]
        away = jnp.where(upper, low_half, high_half)
        stay = jnp.where(upper, high_half, low_half)
        packed = stay + lax.ppermute(away, "row", [(r, r ^ bit) for r in range(rows)])
        bit //= 2
    packed = packed[0]
    bit = 1
    while bit < cols:
        packed = packed + swap_col(packed, bit)
        bit *= 2
    n = gain_first.shape[0]
    m = query_gain.shape[0]

    exact = functools.partial(
        lax.dot_general,
        dimension_numbers=(((1,), (1,)), ((), ())),
        precision=lax.Precision.HIGHEST,
        preferred_element_type=f32,
    )
    return (
        result,
        back_tokens,
        packed[:n],
        slope_both[:, :QR],
        packed[2 * n : 2 * n + m],
        slope_both[:, QR:],
        packed[2 * n + m :],
        exact(slope_query_up, query_one.astype(f32)),
        exact(slope_latent_up, latent_one.astype(f32)),
        slope_output.T,
        packed[n : 2 * n],
        slope_gate.T,
        slope_up.T,
        slope_down,
    )


def solution(mesh):
    placed = (
        P("row", "col"), P(), P("row"), P("row", None), P("row"), P("row", None), P("row"), P("row", "col"),
        P("row", "col"), P("col", "row"), P("row"), P("row", "col"), P("row", "col"), P("col", "row"),
        P("row", "col"),
    )
    outs = (
        P("row", "col"), P("row", "col"), P("row"), P("row", None), P("row"), P("row", None), P("row"),
        P("row", "col"), P("row", "col"), P("col", "row"), P("row"), P("row", "col"), P("row", "col"),
        P("col", "row"),
    )
    return jax.shard_map(shards, mesh=mesh, in_specs=placed, out_specs=outs, check_vma=False)
```

```python
import functools
import math

import jax
import jax.numpy as jnp
from jax import lax
from jax.experimental import pallas as pl
from jax.experimental.pallas import tpu as pltpu
from jax.sharding import PartitionSpec as P

DN = 64
DR = 32
DV = 64
QR = 768
KR = 256
SEQ_LEN = 4096
DOC_MOST = 2000
EPS = 1e-05
RES = 1.4 / math.sqrt(62.0)
THETA = 10000.0
NEG = -1e30
LOG2E = math.log2(math.e)
SCALE = (DN + DR) ** (-0.5)
VMEM_LIMIT = 56 << 20
MESH = pl.DeviceIdType.MESH
bf = jnp.bfloat16
f32 = jnp.float32


def ring_place(row, rows):
    return row // 2 + (row % 2) * (rows - 1 - 2 * (row // 2))


def ring_row(place, rows):
    side = place // (rows // 2)
    return 2 * (place + side * (rows - 1 - 2 * place)) + side


def flip(value, bit):
    return value + bit * (1 - 2 * ((value // bit) % 2))


def ring_barrier(others):
    barrier = pltpu.get_barrier_semaphore()
    for other in others:
        pl.semaphore_signal(barrier, inc=1, device_id=other, device_id_type=MESH)
    pl.semaphore_wait(barrier, len(others))


def ring_gather_kernel(rows, n, *refs):
    blocks, (tokens_ref, back_ref), refs = refs[:n], refs[n : n + 2], refs[n + 2 :]
    wholes, (features_ref, own_back_ref), refs = refs[:n], refs[n : n + 2], refs[n + 2 :]
    own_sem, send_sem, recv_sem, col_send, col_recv = refs
    row, column = lax.axis_index("row"), lax.axis_index("col")
    place = ring_place(row, rows)
    ends = (ring_row((place + 1) % rows, rows), ring_row((place + rows - 1) % rows, rows))
    cols = features_ref.shape[1] // tokens_ref.shape[1]
    quarter = back_ref.shape[0] // cols
    peers = [flip(flip(column, 1) if k & 1 else column, 2) if k & 2 else flip(column, 1) for k in range(1, cols)]
    ring_barrier([(ends[0], column), (ends[1], column)] + [(row, peer) for peer in peers])
    lanes = pl.ds(pl.multiple_of(column * tokens_ref.shape[1], 128), tokens_ref.shape[1])

    def to_col(k, target):
        part = back_ref.at[pl.ds(pl.multiple_of(target * quarter, 128), quarter)]
        return [(tokens_ref, features_ref.at[:, lanes]), (part, own_back_ref.at[:, lanes])]

    crossing = []
    for k, peer in enumerate(peers):
        for which, (source, there) in enumerate(to_col(k, peer)):
            crossing.append(
                pltpu.make_async_remote_copy(
                    src_ref=source,
                    dst_ref=there,
                    send_sem=col_send.at[which, k],
                    recv_sem=col_recv.at[which, k],
                    device_id=(row, peer),
                    device_id_type=MESH,
                )
            )
    staying = [
        pltpu.make_async_copy(source, there, own_sem.at[n + which])
        for which, (source, there) in enumerate(to_col(-1, column))
    ]

    def own(k):
        return pltpu.make_async_copy(blocks[k], wholes[k].at[row], own_sem.at[k])

    def hop(step, side, k):
        origin = ring_row((place + (step if side else rows - step)) % rows, rows)
        return pltpu.make_async_remote_copy(
            src_ref=wholes[k].at[origin, side],
            dst_ref=wholes[k].at[origin, side],
            send_sem=send_sem.at[step, side, k],
            recv_sem=recv_sem.at[step, side, k],
            device_id=(ends[side], column),
            device_id_type=MESH,
        )

    for k in range(n):
        own(k).start()
    for k in range(n):
        own(k).wait()
        for side in (0, 1):
            hop(0, side, k).start()
    for copy in crossing + staying:
        copy.start()

    def advance(step, carry):
        for k in range(n):
            for side in (0, 1):
                hop(step - 1, side, k).wait_recv()
                hop(step, side, k).start()
        return carry

    lax.fori_loop(1, rows - 1, advance, 0)
    for k in range(n):
        for side in (0, 1):
            hop(rows - 2, side, k).wait_recv()

    def drain(step, carry):
        for k in range(n):
            for side in (0, 1):
                hop(step, side, k).wait_send()
        return carry

    lax.fori_loop(0, rows - 1, drain, 0)
    for copy in crossing + staying:
        copy.wait()


def ring_gather(blocks, tokens, back):
    rows, cols, n = lax.axis_size("row"), lax.axis_size("col"), len(blocks)
    halves = [block.reshape(2, block.shape[0] // 2, block.shape[1]) for block in blocks]
    anywhere = pl.BlockSpec(memory_space=pl.ANY)
    *wholes, features, own_back = pl.pallas_call(
        functools.partial(ring_gather_kernel, rows, n),
        out_shape=[jax.ShapeDtypeStruct((rows,) + half.shape, half.dtype) for half in halves]
        + [
            jax.ShapeDtypeStruct((tokens.shape[0], cols * tokens.shape[1]), tokens.dtype),
            jax.ShapeDtypeStruct((back.shape[0] // cols, cols * back.shape[1]), back.dtype),
        ],
        in_specs=[anywhere] * (n + 2),
        out_specs=[anywhere] * (n + 2),
        scratch_shapes=[
            pltpu.SemaphoreType.DMA((n + 2,)),
            pltpu.SemaphoreType.DMA((rows - 1, 2, n)),
            pltpu.SemaphoreType.DMA((rows - 1, 2, n)),
            pltpu.SemaphoreType.DMA((2, cols - 1)),
            pltpu.SemaphoreType.DMA((2, cols - 1)),
        ],
        compiler_params=pltpu.CompilerParams(collective_id=0, has_side_effects=True),
        name="ring_gather",
    )(*halves, tokens, back)
    wholes = [whole.reshape(rows * block.shape[0], block.shape[1]) for whole, block in zip(wholes, blocks)]
    return wholes, features, own_back


def ring_scatter_kernel(rows, n, *refs):
    terms, sums, slots, (send_sem, recv_sem) = refs[:n], refs[n : 2 * n], refs[2 * n : 3 * n], refs[3 * n :]
    row, column = lax.axis_index("row"), lax.axis_index("col")
    place = ring_place(row, rows)
    ends = (ring_row((place + 1) % rows, rows), ring_row((place + rows - 1) % rows, rows))
    ring_barrier([(ends[0], column), (ends[1], column)])

    def target(step, side):
        return ring_row((place + (1 + step if side else 2 * rows - 1 - step)) % rows, rows)

    def hop(step, side, k, source):
        return pltpu.make_async_remote_copy(
            src_ref=source,
            dst_ref=slots[k].at[step, side],
            send_sem=send_sem.at[step, side, k],
            recv_sem=recv_sem.at[step, side, k],
            device_id=(ends[side], column),
            device_id_type=MESH,
        )

    def first(side, k):
        return hop(0, side, k, terms[k].at[target(0, side), side])

    def later(step, side, k):
        return hop(step, side, k, slots[k].at[step - 1, side])

    for k in range(n):
        for side in (0, 1):
            first(side, k).start()

    def arrive(step, side, k):
        return hop(step, side, k, slots[k].at[step, side])

    def advance(step, carry):
        for k in range(n):
            for side in (0, 1):
                arrive(step - 1, side, k).wait_recv()
                total = slots[k][step - 1, side].astype(f32) + terms[k][target(step, side), side].astype(f32)
                slots[k][step - 1, side] = total.astype(slots[k].dtype)
                later(step, side, k).start()
        return carry

    lax.fori_loop(1, rows - 1, advance, 0)
    for k in range(n):
        for side in (0, 1):
            arrive(rows - 2, side, k).wait_recv()
            sums[k][side] = slots[k][rows - 2, side].astype(f32) + terms[k][row, side].astype(f32)

    def drain(step, carry):
        for k in range(n):
            for side in (0, 1):
                arrive(step, side, k).wait_send()
        return carry

    lax.fori_loop(0, rows - 1, drain, 0)


def ring_scatter(*terms):
    rows, n = lax.axis_size("row"), len(terms)
    split = [term.reshape(rows, 2, term.shape[0] // rows // 2, term.shape[1]) for term in terms]
    sums = pl.pallas_call(
        functools.partial(ring_scatter_kernel, rows, n),
        out_shape=[jax.ShapeDtypeStruct(term.shape[1:], f32) for term in split],
        in_specs=[pl.BlockSpec(memory_space=pltpu.VMEM)] * n,
        out_specs=[pl.BlockSpec(memory_space=pltpu.VMEM)] * n,
        scratch_shapes=[pltpu.VMEM((rows - 1,) + term.shape[1:], term.dtype) for term in split]
        + [pltpu.SemaphoreType.DMA((rows - 1, 2, n)), pltpu.SemaphoreType.DMA((rows - 1, 2, n))],
        compiler_params=pltpu.CompilerParams(
            collective_id=1, has_side_effects=True, vmem_limit_bytes=VMEM_LIMIT
        ),
        name="ring_scatter",
    )(*split)
    return [total.reshape(total.shape[0] * total.shape[1], total.shape[2]) for total in sums]


def from_behind(value, steps):
    count = lax.axis_size("row")
    initial, last = (max(0, -steps), min(count, count - steps))
    return lax.ppermute(value, "row", [(source, source + steps) for source in range(initial, last)])


def swap_col(value, bit):
    return lax.ppermute(value, "col", [(c, c ^ bit) for c in range(lax.axis_size("col"))])


def by_owner(pieces, own=None):
    own = lax.axis_index("col") if own is None else own
    bit = 1
    pieces = list(pieces)
    while bit < len(pieces):
        odd = (own // bit) % 2 == 1
        pieces = [jnp.where(odd, pieces[k ^ bit], pieces[k]) for k in range(len(pieces))]
        bit *= 2
    return pieces


def pick(pieces):
    return by_owner(pieces)[0]


def col_gather(own):
    across = swap_col(own, 2)
    beside = swap_col(own, 1)
    return by_owner([own, beside, across, swap_col(across, 1)])


def col_scatter(pieces):
    mine = by_owner(pieces)
    low = [piece.astype(bf) for piece in mine]
    across = mine[2].astype(f32) + swap_col(low[3], 1).astype(f32)
    beside = mine[0].astype(f32) + swap_col(low[1], 1).astype(f32)
    return beside + swap_col(across.astype(bf), 2).astype(f32)


def col_exchange(pieces):
    mine = by_owner(pieces)
    return by_owner([mine[0]] + [swap_col(mine[k], k) for k in range(1, len(mine))])


def quarters(value, axis):
    return jnp.split(value, lax.axis_size("col"), axis=axis)


PAIR = 2


def group_row(group, side):
    return (group // 2) * 4 + side * PAIR + group % 2


def own_group():
    row = lax.axis_index("row")
    return ((row // 4) * 2 + row % 2, (row // PAIR) % 2)


def swap_row(value, mask):
    return lax.ppermute(value, "row", [(r, r ^ mask) for r in range(lax.axis_size("row"))])


def group_masks():
    bits = (lax.axis_size("row") // 2).bit_length() - 1
    return [(1 << b, group_row(1 << b, 0)) for b in reversed(range(bits))]


def after(value, other):
    return lax.optimization_barrier((value, other))[0]


def features_by_group(value):
    rows = lax.axis_size("row")
    chunks = jnp.split(value, rows, axis=1)
    groups = [
        jnp.concatenate([chunks[group_row(g, side)] for side in (0, 1)], axis=1) for g in range(rows // 2)
    ]
    return jnp.concatenate(by_owner(groups, own_group()[0]), axis=1)


def features_in_order(value):
    rows = lax.axis_size("row")
    groups = by_owner(jnp.split(value, rows // 2, axis=1), own_group()[0])
    chunks = [None] * rows
    for g, group in enumerate(groups):
        for side, chunk in enumerate(jnp.split(group, 2, axis=1)):
            chunks[group_row(g, side)] = chunk
    return jnp.concatenate(chunks, axis=1)


def group_gather(own, mark):
    both = after(jnp.concatenate([own, swap_row(own, PAIR)], axis=0), mark)
    across = swap_col(both, 2)
    pieces = [both, swap_col(both, 1), across, swap_col(across, 1)]
    return jnp.concatenate([p for half in zip(*(jnp.split(piece, 2, axis=0) for piece in pieces)) for p in half], axis=0)


class GroupScatter:
    def __init__(self, value):
        x = jnp.split(value, 2 * lax.axis_size("col"), axis=0)
        self.kept = (x[0], x[2], x[4], x[6])
        self.came = swap_col(jnp.concatenate([x[1], x[3], x[5], x[7]], axis=0).astype(bf), 1)

    def add(self, mark):
        self.came = after(self.came, mark)
        return [a + b.astype(f32) for a, b in zip(self.kept, jnp.split(self.came, len(self.kept), axis=0))]

    def across(self, mark):
        y = self.add(mark)
        self.kept = (y[0], y[2])
        self.came = swap_col(jnp.concatenate([y[1], y[3]], axis=0).astype(bf), 2)

    def partner(self, mark):
        z = self.add(mark)
        self.kept = (z[0],)
        self.came = swap_row(z[1].astype(bf), PAIR)

    def result(self):
        return self.kept[0] + self.came.astype(f32)


def pair_halves(value, axis):
    low, high = jnp.split(value, 2, axis=axis)
    upper = own_group()[1] == 1
    return (jnp.where(upper, high, low), jnp.where(upper, low, high))


def in_pair_order(mine, came, axis):
    upper = own_group()[1] == 1
    return jnp.concatenate([jnp.where(upper, came, mine), jnp.where(upper, mine, came)], axis=axis)


class HiddenGather:
    def __init__(self, blocks, late):
        self.late = late
        mine, self.away = pair_halves(blocks, 1)
        self.came = swap_row(self.away, PAIR)
        self.own = in_pair_order(mine, self.came, 2)

    def near_own(self, mark):
        self.beside = swap_row(after(self.own, mark), group_masks()[-1][1])

    def far(self, late, mark):
        n = self.own.shape[0]
        own = after(self.own[n - self.late :] if late else self.own[: n - self.late], mark)
        pieces = {0: own}
        for bit, mask in group_masks()[:-1]:
            for k in list(pieces):
                pieces[k ^ bit] = swap_row(pieces[k], mask)
        return pieces

    def near(self, pieces, late, mark):
        n = self.own.shape[0]
        part = slice(n - self.late, n) if late else slice(0, n - self.late)
        done = {0: self.own[part], 1: self.beside[part]}
        for k in pieces:
            if k:
                done[k] = pieces[k]
                done[k ^ 1] = swap_row(after(pieces[k], mark), group_masks()[-1][1])
        return [done[k] for k in range(len(done))]


class HiddenScatter:
    def __init__(self, left, right):
        groups = lax.axis_size("row") // 2
        chunks = jnp.split(right, groups, axis=1)
        self.kept = [k for k in range(groups) if not k & 1]
        self.away = over_rows(left, jnp.concatenate([chunks[k | 1] for k in self.kept], axis=1)).astype(bf)
        self.total = over_rows(left, jnp.concatenate([chunks[k] for k in self.kept], axis=1))

    def near(self, mark):
        self.came = swap_row(after(self.away, mark), group_masks()[-1][1])

    def add(self):
        pieces = jnp.split(self.total + self.came.astype(f32), len(self.kept), axis=1)
        return dict(zip(self.kept, pieces))

    def far(self, mark):
        for bit, mask in reversed(group_masks()[:-1]):
            self.came = after(self.came, mark)
            pieces = self.add()
            away = [k for k in self.kept if k & bit]
            self.kept = [k for k in self.kept if not k & bit]
            self.total = jnp.concatenate([pieces[k] for k in self.kept], axis=1)
            self.came = swap_row(jnp.concatenate([pieces[k] for k in away], axis=1).astype(bf), mask)

    def halves(self):
        return pair_halves(self.add()[0].astype(bf), 1)


COLS = (("col", 1), ("col", 2))
GROUP = COLS + (("row", PAIR),)


class Cube:
    def __init__(self, dims, parts):
        self.dims, self.parts = dims, parts
        self.row, self.column = lax.axis_index("row"), lax.axis_index("col")
        self.masks = range(1, 1 << len(dims))

    def device(self, mask):
        row, column = self.row, self.column
        for k, (axis, bit) in enumerate(self.dims):
            if mask >> k & 1:
                row, column = (flip(row, bit), column) if axis == "row" else (row, flip(column, bit))
        return (row, column)

    def partner(self):
        return (flip(self.row, PAIR), self.column)

    def greet(self, cargo):
        others = [self.device(1 << k) for k in range(len(self.dims))] + [self.partner()] * cargo
        barrier = pltpu.get_barrier_semaphore()
        for other in others:
            pl.semaphore_signal(barrier, inc=1, device_id=other, device_id_type=MESH)
        pl.semaphore_wait(barrier, len(others))

    def ship(self, cargo):
        return [
            pltpu.make_async_remote_copy(
                src_ref=cargo[0],
                dst_ref=cargo[1],
                send_sem=cargo[2],
                recv_sem=cargo[3],
                device_id=self.partner(),
                device_id_type=MESH,
            )
        ] if cargo else []

    def order(self, part):
        slow = list(range(1, len(self.dims)))
        return [0] + (slow[::-1] if part % 2 else slow)


def cut(ref, index, rows, width):
    if width is None:
        return ref.at[index, rows]
    return ref.at[rows, pl.ds(pl.multiple_of(index * width, 128), width)]


def unpack(cargo, refs, inputs, outputs):
    if not cargo:
        return (refs, ())
    own, swapped = refs[inputs], refs[inputs + 1 + outputs]
    rest = refs[:inputs] + refs[inputs + 1 : inputs + 1 + outputs] + refs[inputs + outputs + 2 : -2]
    return (rest, (own, swapped) + tuple(refs[-2:]))


def spread_kernel(dims, parts, lanes, relative, cargo, *refs):
    (own_ref, all_ref, own_sem, send_sem, recv_sem), cargo = unpack(cargo, refs, 1, 1)
    cube = Cube(dims, parts)
    cube.greet(len(cargo) > 0)
    ship = cube.ship(cargo)
    for copy in ship:
        copy.start()
    height, width = own_ref.shape
    size = height // parts
    width = width if lanes else None

    def index(mask):
        return mask if relative else cube.device(mask)[1]

    def rows(part):
        return pl.ds(part * size, size)

    own = pltpu.make_async_copy(own_ref, cut(all_ref, index(0), pl.ds(0, height), width), own_sem)
    own.start()

    def hop(part, mask, k):
        there = mask | 1 << k
        target = there if relative else index(mask)
        source = cut(all_ref, index(mask), rows(part), width) if mask else own_ref.at[rows(part)]
        return pltpu.make_async_remote_copy(
            src_ref=source,
            dst_ref=cut(all_ref, target, rows(part), width),
            send_sem=send_sem.at[part, there],
            recv_sem=recv_sem.at[part, there],
            device_id=cube.device(1 << k),
            device_id_type=MESH,
        )

    def arrival(part, mask):
        view = cut(all_ref, index(mask), rows(part), width)
        return pltpu.make_async_remote_copy(
            src_ref=view,
            dst_ref=view,
            send_sem=send_sem.at[part, mask],
            recv_sem=recv_sem.at[part, mask],
            device_id=cube.device(1),
            device_id_type=MESH,
        )

    sent = []
    for part in range(parts):
        for k in cube.order(part)[::-1]:
            sent.append(hop(part, 0, k))
            sent[-1].start()
    last = []
    for bits in range(1, len(dims)):
        for part in range(parts):
            order = cube.order(part)[::-1]
            for mask in cube.masks:
                if bin(mask).count("1") != bits:
                    continue
                further = order[max(order.index(k) for k in range(len(dims)) if mask >> k & 1) + 1 :]
                if not further:
                    last.append((part, mask))
                    continue
                arrival(part, mask).wait_recv()
                for k in further:
                    sent.append(hop(part, mask, k))
                    sent[-1].start()
    last += [(part, cube.masks[-1]) for part in range(parts)]
    for part, mask in last:
        arrival(part, mask).wait_recv()
    for copy in sent:
        copy.wait_send()
    own.wait()
    for copy in ship:
        copy.wait()


def cargo_parts(cargo):
    if cargo is None:
        return ([], [], [])
    anywhere = pl.BlockSpec(memory_space=pl.ANY)
    return ([anywhere], [jax.ShapeDtypeStruct(cargo.shape, cargo.dtype)], [pltpu.SemaphoreType.DMA] * 2)


def spread(own, dims, parts, number, lanes=False, relative=False, cargo=None):
    specs, shapes, semaphores = cargo_parts(cargo)
    count = 1 << len(dims)
    shape = (own.shape[0], count * own.shape[1]) if lanes else (count,) + own.shape
    whole, *swapped = pl.pallas_call(
        functools.partial(spread_kernel, dims, parts, lanes, relative, cargo is not None),
        out_shape=[jax.ShapeDtypeStruct(shape, own.dtype)] + shapes,
        in_specs=[pl.BlockSpec(memory_space=pl.ANY)] + specs,
        out_specs=[pl.BlockSpec(memory_space=pl.ANY)] + specs,
        scratch_shapes=[
            pltpu.SemaphoreType.DMA,
            pltpu.SemaphoreType.DMA((parts, count)),
            pltpu.SemaphoreType.DMA((parts, count)),
        ]
        + semaphores,
        compiler_params=pltpu.CompilerParams(collective_id=number, has_side_effects=True),
        name=f"spread{number}",
    )(*([own] if cargo is None else [own, cargo]))
    whole = whole if lanes else whole.reshape(count * own.shape[0], own.shape[1])
    return (whole, swapped[0]) if swapped else whole


def fold_kernel(dims, parts, lanes, relative, cargo, *refs):
    (terms_ref, sum_ref, arrive_ref, leave_ref, send_sem, recv_sem), cargo = unpack(cargo, refs, 1, 1)
    cube = Cube(dims, parts)
    cube.greet(len(cargo) > 0)
    ship = cube.ship(cargo)
    for copy in ship:
        copy.start()
    height, width = sum_ref.shape
    size = height // parts
    width = width if lanes else None

    def term(part, mask):
        return cut(terms_ref, mask if relative else cube.device(mask)[1], pl.ds(part * size, size), width)

    def hop(part, mask, k, source):
        return pltpu.make_async_remote_copy(
            src_ref=source,
            dst_ref=arrive_ref.at[mask, pl.ds(part * size, size)],
            send_sem=send_sem.at[part, mask],
            recv_sem=recv_sem.at[part, mask],
            device_id=cube.device(1 << k),
            device_id_type=MESH,
        )

    sent = []
    for stage in range(len(dims) + 1):
        for part in range(parts):
            rows = pl.ds(part * size, size)
            order = cube.order(part)
            done = sum(1 << k for k in order[:stage])
            if stage:
                for mask in range(1 << len(dims)):
                    if not mask & done:
                        there = mask | 1 << order[stage - 1]
                        hop(part, there, order[stage - 1], arrive_ref.at[there, rows]).wait_recv()
            going = [0] if stage == len(dims) else [m for m in cube.masks if not m & done and m >> order[stage] & 1]
            for mask in going:
                source = term(part, mask)
                if stage:
                    total = source[...].astype(f32)
                    for k in order[:stage]:
                        total = total + arrive_ref[mask | 1 << k, rows].astype(f32)
                    if mask == 0:
                        sum_ref[rows] = total
                        continue
                    leave_ref[mask, rows] = total.astype(bf)
                    source = leave_ref.at[mask, rows]
                sent.append(hop(part, mask, order[stage], source))
                sent[-1].start()
    for copy in sent:
        copy.wait_send()
    for copy in ship:
        copy.wait()


def fold(terms, dims, parts, number, lanes=False, relative=False, cargo=None):
    count = 1 << len(dims)
    terms = terms.astype(bf)
    if lanes:
        shape = (terms.shape[0], terms.shape[1] // count)
    else:
        shape = (terms.shape[0] // count, terms.shape[1])
        terms = terms.reshape((count,) + shape)
    specs, shapes, semaphores = cargo_parts(cargo)
    total, *swapped = pl.pallas_call(
        functools.partial(fold_kernel, dims, parts, lanes, relative, cargo is not None),
        out_shape=[jax.ShapeDtypeStruct(shape, f32)] + shapes,
        in_specs=[pl.BlockSpec(memory_space=pltpu.VMEM)] + specs,
        out_specs=[pl.BlockSpec(memory_space=pltpu.VMEM)] + specs,
        scratch_shapes=[
            pltpu.VMEM((count,) + shape, bf),
            pltpu.VMEM((count,) + shape, bf),
            pltpu.SemaphoreType.DMA((parts, count)),
            pltpu.SemaphoreType.DMA((parts, count)),
        ]
        + semaphores,
        compiler_params=pltpu.CompilerParams(
            collective_id=number, has_side_effects=True, vmem_limit_bytes=VMEM_LIMIT
        ),
        name=f"fold{number}",
    )(*([terms] if cargo is None else [terms, cargo]))
    return (total, swapped[0]) if swapped else total


def dot(left, right, dims):
    return lax.dot_general(left, right, (dims, ((), ())), preferred_element_type=f32)


def multiply(left, right):
    return dot(left, right, ((1,), (0,)))


def against(left, right):
    return dot(left, right, ((1,), (1,)))


def over_rows(left, right):
    return dot(left, right, ((0,), (0,)))


def inverse_of(value, axis):
    return lax.rsqrt(jnp.mean(value * value, axis=axis, keepdims=True) + EPS)


def norm_back(value, inverse, gain, upstream, axis):
    unit = value * inverse
    scaled = upstream * gain
    inward = inverse * (scaled - unit * jnp.mean(scaled * unit, axis=axis, keepdims=True))
    return (inward, jnp.sum(upstream * unit, axis=1 - axis))


def angles(start, count):
    place = ((start + jnp.arange(count, dtype=jnp.int32)) % SEQ_LEN).astype(f32)
    half = DR // 2
    freq = jnp.exp(jnp.arange(half, dtype=f32) * (-math.log(THETA) / half))
    turn = freq[:, None] * place[None, :]
    return (jnp.cos(turn), jnp.sin(turn))


def rotate(front, behind, cosine, sine):
    return (front * cosine - behind * sine, behind * cosine + front * sine)


def query_columns(heads):
    tiles = -(-heads // 4)
    column = lax.iota(jnp.int32, heads * DN + tiles * 128)
    plain = (column // DN) * (DN + DR) + column % DN
    rest = column - heads * DN
    head = (rest // 128) * 4 + (rest % 64) // 16
    turned = head * (DN + DR) + DN + ((rest % 128) // 64) * 16 + rest % 16
    turned = jnp.where(head < heads, turned, -1)
    return jnp.where(column < heads * DN, plain, turned)


def latent_columns(heads):
    column = lax.iota(jnp.int32, heads * (DN + DV))
    rest = column % (heads * DN)
    return (rest // DN) * (DN + DV) + rest % DN + (column // (heads * DN)) * DN


def chosen(origin, width):
    return lax.broadcasted_iota(jnp.int32, (width, origin.shape[0]), 0) == origin[None, :]


BLOCK = 512


def head_rows(step, side, shape, axis):
    place = lax.broadcasted_iota(jnp.int32, shape, axis)
    plain = (place // DN == side).astype(f32).astype(bf)
    turned = ((place % 64) // 16 == 2 * (step % 2) + side).astype(f32).astype(bf)
    return (plain, turned)


def attend_kernel(blocks, first_ref, qn_ref, qr_ref, k_ref, kr_ref, vt_ref, bias_ref, o_ref, lse_ref, s_ref):
    step = pl.program_id(0)
    first = first_ref[0]
    count = qn_ref.shape[1]
    for side in (0, 1):
        plain, turned = head_rows(step, side, qn_ref.shape, 0)
        right = jnp.concatenate([qn_ref[...] * plain, qr_ref[...] * turned], axis=0)

        def score(j, top):
            rows = pl.ds(pl.multiple_of(j * BLOCK, BLOCK), BLOCK)
            left = jnp.concatenate([k_ref[rows, :], kr_ref[rows, :]], axis=1)
            s = multiply(left, right) * (SCALE * LOG2E) + bias_ref[rows, :]
            s_ref[rows, :] = s
            return jnp.maximum(top, jnp.max(s, axis=0, keepdims=True))

        top = lax.fori_loop(first, blocks, score, jnp.full((1, count), NEG, f32))

        def gather(j, carry):
            total, out = carry
            rows = pl.ds(pl.multiple_of(j * BLOCK, BLOCK), BLOCK)
            chance = jnp.exp2(s_ref[rows, :] - top)
            total = total + jnp.sum(chance, axis=0, keepdims=True)
            out = out + multiply(vt_ref[side * DV : (side + 1) * DV, rows], chance.astype(bf))
            return (total, out)

        total, out = lax.fori_loop(
            first, blocks, gather, (jnp.zeros((1, count), f32), jnp.zeros((DV, count), f32))
        )
        o_ref[side * DV : (side + 1) * DV, :] = (out / total).astype(bf)
        lse_ref[0, side : side + 1, :] = top + jnp.log2(total)


def attend(first, query, keys, turned_keys, values_t, bias, heads):
    count, kl = query.shape[1], keys.shape[0]
    pairs, base = heads // 2, heads * DN // 128
    grid = pltpu.PrefetchScalarGridSpec(
        num_scalar_prefetch=1,
        grid=(pairs,),
        in_specs=[
            pl.BlockSpec((128, count), lambda p, s: (p, 0)),
            pl.BlockSpec((128, count), lambda p, s: (base + p // 2, 0)),
            pl.BlockSpec((kl, 128), lambda p, s: (0, p)),
            pl.BlockSpec((kl, 128), lambda p, s: (0, 0)),
            pl.BlockSpec((128, kl), lambda p, s: (p, 0)),
            pl.BlockSpec((kl, count), lambda p, s: (0, 0)),
        ],
        out_specs=[
            pl.BlockSpec((128, count), lambda p, s: (p, 0)),
            pl.BlockSpec((1, 2, count), lambda p, s: (p, 0, 0)),
        ],
        scratch_shapes=[pltpu.VMEM((kl, count), f32)],
    )
    return pl.pallas_call(
        functools.partial(attend_kernel, kl // BLOCK),
        grid_spec=grid,
        out_shape=[
            jax.ShapeDtypeStruct((heads * DV, count), bf),
            jax.ShapeDtypeStruct((pairs, 2, count), f32),
        ],
        compiler_params=pltpu.CompilerParams(vmem_limit_bytes=VMEM_LIMIT),
        name="attend",
    )(first, query, query, keys, turned_keys, values_t, bias)


def attend_back_kernel(
    blocks, first_ref, qn_ref, qr_ref, qnn_ref, qrn_ref, k_ref, kr_ref, kt_ref, krt_ref, v_ref, dot_ref, do_ref,
    bias_ref, lse_ref, dqn_ref, dqr_ref, dk_ref, dv_ref, dkr_ref, p_ref, dp_ref,
):
    step = pl.program_id(0)
    first = first_ref[0]
    count = qn_ref.shape[1]

    @pl.when(step == 0)
    def _():
        dkr_ref[...] = jnp.zeros_like(dkr_ref)

    @pl.when(step % 2 == 0)
    def _():
        dqr_ref[...] = jnp.zeros_like(dqr_ref)

    dk_ref[...] = jnp.zeros_like(dk_ref)
    dv_ref[...] = jnp.zeros_like(dv_ref)
    for side in (0, 1):
        plain, turned = head_rows(step, side, qn_ref.shape, 0)
        right = jnp.concatenate([qn_ref[...] * plain, qr_ref[...] * turned], axis=0)
        out_right = dot_ref[...] * plain
        lse = lse_ref[0, side : side + 1, :]

        def score(j, delta):
            rows = pl.ds(pl.multiple_of(j * BLOCK, BLOCK), BLOCK)
            left = jnp.concatenate([k_ref[rows, :], kr_ref[rows, :]], axis=1)
            s = multiply(left, right) * (SCALE * LOG2E) + bias_ref[rows, :]
            chance = jnp.exp2(s - lse)
            p_ref[rows, :] = chance
            back = multiply(v_ref[rows, :], out_right)
            dp_ref[rows, :] = back
            return delta + jnp.sum(chance * back, axis=0, keepdims=True)

        delta = lax.fori_loop(first, blocks, score, jnp.zeros((1, count), f32))
        plain_l, turned_l = head_rows(step, side, qnn_ref.shape, 1)
        query_right = jnp.concatenate([qnn_ref[...] * plain_l, qrn_ref[...] * turned_l], axis=1)
        value_right = do_ref[...] * plain_l

        def spread(j, dq):
            rows = pl.ds(pl.multiple_of(j * BLOCK, BLOCK), BLOCK)
            chance = p_ref[rows, :]
            ds = (chance * (dp_ref[rows, :] - delta)).astype(bf)
            left = jnp.concatenate([kt_ref[:, rows], krt_ref[:, rows]], axis=0)
            dq = dq + multiply(left, ds)
            dk = multiply(ds, query_right)
            dk_ref[rows, :] += (dk[:, :128] * SCALE).astype(bf)
            dkr_ref[rows, :] += dk[:, 128:] * SCALE
            dv_ref[rows, :] += multiply(chance.astype(bf), value_right).astype(bf)
            return dq

        dq = lax.fori_loop(first, blocks, spread, jnp.zeros((256, count), f32)) * SCALE
        dqn_ref[side * DN : (side + 1) * DN, :] = dq[side * DN : (side + 1) * DN]
        place = lax.broadcasted_iota(jnp.int32, (128, count), 0)
        dqr_ref[...] += jnp.where((place % 64) // 16 == 2 * (step % 2) + side, dq[128:], 0.0)


def attend_back(first, query, query_n, keys, turned_keys, keys_t, turned_keys_t, values, do_t, do, bias, lse, heads):
    count, kl = query.shape[1], keys.shape[0]
    pairs, base, tiles = heads // 2, heads * DN // 128, -(-heads // 4)
    across = lambda p, s: (0, p)
    along = lambda p, s: (p, 0)
    fixed = lambda p, s: (0, 0)
    grid = pltpu.PrefetchScalarGridSpec(
        num_scalar_prefetch=1,
        grid=(pairs,),
        in_specs=[
            pl.BlockSpec((128, count), along),
            pl.BlockSpec((128, count), lambda p, s: (base + p // 2, 0)),
            pl.BlockSpec((count, 128), across),
            pl.BlockSpec((count, 128), lambda p, s: (0, base + p // 2)),
            pl.BlockSpec((kl, 128), across),
            pl.BlockSpec((kl, 128), fixed),
            pl.BlockSpec((128, kl), along),
            pl.BlockSpec((128, kl), fixed),
            pl.BlockSpec((kl, 128), across),
            pl.BlockSpec((128, count), along),
            pl.BlockSpec((count, 128), across),
            pl.BlockSpec((kl, count), fixed),
            pl.BlockSpec((1, 2, count), lambda p, s: (p, 0, 0)),
        ],
        out_specs=[
            pl.BlockSpec((128, count), along),
            pl.BlockSpec((128, count), lambda p, s: (p // 2, 0)),
            pl.BlockSpec((kl, 128), across),
            pl.BlockSpec((kl, 128), across),
            pl.BlockSpec((kl, 128), fixed),
        ],
        scratch_shapes=[pltpu.VMEM((kl, count), f32), pltpu.VMEM((kl, count), f32)],
    )
    return pl.pallas_call(
        functools.partial(attend_back_kernel, kl // BLOCK),
        grid_spec=grid,
        out_shape=[
            jax.ShapeDtypeStruct((heads * DN, count), f32),
            jax.ShapeDtypeStruct((tiles * 128, count), f32),
            jax.ShapeDtypeStruct((kl, heads * DN), bf),
            jax.ShapeDtypeStruct((kl, heads * DV), bf),
            jax.ShapeDtypeStruct((kl, 128), f32),
        ],
        compiler_params=pltpu.CompilerParams(vmem_limit_bytes=VMEM_LIMIT),
        name="attend_back",
    )(first, query, query, query_n, query_n, keys, turned_keys, keys_t, turned_keys_t, values, do_t, do, bias, lse)


TOKENS = 256


def dot_pieces(left, pieces, which):
    width = pieces[0].shape[2]
    total = None
    for k, piece in enumerate(pieces):
        term = against(left[:, k * width : (k + 1) * width], piece[which])
        total = term if total is None else total + term
    return total


def ffn_kernel(n, x_ref, *refs):
    pieces, (gate_ref, up_ref, hidden_ref) = refs[:n], refs[n:]
    gate = dot_pieces(x_ref, pieces, 0)
    upward = dot_pieces(x_ref, pieces, 1)
    gate_ref[...] = gate
    up_ref[...] = upward
    hidden_ref[...] = (gate / (1.0 + jnp.exp(-gate)) * upward).astype(bf)


def piece_specs(pieces, count):
    shape = (count,) + pieces[0].shape[1:]
    return [pl.BlockSpec(shape, lambda i: (0, 0, 0), pipeline_mode=pl.Buffered(1)) for _ in pieces]


def ffn(x, pieces):
    tokens, hidden = x.shape[0], pieces[0].shape[1]
    tile = lambda width: pl.BlockSpec((TOKENS, width), lambda i: (i, 0))
    return pl.pallas_call(
        functools.partial(ffn_kernel, len(pieces)),
        grid=(tokens // TOKENS,),
        out_shape=[
            jax.ShapeDtypeStruct((tokens, hidden), f32),
            jax.ShapeDtypeStruct((tokens, hidden), f32),
            jax.ShapeDtypeStruct((tokens, hidden), bf),
        ],
        in_specs=[tile(x.shape[1])] + piece_specs(pieces, 2),
        out_specs=[tile(hidden)] * 3,
        compiler_params=pltpu.CompilerParams(vmem_limit_bytes=VMEM_LIMIT),
        name="ffn",
    )(x, *pieces)


def ffn_back_kernel(n, dm_ref, gate_ref, up_ref, hidden_ref, *refs):
    first, down, (dgate_ref, dup_ref, dx_ref, out_ref) = refs[:n], refs[n : 2 * n], refs[2 * n :]
    width = down[0].shape[2]
    back_hidden = dot_pieces(dm_ref, down, 0)
    gate, upward = gate_ref[...], up_ref[...]
    sigma = 1.0 / (1.0 + jnp.exp(-gate))
    dgate_ref[...] = (back_hidden * upward * sigma * (1.0 + gate * (1.0 - sigma))).astype(bf)
    dup_ref[...] = (back_hidden * gate * sigma).astype(bf)
    for k in range(n):
        lanes = slice(k * width, (k + 1) * width)
        dx_ref[:, lanes] = (multiply(dgate_ref[...], first[k][0]) + multiply(dup_ref[...], first[k][1])).astype(bf)
        out_ref[:, lanes] = multiply(hidden_ref[...], down[k][0]).astype(bf)


def ffn_back(dm, gate, upward, hidden, pieces, down):
    tokens, units = gate.shape
    tile = lambda width: pl.BlockSpec((TOKENS, width), lambda i: (i, 0))
    return pl.pallas_call(
        functools.partial(ffn_back_kernel, len(pieces)),
        grid=(tokens // TOKENS,),
        out_shape=[
            jax.ShapeDtypeStruct((tokens, units), bf),
            jax.ShapeDtypeStruct((tokens, units), bf),
            jax.ShapeDtypeStruct(dm.shape, bf),
            jax.ShapeDtypeStruct(dm.shape, bf),
        ],
        in_specs=[tile(dm.shape[1]), tile(units), tile(units), tile(units)]
        + piece_specs(pieces, 2)
        + piece_specs(down, 1),
        out_specs=[tile(units), tile(units), tile(dm.shape[1]), tile(dm.shape[1])],
        compiler_params=pltpu.CompilerParams(vmem_limit_bytes=VMEM_LIMIT),
        name="ffn_back",
    )(dm, gate, upward, hidden, *pieces, *down)


def shards(
    tokens, document_ids, gain_first, query_down, query_gain, latent_down, latent_gain, query_up, latent_up,
    output_weight, gain_second, gate_weight, up_weight, down_weight, cotangent,
):
    count, own_width = tokens.shape
    rows, cols = lax.axis_size("row"), lax.axis_size("col")
    row, column = lax.axis_index("row"), lax.axis_index("col")
    start = row * count
    heads = query_up.shape[1] // (DN + DR)
    reach = -(-(DOC_MOST - 1) // count)
    blocks = reach + 1
    wide = heads * DN
    quarter = count // cols
    cosine, sine = angles(start, count)

    both_down = jnp.concatenate([query_down, latent_down], axis=1).astype(bf)
    down_slice = pick(quarters(both_down, 1))
    slice_width = down_slice.shape[1]
    small = jnp.concatenate([query_gain, latent_gain]).astype(bf)
    small = jnp.pad(small, (0, gain_first.shape[0] - small.shape[0]))
    gains = jnp.stack([gain_first.astype(bf), gain_second.astype(bf), small], axis=1)
    query_one = chosen(query_columns(heads), heads * (DN + DR))
    latent_one = chosen(latent_columns(heads), heads * (DN + DV))
    query_up_low = multiply(query_up.astype(bf), query_one.astype(bf)).astype(bf)
    latent_up_low = multiply(latent_up.astype(bf), latent_one.astype(bf)).astype(bf)
    down_block = jnp.concatenate([down_slice, gains], axis=1)
    down_block = jnp.pad(down_block, ((0, 0), (0, -down_block.shape[1] % 128)))
    ffn_weights = HiddenGather(
        jnp.stack([gate_weight.astype(bf).T, up_weight.astype(bf).T, down_weight.astype(bf)]), 1
    )
    (wide_down, wide_query_up, wide_latent_up), features, own_up = ring_gather(
        (after(down_block, ffn_weights.away), query_up_low, latent_up_low), tokens, cotangent
    )
    wide_output = lax.all_gather(after(output_weight, wide_down).astype(bf).T, "row", axis=0, tiled=True)
    gain_one = wide_down[:, slice_width].astype(f32)
    gain_two = wide_down[:, slice_width + 1].astype(f32)
    small_gains = wide_down[:, slice_width + 2].reshape(rows, -1).astype(f32)
    own_q = query_gain.shape[0]
    query_scale = small_gains[:, :own_q].reshape(-1)[:, None]
    latent_scale = small_gains[:, own_q : own_q + latent_gain.shape[0]].reshape(-1)[:, None]
    wide_down = wide_down[:, :slice_width]

    residual = features.astype(f32)
    first_in = (residual * inverse_of(residual, 1) * gain_one).astype(bf)
    own_residual = pick(quarters(features, 0)).astype(f32)

    latents = jnp.concatenate(col_gather(dot(wide_down, first_in, ((0,), (1,)))), axis=0)
    query_latent, latent_part = latents[:QR], latents[QR : QR + KR]
    inverse_query, inverse_latent = inverse_of(query_latent, 0), inverse_of(latent_part, 0)
    query_in = (query_latent * inverse_query * query_scale).astype(bf)
    latent_in = (latent_part * inverse_latent * latent_scale).astype(bf)
    half = DR // 2
    key_front, key_back = rotate(latents[QR + KR : QR + KR + half], latents[QR + KR + half :], cosine, sine)
    key_part = jnp.concatenate([latent_in, key_front.astype(bf), key_back.astype(bf)], axis=0)
    key_part = after(key_part, ffn_weights.came)
    key_parts = jnp.concatenate([from_behind(key_part, step) for step in range(reach, 0, -1)] + [key_part], axis=1)
    ffn_weights.near_own(key_parts)
    far_first = ffn_weights.far(False, key_parts)
    back_down = group_gather(features_by_group((RES * own_up).astype(bf)), key_parts)
    latent_all = key_parts[:KR]
    turned_t = jnp.concatenate([key_parts[KR : KR + half]] * 4 + [key_parts[KR + half :]] * 4, axis=0)
    turned = turned_t.T

    key_place = start - reach * count + jnp.arange(blocks * count, dtype=jnp.int32)
    place = start + jnp.arange(count, dtype=jnp.int32)
    key_doc = lax.dynamic_slice_in_dim(jnp.pad(document_ids, (reach * count, 0)), start, blocks * count)
    doc = lax.dynamic_slice_in_dim(document_ids, start, count)
    allowed = (key_doc[:, None] == doc[None, :]) & (key_place[:, None] <= place[None, :])
    allowed = allowed & (key_place[:, None] >= (place // SEQ_LEN * SEQ_LEN)[None, :])
    bias = jnp.where(allowed, 0.0, NEG).astype(f32)
    doc_start = jnp.sum((document_ids < doc[0]).astype(jnp.int32))
    first = jnp.clip((doc_start - (start - reach * count)) // BLOCK, 0, reach).reshape(1)

    raw = over_rows(wide_query_up, query_in)
    tiles = raw[wide:].reshape(-1, 2, 64, count)
    cos_tile, sin_tile = jnp.tile(cosine, (4, 1)), jnp.tile(sine, (4, 1))
    query_turned = jnp.stack(rotate(tiles[:, 0], tiles[:, 1], cos_tile, sin_tile), axis=1).reshape(-1, count)
    query = jnp.concatenate([raw[:wide], query_turned], axis=0).astype(bf)
    up_keys, up_values = wide_latent_up[:, :wide], wide_latent_up[:, wide:]
    keys = over_rows(latent_all, up_keys).astype(bf)
    values_t = over_rows(up_values, latent_all).astype(bf)
    out_t, lse = attend(first, query, keys, turned, values_t, bias, heads)

    out_t = after(out_t, ffn_weights.beside)
    branch = after(dot(out_t, wide_output, ((0,), (1,))), back_down)
    middle = own_residual + RES * fold(branch, COLS, 4, 4)
    middle = after(middle, [piece for k, piece in far_first.items() if k])
    far_down = ffn_weights.far(True, middle)
    first_pieces = ffn_weights.near(far_first, False, middle)
    inverse_second = inverse_of(middle, 1)
    second_in = features_by_group((middle * inverse_second * gain_two).astype(bf))
    second_in = spread(second_in, GROUP, 4, 5, relative=True)

    gate, upward, hidden = ffn(second_in, first_pieces)
    down_pieces = ffn_weights.near(far_down, True, second_in)
    slope_down = HiddenScatter(hidden, back_down)
    slope_down.near(hidden)
    back_gate, back_upward, back_second, out_part = ffn_back(
        back_down, gate, upward, hidden, first_pieces, down_pieces
    )
    slope_gate = HiddenScatter(back_gate, second_in)
    slope_gate.near(back_gate)
    back_second = after(back_second, slope_gate.away)
    back_second = features_in_order(fold(back_second, GROUP, 4, 6, relative=True))
    slope_up = HiddenScatter(back_upward, second_in)
    own_result = GroupScatter(out_part)
    back_norm, gain_second_part = norm_back(middle, inverse_second, gain_two, back_second, 1)
    back_middle = own_up + back_norm
    back_branch = after((RES * back_middle).astype(bf), (slope_down.came, own_result.came, slope_up.away))
    slope_up.near(back_branch)
    slope_down.far(back_branch)
    back_branch = spread(back_branch, COLS, 4, 7)
    own_result.across(back_branch)

    out = out_t.T
    back_out = multiply(back_branch, wide_output).astype(bf)
    slope_output = lax.psum_scatter(
        over_rows(back_branch, out).astype(bf), "row", scatter_dimension=0, tiled=True
    )
    slope_gate.far(back_out)
    keys_t = over_rows(up_keys, latent_all).astype(bf)
    values = over_rows(latent_all, up_values).astype(bf)
    back_query_n, back_query_r, back_keys, back_values, back_turned = attend_back(
        first, query, query.T, keys, turned, keys_t, turned_t, values, back_out.T, back_out, bias, lse, heads
    )
    back_query_n = after(back_query_n, (slope_down.came, slope_up.came, own_result.came))
    slope_up.far(back_query_n)
    own_result.partner(back_query_n)
    tiles = back_query_r.reshape(-1, 2, 64, count)
    back_turn = jnp.stack(rotate(tiles[:, 0], tiles[:, 1], cos_tile, -sin_tile), axis=1).reshape(-1, count)
    back_raw = jnp.concatenate([back_query_n, back_turn], axis=0).astype(bf)
    query_part = multiply(wide_query_up, back_raw)
    latent_back = against(up_keys, back_keys) + against(up_values, back_values)
    turned_back = jnp.sum(back_turned.T.reshape(2, 4, half, blocks * count), axis=1).reshape(DR, blocks * count)
    far = jnp.concatenate([latent_back, turned_back], axis=0)
    to_send = jnp.concatenate(
        [query_part] + [far[:, b * count : (b + 1) * count] for b in range(blocks)], axis=0
    )
    to_send = after(to_send, (slope_gate.came, own_result.came))
    slope_down, away = slope_down.halves()
    summed, came = fold(to_send, COLS, 3, 8, lanes=True, cargo=away)
    slope_down = in_pair_order(slope_down, came, 0)
    own_result = after(middle + RES * features_in_order(own_result.result()), summed)
    result = jnp.concatenate(col_exchange(quarters(own_result, 1)), axis=0)
    back_query_in = summed[:QR]
    wide_far = KR + DR
    parts = [summed[QR + b * wide_far : QR + (b + 1) * wide_far] for b in range(blocks)]
    back_key = parts[reach]
    for step in range(1, reach + 1):
        back_key = back_key + from_behind(parts[reach - step], -step)

    own_latents = pick(quarters(latents, 1))
    own_query, own_latent = own_latents[:QR], own_latents[QR : QR + KR]
    back_query_latent, query_gain_part = norm_back(
        own_query, inverse_of(own_query, 0), query_scale, back_query_in, 0
    )
    back_latent, latent_gain_part = norm_back(
        own_latent, inverse_of(own_latent, 0), latent_scale, back_key[:KR], 0
    )
    own_cosine, own_sine = pick(quarters(cosine, 1)), pick(quarters(sine, 1))
    back_front, back_behind = rotate(back_key[KR : KR + half], back_key[KR + half :], own_cosine, -own_sine)
    back_latents = jnp.concatenate([back_query_latent, back_latent, back_front, back_behind], axis=0).astype(bf)
    back_latents = spread(back_latents, COLS, 3, 9, lanes=True)
    back_slice = lax.dynamic_slice_in_dim(back_latents, column * slice_width, slice_width, 0)
    slope_gate, away = after(slope_gate.halves(), (result, slope_up.came))
    back_first, came = fold(dot(back_slice, wide_down, ((0,), (1,))), COLS, 4, 10, cargo=away)
    slope_gate = in_pair_order(slope_gate, came, 0)
    back_norm_first, gain_first_part = norm_back(own_residual, inverse_of(own_residual, 1), gain_one, back_first, 1)
    back_tokens = jnp.concatenate(col_exchange(quarters(back_middle + back_norm_first, 1)), axis=0)

    packed = jnp.concatenate(
        [part.reshape(rows, -1) for part in (gain_first_part, gain_second_part, query_gain_part, latent_gain_part)],
        axis=1,
    )
    packed = jnp.pad(packed, ((0, 0), (0, -packed.shape[1] % 256))).reshape(-1, 128)
    back_slice_n = jnp.pad(back_slice.T, ((0, 0), (0, -slice_width % 128)))
    slope_query_up, slope_latent_up, slope_down_slice, packed = ring_scatter(
        against(query_in, back_raw).astype(bf),
        multiply(latent_all, jnp.concatenate([back_keys, back_values], axis=1)).astype(bf),
        over_rows(first_in, back_slice_n).astype(bf),
        packed,
    )
    slope_up, away = slope_up.halves()
    slope_both, came = spread(slope_down_slice.astype(bf), COLS, 2, 11, lanes=True, cargo=away)
    slope_up = in_pair_order(slope_up, came, 0)
    slope_both = jnp.concatenate([piece[:, :slice_width] for piece in quarters(slope_both, 1)], axis=1).astype(f32)
    packed = packed.reshape(-1)
    bit = 1
    while bit < cols:
        packed = packed + swap_col(packed, bit)
        bit *= 2
    n = gain_first.shape[0]
    m = query_gain.shape[0]
    k = latent_gain.shape[0]

    exact = functools.partial(
        lax.dot_general,
        dimension_numbers=(((1,), (1,)), ((), ())),
        precision=lax.Precision.HIGHEST,
        preferred_element_type=f32,
    )
    return (
        result,
        back_tokens,
        packed[:n],
        slope_both[:, :QR],
        packed[2 * n : 2 * n + m],
        slope_both[:, QR:],
        packed[2 * n + m : 2 * n + m + k],
        exact(slope_query_up, query_one.astype(f32)),
        exact(slope_latent_up, latent_one.astype(f32)),
        slope_output.T.astype(f32),
        packed[n : 2 * n],
        slope_gate.T.astype(f32),
        slope_up.T.astype(f32),
        slope_down.astype(f32),
    )


def solution(mesh):
    placed = (
        P("row", "col"), P(), P("row"), P("row", None), P("row"), P("row", None), P("row"), P("row", "col"),
        P("row", "col"), P("col", "row"), P("row"), P("row", "col"), P("row", "col"), P("col", "row"),
        P("row", "col"),
    )
    outs = (
        P("row", "col"), P("row", "col"), P("row"), P("row", None), P("row"), P("row", None), P("row"),
        P("row", "col"), P("row", "col"), P("col", "row"), P("row"), P("row", "col"), P("row", "col"),
        P("col", "row"),
    )
    return jax.shard_map(shards, mesh=mesh, in_specs=placed, out_specs=outs, check_vma=False)
```

```python
import functools
import math

import jax
import jax.numpy as jnp
from jax import lax
from jax.experimental import pallas as pl
from jax.experimental.pallas import tpu as pltpu
from jax.sharding import PartitionSpec as P

DN = 64
DR = 32
DV = 64
QR = 768
KR = 256
SEQ_LEN = 4096
DOC_MOST = 2000
EPS = 1e-05
RES = 1.4 / math.sqrt(62.0)
THETA = 10000.0
NEG = -1e30
LOG2E = math.log2(math.e)
SCALE = (DN + DR) ** (-0.5)
VMEM_LIMIT = 56 << 20
MESH = pl.DeviceIdType.MESH
PAIR = 2
bf = jnp.bfloat16
f32 = jnp.float32


def ring_place(row, rows):
    return row // 2 + (row % 2) * (rows - 1 - 2 * (row // 2))


def ring_row(place, rows):
    side = place // (rows // 2)
    return 2 * (place + side * (rows - 1 - 2 * place)) + side


def flip(value, bit):
    return value + bit * (1 - 2 * ((value // bit) % 2))


def ring_barrier(others):
    barrier = pltpu.get_barrier_semaphore()
    for other in others:
        pl.semaphore_signal(barrier, inc=1, device_id=other, device_id_type=MESH)
    pl.semaphore_wait(barrier, len(others))


def col_peers(column, cols):
    return [flip(flip(column, 1) if k & 1 else column, 2) if k & 2 else flip(column, 1) for k in range(1, cols)]


def ring_gather_kernel(rows, n, *refs):
    blocks, (tokens_ref, back_ref, away_ref), refs = refs[:n], refs[n : n + 3], refs[n + 3 :]
    wholes, (features_ref, own_back_ref, came_ref), refs = refs[:n], refs[n : n + 3], refs[n + 3 :]
    own_sem, send_sem, recv_sem, col_send, col_recv = refs
    row, column = lax.axis_index("row"), lax.axis_index("col")
    place = ring_place(row, rows)
    ends = (ring_row((place + 1) % rows, rows), ring_row((place + rows - 1) % rows, rows))
    cols = features_ref.shape[1] // tokens_ref.shape[1]
    quarter = back_ref.shape[0] // cols
    peers = col_peers(column, cols)
    partner = (flip(row, PAIR), column)
    ring_barrier([(ends[0], column), (ends[1], column), partner] + [(row, peer) for peer in peers])
    lanes = pl.ds(pl.multiple_of(column * tokens_ref.shape[1], 128), tokens_ref.shape[1])

    def to_col(k, target):
        part = back_ref.at[pl.ds(pl.multiple_of(target * quarter, 128), quarter)]
        return [(tokens_ref, features_ref.at[:, lanes]), (part, own_back_ref.at[:, lanes])]

    crossing = []
    for k, peer in enumerate(peers):
        for which, (source, there) in enumerate(to_col(k, peer)):
            crossing.append(
                pltpu.make_async_remote_copy(
                    src_ref=source,
                    dst_ref=there,
                    send_sem=col_send.at[which, k],
                    recv_sem=col_recv.at[which, k],
                    device_id=(row, peer),
                    device_id_type=MESH,
                )
            )
    crossing.append(
        pltpu.make_async_remote_copy(
            src_ref=away_ref,
            dst_ref=came_ref,
            send_sem=col_send.at[2, 0],
            recv_sem=col_recv.at[2, 0],
            device_id=partner,
            device_id_type=MESH,
        )
    )
    staying = [
        pltpu.make_async_copy(source, there, own_sem.at[n + which])
        for which, (source, there) in enumerate(to_col(-1, column))
    ]

    def own(k):
        return pltpu.make_async_copy(blocks[k], wholes[k].at[row], own_sem.at[k])

    def hop(step, side, k):
        origin = ring_row((place + (step if side else rows - step)) % rows, rows)
        return pltpu.make_async_remote_copy(
            src_ref=wholes[k].at[origin, side],
            dst_ref=wholes[k].at[origin, side],
            send_sem=send_sem.at[step, side, k],
            recv_sem=recv_sem.at[step, side, k],
            device_id=(ends[side], column),
            device_id_type=MESH,
        )

    for k in range(n):
        own(k).start()
    for k in range(n):
        own(k).wait()
        for side in (0, 1):
            hop(0, side, k).start()
    for copy in crossing + staying:
        copy.start()

    def advance(step, carry):
        for k in range(n):
            for side in (0, 1):
                hop(step - 1, side, k).wait_recv()
                hop(step, side, k).start()
        return carry

    lax.fori_loop(1, rows - 1, advance, 0)
    for k in range(n):
        for side in (0, 1):
            hop(rows - 2, side, k).wait_recv()

    def drain(step, carry):
        for k in range(n):
            for side in (0, 1):
                hop(step, side, k).wait_send()
        return carry

    lax.fori_loop(0, rows - 1, drain, 0)
    for copy in crossing + staying:
        copy.wait()


def ring_gather(blocks, tokens, back, away):
    rows, cols, n = lax.axis_size("row"), lax.axis_size("col"), len(blocks)
    halves = [block.reshape(2, block.shape[0] // 2, block.shape[1]) for block in blocks]
    anywhere = pl.BlockSpec(memory_space=pl.ANY)
    *wholes, features, own_back, came = pl.pallas_call(
        functools.partial(ring_gather_kernel, rows, n),
        out_shape=[jax.ShapeDtypeStruct((rows,) + half.shape, half.dtype) for half in halves]
        + [
            jax.ShapeDtypeStruct((tokens.shape[0], cols * tokens.shape[1]), tokens.dtype),
            jax.ShapeDtypeStruct((back.shape[0] // cols, cols * back.shape[1]), back.dtype),
            jax.ShapeDtypeStruct(away.shape, away.dtype),
        ],
        in_specs=[anywhere] * (n + 3),
        out_specs=[anywhere] * (n + 3),
        scratch_shapes=[
            pltpu.SemaphoreType.DMA((n + 2,)),
            pltpu.SemaphoreType.DMA((rows - 1, 2, n)),
            pltpu.SemaphoreType.DMA((rows - 1, 2, n)),
            pltpu.SemaphoreType.DMA((3, cols - 1)),
            pltpu.SemaphoreType.DMA((3, cols - 1)),
        ],
        compiler_params=pltpu.CompilerParams(collective_id=0, has_side_effects=True),
        name="ring_gather",
    )(*halves, tokens, back, away)
    wholes = [whole.reshape(rows * block.shape[0], block.shape[1]) for whole, block in zip(wholes, blocks)]
    return wholes, features, own_back, came


def ring_scatter_kernel(rows, n, extra, *refs):
    terms, away_ref, leaving, refs = refs[:n], refs[n], refs[n + 1 : n + 1 + extra], refs[n + 1 + extra :]
    sums, came_ref, arriving, refs = refs[:n], refs[n], refs[n + 1 : n + 1 + extra], refs[n + 1 + extra :]
    slots, refs = refs[:n], refs[n:]
    send_sem, recv_sem, swap_send, swap_recv, own_sem, col_send, col_recv = refs
    row, column = lax.axis_index("row"), lax.axis_index("col")
    place = ring_place(row, rows)
    ends = (ring_row((place + 1) % rows, rows), ring_row((place + rows - 1) % rows, rows))
    partner = (flip(row, PAIR), column)
    cols = lax.axis_size("col")
    peers = col_peers(column, cols)
    ring_barrier([(ends[0], column), (ends[1], column), partner] + [(row, peer) for peer in peers])
    crossing = []
    for e in range(extra):
        quarter, width = leaving[e].shape[0], leaving[e].shape[1] // cols
        place_there = arriving[e].at[pl.ds(pl.multiple_of(column * quarter, 128), quarter)]

        def features(target):
            return leaving[e].at[:, pl.ds(pl.multiple_of(target * width, 128), width)]

        crossing.append(pltpu.make_async_copy(features(column), place_there, own_sem.at[e]))
        for k, peer in enumerate(peers):
            crossing.append(
                pltpu.make_async_remote_copy(
                    src_ref=features(peer),
                    dst_ref=place_there,
                    send_sem=col_send.at[e, k],
                    recv_sem=col_recv.at[e, k],
                    device_id=(row, peer),
                    device_id_type=MESH,
                )
            )
    swap = pltpu.make_async_remote_copy(
        src_ref=away_ref,
        dst_ref=came_ref,
        send_sem=swap_send,
        recv_sem=swap_recv,
        device_id=partner,
        device_id_type=MESH,
    )

    def target(step, side):
        return ring_row((place + (1 + step if side else 2 * rows - 1 - step)) % rows, rows)

    def hop(step, side, k, source):
        return pltpu.make_async_remote_copy(
            src_ref=source,
            dst_ref=slots[k].at[step, side],
            send_sem=send_sem.at[step, side, k],
            recv_sem=recv_sem.at[step, side, k],
            device_id=(ends[side], column),
            device_id_type=MESH,
        )

    def first(side, k):
        return hop(0, side, k, terms[k].at[target(0, side), side])

    def later(step, side, k):
        return hop(step, side, k, slots[k].at[step - 1, side])

    for k in range(n):
        for side in (0, 1):
            first(side, k).start()
    swap.start()
    for copy in crossing:
        copy.start()

    def arrive(step, side, k):
        return hop(step, side, k, slots[k].at[step, side])

    def advance(step, carry):
        for k in range(n):
            for side in (0, 1):
                arrive(step - 1, side, k).wait_recv()
                total = slots[k][step - 1, side].astype(f32) + terms[k][target(step, side), side].astype(f32)
                slots[k][step - 1, side] = total.astype(slots[k].dtype)
                later(step, side, k).start()
        return carry

    lax.fori_loop(1, rows - 1, advance, 0)
    for k in range(n):
        for side in (0, 1):
            arrive(rows - 2, side, k).wait_recv()
            sums[k][side] = slots[k][rows - 2, side].astype(f32) + terms[k][row, side].astype(f32)

    def drain(step, carry):
        for k in range(n):
            for side in (0, 1):
                arrive(step, side, k).wait_send()
        return carry

    lax.fori_loop(0, rows - 1, drain, 0)
    swap.wait()
    for copy in crossing:
        copy.wait()


def ring_scatter(terms, away, leaving):
    rows, n = lax.axis_size("row"), len(terms)
    split = [term.reshape(rows, 2, term.shape[0] // rows // 2, term.shape[1]) for term in terms]
    anywhere = pl.BlockSpec(memory_space=pl.ANY)
    cols, extra = lax.axis_size("col"), len(leaving)
    *sums, came, first, second = pl.pallas_call(
        functools.partial(ring_scatter_kernel, rows, n, extra),
        out_shape=[jax.ShapeDtypeStruct(term.shape[1:], f32) for term in split]
        + [jax.ShapeDtypeStruct(away.shape, away.dtype)]
        + [jax.ShapeDtypeStruct((v.shape[0] * cols, v.shape[1] // cols), v.dtype) for v in leaving],
        in_specs=[pl.BlockSpec(memory_space=pltpu.VMEM)] * n + [anywhere] * (1 + extra),
        out_specs=[pl.BlockSpec(memory_space=pltpu.VMEM)] * n + [anywhere] * (1 + extra),
        scratch_shapes=[pltpu.VMEM((rows - 1,) + term.shape[1:], term.dtype) for term in split]
        + [pltpu.SemaphoreType.DMA((rows - 1, 2, n)), pltpu.SemaphoreType.DMA((rows - 1, 2, n))]
        + [pltpu.SemaphoreType.DMA, pltpu.SemaphoreType.DMA, pltpu.SemaphoreType.DMA((extra,))]
        + [pltpu.SemaphoreType.DMA((extra, cols - 1)), pltpu.SemaphoreType.DMA((extra, cols - 1))],
        compiler_params=pltpu.CompilerParams(
            collective_id=1, has_side_effects=True, vmem_limit_bytes=VMEM_LIMIT
        ),
        name="ring_scatter",
    )(*split, away, *leaving)
    return [total.reshape(total.shape[0] * total.shape[1], total.shape[2]) for total in sums], came, (first, second)


def from_behind(value, steps):
    count = lax.axis_size("row")
    initial, last = (max(0, -steps), min(count, count - steps))
    return lax.ppermute(value, "row", [(source, source + steps) for source in range(initial, last)])


def swap_col(value, bit):
    return lax.ppermute(value, "col", [(c, c ^ bit) for c in range(lax.axis_size("col"))])


def by_owner(pieces, own=None):
    own = lax.axis_index("col") if own is None else own
    bit = 1
    pieces = list(pieces)
    while bit < len(pieces):
        odd = (own // bit) % 2 == 1
        pieces = [jnp.where(odd, pieces[k ^ bit], pieces[k]) for k in range(len(pieces))]
        bit *= 2
    return pieces


def pick(pieces):
    return by_owner(pieces)[0]


def col_gather(own):
    across = swap_col(own, 2)
    beside = swap_col(own, 1)
    return by_owner([own, beside, across, swap_col(across, 1)])


def col_scatter(pieces):
    mine = by_owner(pieces)
    low = [piece.astype(bf) for piece in mine]
    across = mine[2].astype(f32) + swap_col(low[3], 1).astype(f32)
    beside = mine[0].astype(f32) + swap_col(low[1], 1).astype(f32)
    return beside + swap_col(across.astype(bf), 2).astype(f32)


def quarters(value, axis):
    return jnp.split(value, lax.axis_size("col"), axis=axis)


def group_row(group, side):
    return (group // 2) * 4 + side * PAIR + group % 2


def own_group():
    row = lax.axis_index("row")
    return ((row // 4) * 2 + row % 2, (row // PAIR) % 2)


def swap_row(value, mask):
    return lax.ppermute(value, "row", [(r, r ^ mask) for r in range(lax.axis_size("row"))])


def group_masks():
    bits = (lax.axis_size("row") // 2).bit_length() - 1
    return [(1 << b, group_row(1 << b, 0)) for b in reversed(range(bits))]


def after(value, other):
    return lax.optimization_barrier((value, other))[0]


def features_by_group(value):
    rows = lax.axis_size("row")
    chunks = jnp.split(value, rows, axis=1)
    groups = [
        jnp.concatenate([chunks[group_row(g, side)] for side in (0, 1)], axis=1) for g in range(rows // 2)
    ]
    return jnp.concatenate(by_owner(groups, own_group()[0]), axis=1)


def features_in_order(value):
    rows = lax.axis_size("row")
    groups = by_owner(jnp.split(value, rows // 2, axis=1), own_group()[0])
    chunks = [None] * rows
    for g, group in enumerate(groups):
        for side, chunk in enumerate(jnp.split(group, 2, axis=1)):
            chunks[group_row(g, side)] = chunk
    return jnp.concatenate(chunks, axis=1)


def group_gather(own, mark):
    both = after(jnp.concatenate([own, swap_row(own, PAIR)], axis=0), mark)
    across = swap_col(both, 2)
    pieces = [both, swap_col(both, 1), across, swap_col(across, 1)]
    return jnp.concatenate([p for half in zip(*(jnp.split(piece, 2, axis=0) for piece in pieces)) for p in half], axis=0)


class GroupScatter:
    def __init__(self, value):
        x = jnp.split(value, 2 * lax.axis_size("col"), axis=0)
        self.kept = (x[0], x[2], x[4], x[6])
        self.came = swap_col(jnp.concatenate([x[1], x[3], x[5], x[7]], axis=0).astype(bf), 1)

    def add(self, mark):
        self.came = after(self.came, mark)
        return [a + b.astype(f32) for a, b in zip(self.kept, jnp.split(self.came, len(self.kept), axis=0))]

    def across(self, mark):
        y = self.add(mark)
        self.kept = (y[0], y[2])
        self.came = swap_col(jnp.concatenate([y[1], y[3]], axis=0).astype(bf), 2)

    def partner(self, mark):
        z = self.add(mark)
        self.kept = (z[0],)
        self.came = swap_row(z[1].astype(bf), PAIR)

    def result(self):
        return self.kept[0] + self.came.astype(f32)


def pair_halves(value, axis):
    low, high = jnp.split(value, 2, axis=axis)
    upper = own_group()[1] == 1
    return (jnp.where(upper, high, low), jnp.where(upper, low, high))


def in_pair_order(mine, came, axis):
    upper = own_group()[1] == 1
    return jnp.concatenate([jnp.where(upper, came, mine), jnp.where(upper, mine, came)], axis=axis)


class HiddenGather:
    def __init__(self, blocks):
        self.mine, self.away = pair_halves(blocks, 1)
        self.pieces = [{} for _ in range(blocks.shape[0])]

    def arrived(self, came):
        self.own = in_pair_order(self.mine, came, 2)
        for which, pieces in enumerate(self.pieces):
            pieces[0] = (self.own, which)

    def near_own(self, first, last, mark):
        beside = swap_row(after(self.own[first:last], mark), group_masks()[-1][1])
        for which in range(first, last):
            self.pieces[which][1] = (beside, which - first)
        return beside

    def far(self, which, mark):
        moved = {0: after(self.own[which : which + 1], mark)}
        for bit, mask in group_masks()[:-1]:
            for k in list(moved):
                moved[k ^ bit] = swap_row(moved[k], mask)
        self.pieces[which].update((k, (piece, 0)) for k, piece in moved.items() if k)
        return [piece for k, piece in moved.items() if k]

    def near(self, which, mark):
        pieces = self.pieces[which]
        for k in [k for k in pieces if k > 1]:
            pieces[k ^ 1] = (swap_row(after(pieces[k][0], mark), group_masks()[-1][1]), 0)
        return [pieces[k] for k in range(len(pieces))]


class HiddenScatter:
    def __init__(self, left, right):
        groups = lax.axis_size("row") // 2
        chunks = jnp.split(right, groups, axis=1)
        self.kept = [k for k in range(groups) if not k & 1]
        self.away = over_rows(left, jnp.concatenate([chunks[k | 1] for k in self.kept], axis=1)).astype(bf)
        self.total = over_rows(left, jnp.concatenate([chunks[k] for k in self.kept], axis=1))

    def near(self, mark):
        self.came = swap_row(after(self.away, mark), group_masks()[-1][1])

    def add(self):
        pieces = jnp.split(self.total + self.came.astype(f32), len(self.kept), axis=1)
        return dict(zip(self.kept, pieces))

    def far(self, mark):
        for bit, mask in reversed(group_masks()[:-1]):
            self.came = after(self.came, mark)
            pieces = self.add()
            away = [k for k in self.kept if k & bit]
            self.kept = [k for k in self.kept if not k & bit]
            self.total = jnp.concatenate([pieces[k] for k in self.kept], axis=1)
            self.came = swap_row(jnp.concatenate([pieces[k] for k in away], axis=1).astype(bf), mask)

    def halves(self):
        return pair_halves(self.add()[0].astype(bf), 1)


COLS = (("col", 1), ("col", 2))
GROUP = COLS + (("row", PAIR),)


class Cube:
    def __init__(self, dims, parts):
        self.dims, self.parts = dims, parts
        self.row, self.column = lax.axis_index("row"), lax.axis_index("col")
        self.masks = range(1, 1 << len(dims))

    def device(self, mask):
        row, column = self.row, self.column
        for k, (axis, bit) in enumerate(self.dims):
            if mask >> k & 1:
                row, column = (flip(row, bit), column) if axis == "row" else (row, flip(column, bit))
        return (row, column)

    def partner(self):
        return (flip(self.row, PAIR), self.column)

    def greet(self, cargo):
        others = [self.device(1 << k) for k in range(len(self.dims))] + [self.partner()] * cargo
        barrier = pltpu.get_barrier_semaphore()
        for other in others:
            pl.semaphore_signal(barrier, inc=1, device_id=other, device_id_type=MESH)
        pl.semaphore_wait(barrier, len(others))

    def ship(self, cargo):
        return [
            pltpu.make_async_remote_copy(
                src_ref=cargo[0],
                dst_ref=cargo[1],
                send_sem=cargo[2],
                recv_sem=cargo[3],
                device_id=self.partner(),
                device_id_type=MESH,
            )
        ] if cargo else []

    def order(self, part):
        slow = list(range(1, len(self.dims)))
        return [0] + (slow[::-1] if part % 2 else slow)


def cut(ref, index, rows, width):
    if width is None:
        return ref.at[index, rows]
    return ref.at[rows, pl.ds(pl.multiple_of(index * width, 128), width)]


def unpack(cargo, refs, inputs, outputs):
    if not cargo:
        return (refs, ())
    own, swapped = refs[inputs], refs[inputs + 1 + outputs]
    rest = refs[:inputs] + refs[inputs + 1 : inputs + 1 + outputs] + refs[inputs + outputs + 2 : -2]
    return (rest, (own, swapped) + tuple(refs[-2:]))


def spread_kernel(dims, parts, lanes, relative, cargo, *refs):
    (own_ref, all_ref, own_sem, send_sem, recv_sem), cargo = unpack(cargo, refs, 1, 1)
    cube = Cube(dims, parts)
    cube.greet(len(cargo) > 0)
    ship = cube.ship(cargo)
    for copy in ship:
        copy.start()
    height, width = own_ref.shape
    size = height // parts
    width = width if lanes else None

    def index(mask):
        return mask if relative else cube.device(mask)[1]

    def rows(part):
        return pl.ds(part * size, size)

    own = pltpu.make_async_copy(own_ref, cut(all_ref, index(0), pl.ds(0, height), width), own_sem)
    own.start()

    def hop(part, mask, k):
        there = mask | 1 << k
        target = there if relative else index(mask)
        source = cut(all_ref, index(mask), rows(part), width) if mask else own_ref.at[rows(part)]
        return pltpu.make_async_remote_copy(
            src_ref=source,
            dst_ref=cut(all_ref, target, rows(part), width),
            send_sem=send_sem.at[part, there],
            recv_sem=recv_sem.at[part, there],
            device_id=cube.device(1 << k),
            device_id_type=MESH,
        )

    def arrival(part, mask):
        view = cut(all_ref, index(mask), rows(part), width)
        return pltpu.make_async_remote_copy(
            src_ref=view,
            dst_ref=view,
            send_sem=send_sem.at[part, mask],
            recv_sem=recv_sem.at[part, mask],
            device_id=cube.device(1),
            device_id_type=MESH,
        )

    sent = []
    for part in range(parts):
        for k in cube.order(part)[::-1]:
            sent.append(hop(part, 0, k))
            sent[-1].start()
    last = []
    for bits in range(1, len(dims)):
        for part in range(parts):
            order = cube.order(part)[::-1]
            for mask in cube.masks:
                if bin(mask).count("1") != bits:
                    continue
                further = order[max(order.index(k) for k in range(len(dims)) if mask >> k & 1) + 1 :]
                if not further:
                    last.append((part, mask))
                    continue
                arrival(part, mask).wait_recv()
                for k in further:
                    sent.append(hop(part, mask, k))
                    sent[-1].start()
    last += [(part, cube.masks[-1]) for part in range(parts)]
    for part, mask in last:
        arrival(part, mask).wait_recv()
    for copy in sent:
        copy.wait_send()
    own.wait()
    for copy in ship:
        copy.wait()


def cargo_parts(cargo):
    if cargo is None:
        return ([], [], [])
    anywhere = pl.BlockSpec(memory_space=pl.ANY)
    return ([anywhere], [jax.ShapeDtypeStruct(cargo.shape, cargo.dtype)], [pltpu.SemaphoreType.DMA] * 2)


def spread(own, dims, parts, number, lanes=False, relative=False, cargo=None):
    specs, shapes, semaphores = cargo_parts(cargo)
    count = 1 << len(dims)
    shape = (own.shape[0], count * own.shape[1]) if lanes else (count,) + own.shape
    whole, *swapped = pl.pallas_call(
        functools.partial(spread_kernel, dims, parts, lanes, relative, cargo is not None),
        out_shape=[jax.ShapeDtypeStruct(shape, own.dtype)] + shapes,
        in_specs=[pl.BlockSpec(memory_space=pl.ANY)] + specs,
        out_specs=[pl.BlockSpec(memory_space=pl.ANY)] + specs,
        scratch_shapes=[
            pltpu.SemaphoreType.DMA,
            pltpu.SemaphoreType.DMA((parts, count)),
            pltpu.SemaphoreType.DMA((parts, count)),
        ]
        + semaphores,
        compiler_params=pltpu.CompilerParams(collective_id=number, has_side_effects=True),
        name=f"spread{number}",
    )(*([own] if cargo is None else [own, cargo]))
    whole = whole if lanes else whole.reshape(count * own.shape[0], own.shape[1])
    return (whole, swapped[0]) if swapped else whole


def behind_kernel(reach, key_ref, all_ref, own_sem, send_sem, recv_sem):
    rows, cols = lax.axis_size("row"), lax.axis_size("col")
    row, column = lax.axis_index("row"), lax.axis_index("col")
    count = key_ref.shape[1]
    quarter = count // cols
    beside, across = (row, flip(column, 1)), (row, flip(column, 2))
    ring_barrier([((row + rows - k) % rows, column) for k in range(1, reach + 1)] + [beside, across])
    own = pltpu.make_async_copy(key_ref, all_ref.at[:, pl.ds(reach * count, count)], own_sem)
    own.start()

    def view(k, mask):
        owner = flip(flip(column, 1) if mask & 1 else column, 2) if mask & 2 else (flip(column, 1) if mask else column)
        return all_ref.at[:, pl.ds(pl.multiple_of((reach - k) * count + owner * quarter, 128), quarter)]

    def hop(k, mask, target, there, source=None):
        return pltpu.make_async_remote_copy(
            src_ref=view(k, mask) if source is None else source,
            dst_ref=view(k, mask),
            send_sem=send_sem.at[k - 1, there],
            recv_sem=recv_sem.at[k - 1, there],
            device_id=target,
            device_id_type=MESH,
        )

    mine = key_ref.at[:, pl.ds(pl.multiple_of(column * quarter, 128), quarter)]
    sent = []
    for k in range(1, reach + 1):
        sent.append(hop(k, 0, ((row + k) % rows, column), 0, mine))
        sent[-1].start()
    for k in range(1, reach + 1):
        hop(k, 0, beside, 0).wait_recv()
        sent += [hop(k, 0, across, 2), hop(k, 0, beside, 1)]
        sent[-2].start()
        sent[-1].start()
    for k in range(1, reach + 1):
        hop(k, 2, across, 2).wait_recv()
        sent.append(hop(k, 2, beside, 3))
        sent[-1].start()
    for k in range(1, reach + 1):
        hop(k, 1, beside, 1).wait_recv()
        hop(k, 3, beside, 3).wait_recv()
    for copy in sent:
        copy.wait_send()
    own.wait()


def gather_behind(key, reach):
    height, count = key.shape
    return pl.pallas_call(
        functools.partial(behind_kernel, reach),
        out_shape=jax.ShapeDtypeStruct((height, (reach + 1) * count), key.dtype),
        in_specs=[pl.BlockSpec(memory_space=pl.ANY)],
        out_specs=pl.BlockSpec(memory_space=pl.ANY),
        scratch_shapes=[
            pltpu.SemaphoreType.DMA,
            pltpu.SemaphoreType.DMA((reach, 4)),
            pltpu.SemaphoreType.DMA((reach, 4)),
        ],
        compiler_params=pltpu.CompilerParams(collective_id=2, has_side_effects=True),
        name="gather_behind",
    )(key)


def fold_kernel(dims, parts, lanes, relative, cargo, *refs):
    (terms_ref, sum_ref, arrive_ref, leave_ref, send_sem, recv_sem), cargo = unpack(cargo, refs, 1, 1)
    cube = Cube(dims, parts)
    cube.greet(len(cargo) > 0)
    ship = cube.ship(cargo)
    for copy in ship:
        copy.start()
    height, width = sum_ref.shape
    size = height // parts
    width = width if lanes else None

    def term(part, mask):
        return cut(terms_ref, mask if relative else cube.device(mask)[1], pl.ds(part * size, size), width)

    def hop(part, mask, k, source):
        return pltpu.make_async_remote_copy(
            src_ref=source,
            dst_ref=arrive_ref.at[mask, pl.ds(part * size, size)],
            send_sem=send_sem.at[part, mask],
            recv_sem=recv_sem.at[part, mask],
            device_id=cube.device(1 << k),
            device_id_type=MESH,
        )

    sent = []
    for stage in range(len(dims) + 1):
        for part in range(parts):
            rows = pl.ds(part * size, size)
            order = cube.order(part)
            done = sum(1 << k for k in order[:stage])
            if stage:
                for mask in range(1 << len(dims)):
                    if not mask & done:
                        there = mask | 1 << order[stage - 1]
                        hop(part, there, order[stage - 1], arrive_ref.at[there, rows]).wait_recv()
            going = [0] if stage == len(dims) else [m for m in cube.masks if not m & done and m >> order[stage] & 1]
            for mask in going:
                source = term(part, mask)
                if stage:
                    total = source[...].astype(f32)
                    for k in order[:stage]:
                        total = total + arrive_ref[mask | 1 << k, rows].astype(f32)
                    if mask == 0:
                        sum_ref[rows] = total
                        continue
                    leave_ref[mask, rows] = total.astype(bf)
                    source = leave_ref.at[mask, rows]
                sent.append(hop(part, mask, order[stage], source))
                sent[-1].start()
    for copy in sent:
        copy.wait_send()
    for copy in ship:
        copy.wait()


def fold(terms, dims, parts, number, lanes=False, relative=False, cargo=None):
    count = 1 << len(dims)
    terms = terms.astype(bf)
    if lanes:
        shape = (terms.shape[0], terms.shape[1] // count)
    else:
        shape = (terms.shape[0] // count, terms.shape[1])
        terms = terms.reshape((count,) + shape)
    specs, shapes, semaphores = cargo_parts(cargo)
    total, *swapped = pl.pallas_call(
        functools.partial(fold_kernel, dims, parts, lanes, relative, cargo is not None),
        out_shape=[jax.ShapeDtypeStruct(shape, f32)] + shapes,
        in_specs=[pl.BlockSpec(memory_space=pltpu.VMEM)] + specs,
        out_specs=[pl.BlockSpec(memory_space=pltpu.VMEM)] + specs,
        scratch_shapes=[
            pltpu.VMEM((count,) + shape, bf),
            pltpu.VMEM((count,) + shape, bf),
            pltpu.SemaphoreType.DMA((parts, count)),
            pltpu.SemaphoreType.DMA((parts, count)),
        ]
        + semaphores,
        compiler_params=pltpu.CompilerParams(
            collective_id=number, has_side_effects=True, vmem_limit_bytes=VMEM_LIMIT
        ),
        name=f"fold{number}",
    )(*([terms] if cargo is None else [terms, cargo]))
    return (total, swapped[0]) if swapped else total


def dot(left, right, dims):
    return lax.dot_general(left, right, (dims, ((), ())), preferred_element_type=f32)


def multiply(left, right):
    return dot(left, right, ((1,), (0,)))


def against(left, right):
    return dot(left, right, ((1,), (1,)))


def over_rows(left, right):
    return dot(left, right, ((0,), (0,)))


def inverse_of(value, axis):
    return lax.rsqrt(jnp.mean(value * value, axis=axis, keepdims=True) + EPS)


def norm_back(value, inverse, gain, upstream, axis):
    unit = value * inverse
    scaled = upstream * gain
    inward = inverse * (scaled - unit * jnp.mean(scaled * unit, axis=axis, keepdims=True))
    return (inward, jnp.sum(upstream * unit, axis=1 - axis))


def angles(start, count):
    place = ((start + jnp.arange(count, dtype=jnp.int32)) % SEQ_LEN).astype(f32)
    half = DR // 2
    freq = jnp.exp(jnp.arange(half, dtype=f32) * (-math.log(THETA) / half))
    turn = freq[:, None] * place[None, :]
    return (jnp.cos(turn), jnp.sin(turn))


def rotate(front, behind, cosine, sine):
    return (front * cosine - behind * sine, behind * cosine + front * sine)


def query_columns(heads):
    tiles = -(-heads // 4)
    column = lax.iota(jnp.int32, heads * DN + tiles * 128)
    plain = (column // DN) * (DN + DR) + column % DN
    rest = column - heads * DN
    head = (rest // 128) * 4 + (rest % 64) // 16
    turned = head * (DN + DR) + DN + ((rest % 128) // 64) * 16 + rest % 16
    turned = jnp.where(head < heads, turned, -1)
    return jnp.where(column < heads * DN, plain, turned)


def latent_columns(heads):
    column = lax.iota(jnp.int32, heads * (DN + DV))
    rest = column % (heads * DN)
    return (rest // DN) * (DN + DV) + rest % DN + (column // (heads * DN)) * DN


def chosen(origin, width):
    return lax.broadcasted_iota(jnp.int32, (width, origin.shape[0]), 0) == origin[None, :]


BLOCK = 512


def head_rows(step, side, shape, axis):
    place = lax.broadcasted_iota(jnp.int32, shape, axis)
    plain = (place // DN == side).astype(f32).astype(bf)
    turned = ((place % 64) // 16 == 2 * (step % 2) + side).astype(f32).astype(bf)
    return (plain, turned)


def attend_kernel(
    blocks, first_ref, qn_ref, qr_ref, k_ref, kr_ref, vt_ref, bias_ref, o_ref, wide_ref, lse_ref, s_ref
):
    step = pl.program_id(0)
    first = first_ref[0]
    count = qn_ref.shape[1]
    sides = (0, 1)
    rights = []
    for side in sides:
        plain, turned = head_rows(step, side, qn_ref.shape, 0)
        rights.append(jnp.concatenate([qn_ref[...] * plain, qr_ref[...] * turned], axis=0))

    def score(j, tops):
        rows = pl.ds(pl.multiple_of(j * BLOCK, BLOCK), BLOCK)
        left = jnp.concatenate([k_ref[rows, :], kr_ref[rows, :]], axis=1)
        new = []
        for side in sides:
            s = multiply(left, rights[side]) * (SCALE * LOG2E) + bias_ref[rows, :]
            s_ref[side, rows, :] = s
            new.append(jnp.maximum(tops[side], jnp.max(s, axis=0, keepdims=True)))
        return tuple(new)

    tops = lax.fori_loop(first, blocks, score, (jnp.full((1, count), NEG, f32),) * 2)

    def gather(j, carry):
        rows = pl.ds(pl.multiple_of(j * BLOCK, BLOCK), BLOCK)
        new = []
        for side in sides:
            total, out = carry[side]
            chance = jnp.exp2(s_ref[side, rows, :] - tops[side])
            total = total + jnp.sum(chance, axis=0, keepdims=True)
            out = out + multiply(vt_ref[side * DV : (side + 1) * DV, rows], chance.astype(bf))
            new.append((total, out))
        return tuple(new)

    start = (jnp.zeros((1, count), f32), jnp.zeros((DV, count), f32))
    sums = lax.fori_loop(first, blocks, gather, (start, start))
    for side in sides:
        total, out = sums[side]
        out = out / total
        o_ref[side * DV : (side + 1) * DV, :] = out.astype(bf)
        wide_ref[side * DV : (side + 1) * DV, :] = out
        lse_ref[0, side : side + 1, :] = tops[side] + jnp.log2(total)


def attend(first, query, keys, turned_keys, values_t, bias, heads):
    count, kl = query.shape[1], keys.shape[0]
    pairs, base = heads // 2, heads * DN // 128
    grid = pltpu.PrefetchScalarGridSpec(
        num_scalar_prefetch=1,
        grid=(pairs,),
        in_specs=[
            pl.BlockSpec((128, count), lambda p, s: (p, 0)),
            pl.BlockSpec((128, count), lambda p, s: (base + p // 2, 0)),
            pl.BlockSpec((kl, 128), lambda p, s: (0, p)),
            pl.BlockSpec((kl, 128), lambda p, s: (0, 0)),
            pl.BlockSpec((128, kl), lambda p, s: (p, 0)),
            pl.BlockSpec((kl, count), lambda p, s: (0, 0)),
        ],
        out_specs=[
            pl.BlockSpec((128, count), lambda p, s: (p, 0)),
            pl.BlockSpec((128, count), lambda p, s: (p, 0)),
            pl.BlockSpec((1, 2, count), lambda p, s: (p, 0, 0)),
        ],
        scratch_shapes=[pltpu.VMEM((2, kl, count), f32)],
    )
    return pl.pallas_call(
        functools.partial(attend_kernel, kl // BLOCK),
        grid_spec=grid,
        out_shape=[
            jax.ShapeDtypeStruct((heads * DV, count), bf),
            jax.ShapeDtypeStruct((heads * DV, count), f32),
            jax.ShapeDtypeStruct((pairs, 2, count), f32),
        ],
        compiler_params=pltpu.CompilerParams(vmem_limit_bytes=VMEM_LIMIT),
        name="attend",
    )(first, query, query, keys, turned_keys, values_t, bias)


def attend_back_kernel(
    blocks, first_ref, qn_ref, qr_ref, qnn_ref, qrn_ref, k_ref, kr_ref, kt_ref, krt_ref, v_ref, dot_ref, do_ref, o_ref,
    bias_ref, lse_ref, dqn_ref, dqr_ref, dk_ref, dv_ref, dkr_ref,
):
    step = pl.program_id(0)
    first = first_ref[0]
    count = qn_ref.shape[1]
    sides = (0, 1)

    @pl.when(step == 0)
    def _():
        dkr_ref[...] = jnp.zeros_like(dkr_ref)

    @pl.when(step % 2 == 0)
    def _():
        dqr_ref[...] = jnp.zeros_like(dqr_ref)

    dk_ref[...] = jnp.zeros_like(dk_ref)
    dv_ref[...] = jnp.zeros_like(dv_ref)
    rights, out_rights, query_rights, value_rights, lses, deltas = [], [], [], [], [], []
    for side in sides:
        plain, turned = head_rows(step, side, qn_ref.shape, 0)
        rights.append(jnp.concatenate([qn_ref[...] * plain, qr_ref[...] * turned], axis=0))
        out_rights.append(dot_ref[...] * plain)
        plain_l, turned_l = head_rows(step, side, qnn_ref.shape, 1)
        query_rights.append(jnp.concatenate([qnn_ref[...] * plain_l, qrn_ref[...] * turned_l], axis=1))
        value_rights.append(do_ref[...] * plain_l)
        lses.append(lse_ref[0, side : side + 1, :])
        rows = slice(side * DV, (side + 1) * DV)
        deltas.append(jnp.sum(dot_ref[rows, :].astype(f32) * o_ref[rows, :], axis=0, keepdims=True))

    def block(j, dqs):
        rows = pl.ds(pl.multiple_of(j * BLOCK, BLOCK), BLOCK)
        left = jnp.concatenate([k_ref[rows, :], kr_ref[rows, :]], axis=1)
        left_t = jnp.concatenate([kt_ref[:, rows], krt_ref[:, rows]], axis=0)
        new, dk, dv = [], 0.0, 0.0
        for side in sides:
            s = multiply(left, rights[side]) * (SCALE * LOG2E) + bias_ref[rows, :]
            chance = jnp.exp2(s - lses[side])
            back = multiply(v_ref[rows, :], out_rights[side])
            ds = (chance * (back - deltas[side])).astype(bf)
            new.append(dqs[side] + multiply(left_t, ds))
            dk = dk + multiply(ds, query_rights[side])
            dv = dv + multiply(chance.astype(bf), value_rights[side])
        dk_ref[rows, :] = (dk[:, :128] * SCALE).astype(bf)
        dkr_ref[rows, :] += dk[:, 128:] * SCALE
        dv_ref[rows, :] = dv.astype(bf)
        return tuple(new)

    dqs = lax.fori_loop(first, blocks, block, (jnp.zeros((256, count), f32),) * 2)
    place = lax.broadcasted_iota(jnp.int32, (128, count), 0)
    for side in sides:
        dq = dqs[side] * SCALE
        dqn_ref[side * DN : (side + 1) * DN, :] = dq[side * DN : (side + 1) * DN]
        dqr_ref[...] += jnp.where((place % 64) // 16 == 2 * (step % 2) + side, dq[128:], 0.0)


def attend_back(
    first, query, query_n, keys, turned_keys, keys_t, turned_keys_t, values, do_t, do, out, bias, lse, heads
):
    count, kl = query.shape[1], keys.shape[0]
    pairs, base, tiles = heads // 2, heads * DN // 128, -(-heads // 4)
    across = lambda p, s: (0, p)
    along = lambda p, s: (p, 0)
    fixed = lambda p, s: (0, 0)
    grid = pltpu.PrefetchScalarGridSpec(
        num_scalar_prefetch=1,
        grid=(pairs,),
        in_specs=[
            pl.BlockSpec((128, count), along),
            pl.BlockSpec((128, count), lambda p, s: (base + p // 2, 0)),
            pl.BlockSpec((count, 128), across),
            pl.BlockSpec((count, 128), lambda p, s: (0, base + p // 2)),
            pl.BlockSpec((kl, 128), across),
            pl.BlockSpec((kl, 128), fixed),
            pl.BlockSpec((128, kl), along),
            pl.BlockSpec((128, kl), fixed),
            pl.BlockSpec((kl, 128), across),
            pl.BlockSpec((128, count), along),
            pl.BlockSpec((count, 128), across),
            pl.BlockSpec((128, count), along),
            pl.BlockSpec((kl, count), fixed),
            pl.BlockSpec((1, 2, count), lambda p, s: (p, 0, 0)),
        ],
        out_specs=[
            pl.BlockSpec((128, count), along),
            pl.BlockSpec((128, count), lambda p, s: (p // 2, 0)),
            pl.BlockSpec((kl, 128), across),
            pl.BlockSpec((kl, 128), across),
            pl.BlockSpec((kl, 128), fixed),
        ],
    )
    return pl.pallas_call(
        functools.partial(attend_back_kernel, kl // BLOCK),
        grid_spec=grid,
        out_shape=[
            jax.ShapeDtypeStruct((heads * DN, count), f32),
            jax.ShapeDtypeStruct((tiles * 128, count), f32),
            jax.ShapeDtypeStruct((kl, heads * DN), bf),
            jax.ShapeDtypeStruct((kl, heads * DV), bf),
            jax.ShapeDtypeStruct((kl, 128), f32),
        ],
        compiler_params=pltpu.CompilerParams(vmem_limit_bytes=VMEM_LIMIT),
        name="attend_back",
    )(first, query, query, query_n, query_n, keys, turned_keys, keys_t, turned_keys_t, values, do_t, do, out, bias, lse)


TOKENS = 256


def dot_pieces(left, pieces):
    width = pieces[0].shape[2]
    total = None
    for k, piece in enumerate(pieces):
        term = against(left[:, k * width : (k + 1) * width], piece[0])
        total = term if total is None else total + term
    return total


def ffn_kernel(n, x_ref, *refs):
    gate = dot_pieces(x_ref, refs[:n])
    upward = dot_pieces(x_ref, refs[n : 2 * n])
    gate_ref, up_ref, hidden_ref = refs[2 * n :]
    gate_ref[...] = gate
    up_ref[...] = upward
    hidden_ref[...] = (gate / (1.0 + jnp.exp(-gate)) * upward).astype(bf)


def piece_specs(pieces):
    def spec(array, index):
        return pl.BlockSpec((1,) + array.shape[1:], lambda i: (index, 0, 0), pipeline_mode=pl.Buffered(1))

    return [spec(array, index) for array, index in pieces]


def ffn(x, gate, up):
    tokens, hidden = x.shape[0], gate[0][0].shape[1]
    tile = lambda width: pl.BlockSpec((TOKENS, width), lambda i: (i, 0))
    return pl.pallas_call(
        functools.partial(ffn_kernel, len(gate)),
        grid=(tokens // TOKENS,),
        out_shape=[
            jax.ShapeDtypeStruct((tokens, hidden), f32),
            jax.ShapeDtypeStruct((tokens, hidden), f32),
            jax.ShapeDtypeStruct((tokens, hidden), bf),
        ],
        in_specs=[tile(x.shape[1])] + piece_specs(gate + up),
        out_specs=[tile(hidden)] * 3,
        compiler_params=pltpu.CompilerParams(vmem_limit_bytes=VMEM_LIMIT),
        name="ffn",
    )(x, *[array for array, _ in gate + up])


def ffn_back_kernel(n, dm_ref, gate_ref, up_ref, hidden_ref, *refs):
    gates, ups, down = refs[:n], refs[n : 2 * n], refs[2 * n : 3 * n]
    dgate_ref, dup_ref, dx_ref, out_ref = refs[3 * n :]
    width = down[0].shape[2]
    back_hidden = dot_pieces(dm_ref, down)
    gate, upward = gate_ref[...], up_ref[...]
    sigma = 1.0 / (1.0 + jnp.exp(-gate))
    dgate_ref[...] = (back_hidden * upward * sigma * (1.0 + gate * (1.0 - sigma))).astype(bf)
    dup_ref[...] = (back_hidden * gate * sigma).astype(bf)
    for k in range(n):
        lanes = slice(k * width, (k + 1) * width)
        dx_ref[:, lanes] = (multiply(dgate_ref[...], gates[k][0]) + multiply(dup_ref[...], ups[k][0])).astype(bf)
        out_ref[:, lanes] = multiply(hidden_ref[...], down[k][0]).astype(bf)


def ffn_back(dm, gate, upward, hidden, pieces, n):
    tokens, units = gate.shape
    tile = lambda width: pl.BlockSpec((TOKENS, width), lambda i: (i, 0))
    return pl.pallas_call(
        functools.partial(ffn_back_kernel, n),
        grid=(tokens // TOKENS,),
        out_shape=[
            jax.ShapeDtypeStruct((tokens, units), bf),
            jax.ShapeDtypeStruct((tokens, units), bf),
            jax.ShapeDtypeStruct(dm.shape, bf),
            jax.ShapeDtypeStruct(dm.shape, bf),
        ],
        in_specs=[tile(dm.shape[1]), tile(units), tile(units), tile(units)] + piece_specs(pieces),
        out_specs=[tile(units), tile(units), tile(dm.shape[1]), tile(dm.shape[1])],
        compiler_params=pltpu.CompilerParams(vmem_limit_bytes=VMEM_LIMIT),
        name="ffn_back",
    )(dm, gate, upward, hidden, *[array for array, _ in pieces])


def shards(
    tokens, document_ids, gain_first, query_down, query_gain, latent_down, latent_gain, query_up, latent_up,
    output_weight, gain_second, gate_weight, up_weight, down_weight, cotangent,
):
    count, own_width = tokens.shape
    rows, cols = lax.axis_size("row"), lax.axis_size("col")
    row, column = lax.axis_index("row"), lax.axis_index("col")
    start = row * count
    heads = query_up.shape[1] // (DN + DR)
    reach = -(-(DOC_MOST - 1) // count)
    blocks = reach + 1
    wide = heads * DN
    quarter = count // cols
    cosine, sine = angles(start, count)

    both_down = jnp.concatenate([query_down, latent_down], axis=1).astype(bf)
    down_slice = pick(quarters(both_down, 1))
    slice_width = down_slice.shape[1]
    small = jnp.concatenate([query_gain, latent_gain]).astype(bf)
    small = jnp.pad(small, (0, gain_first.shape[0] - small.shape[0]))
    gains = jnp.stack([gain_first.astype(bf), gain_second.astype(bf), small], axis=1)
    query_one = chosen(query_columns(heads), heads * (DN + DR))
    latent_one = chosen(latent_columns(heads), heads * (DN + DV))
    query_up_low = multiply(query_up.astype(bf), query_one.astype(bf)).astype(bf)
    latent_up_low = multiply(latent_up.astype(bf), latent_one.astype(bf)).astype(bf)
    down_block = jnp.concatenate([down_slice, gains], axis=1)
    down_block = jnp.pad(down_block, ((0, 0), (0, -down_block.shape[1] % 128)))
    ffn_weights = HiddenGather(
        jnp.stack([gate_weight.astype(bf).T, up_weight.astype(bf).T, down_weight.astype(bf)])
    )
    (wide_down, wide_query_up, wide_latent_up), features, own_up, came = ring_gather(
        (down_block, query_up_low, latent_up_low), tokens, cotangent, ffn_weights.away
    )
    ffn_weights.arrived(came)
    early = (ffn_weights.near_own(0, 1, wide_down), ffn_weights.far(0, wide_down))
    wide_output = lax.all_gather(after(output_weight, wide_down).astype(bf).T, "row", axis=0, tiled=True)
    gain_one = wide_down[:, slice_width].astype(f32)
    gain_two = wide_down[:, slice_width + 1].astype(f32)
    small_gains = wide_down[:, slice_width + 2].reshape(rows, -1).astype(f32)
    own_q = query_gain.shape[0]
    query_scale = small_gains[:, :own_q].reshape(-1)[:, None]
    latent_scale = small_gains[:, own_q : own_q + latent_gain.shape[0]].reshape(-1)[:, None]
    wide_down = wide_down[:, :slice_width]

    residual = features.astype(f32)
    first_in = (residual * inverse_of(residual, 1) * gain_one).astype(bf)
    own_residual = pick(quarters(features, 0)).astype(f32)

    latents = jnp.concatenate(col_gather(dot(wide_down, first_in, ((0,), (1,)))), axis=0)
    query_latent, latent_part = latents[:QR], latents[QR : QR + KR]
    inverse_query, inverse_latent = inverse_of(query_latent, 0), inverse_of(latent_part, 0)
    query_in = (query_latent * inverse_query * query_scale).astype(bf)
    latent_in = (latent_part * inverse_latent * latent_scale).astype(bf)
    half = DR // 2
    key_front, key_back = rotate(latents[QR + KR : QR + KR + half], latents[QR + KR + half :], cosine, sine)
    key_part = jnp.concatenate([latent_in, key_front.astype(bf), key_back.astype(bf)], axis=0)
    key_parts = gather_behind(after(key_part, early), reach)
    beside = ffn_weights.near_own(1, 3, key_parts)
    far_up, far_down = ffn_weights.far(1, key_parts), ffn_weights.far(2, key_parts)
    back_down = group_gather(features_by_group((RES * own_up).astype(bf)), key_parts)
    latent_all = key_parts[:KR]
    turned_t = jnp.concatenate([key_parts[KR : KR + half]] * 4 + [key_parts[KR + half :]] * 4, axis=0)
    turned = turned_t.T

    key_place = start - reach * count + jnp.arange(blocks * count, dtype=jnp.int32)
    place = start + jnp.arange(count, dtype=jnp.int32)
    key_doc = lax.dynamic_slice_in_dim(jnp.pad(document_ids, (reach * count, 0)), start, blocks * count)
    doc = lax.dynamic_slice_in_dim(document_ids, start, count)
    allowed = (key_doc[:, None] == doc[None, :]) & (key_place[:, None] <= place[None, :])
    allowed = allowed & (key_place[:, None] >= (place // SEQ_LEN * SEQ_LEN)[None, :])
    bias = jnp.where(allowed, 0.0, NEG).astype(f32)
    doc_start = jnp.sum((document_ids < doc[0]).astype(jnp.int32))
    first = jnp.clip((doc_start - (start - reach * count)) // BLOCK, 0, reach).reshape(1)

    raw = over_rows(wide_query_up, query_in)
    tiles = raw[wide:].reshape(-1, 2, 64, count)
    cos_tile, sin_tile = jnp.tile(cosine, (4, 1)), jnp.tile(sine, (4, 1))
    query_turned = jnp.stack(rotate(tiles[:, 0], tiles[:, 1], cos_tile, sin_tile), axis=1).reshape(-1, count)
    query = jnp.concatenate([raw[:wide], query_turned], axis=0).astype(bf)
    up_keys, up_values = wide_latent_up[:, :wide], wide_latent_up[:, wide:]
    keys = over_rows(latent_all, up_keys).astype(bf)
    values_t = over_rows(up_values, latent_all).astype(bf)
    out_t, out_wide, lse = attend(first, query, keys, turned, values_t, bias, heads)

    gate_pieces = ffn_weights.near(0, out_t)
    out_t = after(out_t, beside)
    branch = after(dot(out_t, wide_output, ((0,), (1,))), back_down)
    middle = own_residual + RES * fold(branch, COLS, 4, 4)
    middle = after(middle, far_up)
    up_pieces = ffn_weights.near(1, middle)
    middle = after(middle, far_down)
    down_pieces = ffn_weights.near(2, middle)
    inverse_second = inverse_of(middle, 1)
    second_in = features_by_group((middle * inverse_second * gain_two).astype(bf))
    second_in = spread(second_in, GROUP, 4, 5, relative=True)

    gate, upward, hidden = ffn(second_in, gate_pieces, up_pieces)
    slope_down = HiddenScatter(hidden, back_down)
    slope_down.near(hidden)
    gate = after(gate, slope_down.away)
    back_gate, back_upward, back_second, out_part = ffn_back(
        back_down, gate, upward, hidden, gate_pieces + up_pieces + down_pieces, len(gate_pieces)
    )
    slope_gate = HiddenScatter(back_gate, second_in)
    slope_gate.near(back_gate)
    back_second = after(back_second, slope_gate.away)
    back_second = features_in_order(fold(back_second, GROUP, 4, 6, relative=True))
    slope_up = HiddenScatter(back_upward, second_in)
    own_result = GroupScatter(out_part)
    back_norm, gain_second_part = norm_back(middle, inverse_second, gain_two, back_second, 1)
    back_middle = own_up + back_norm
    back_branch = after((RES * back_middle).astype(bf), (slope_down.came, own_result.came, slope_up.away))
    slope_up.near(back_branch)
    slope_down.far(back_branch)
    back_branch = spread(back_branch, COLS, 4, 7)
    own_result.across(back_branch)

    out = out_t.T
    back_out = multiply(back_branch, wide_output).astype(bf)
    slope_gate.far(back_out)
    keys_t = over_rows(up_keys, latent_all).astype(bf)
    values = over_rows(latent_all, up_values).astype(bf)
    back_query_n, back_query_r, back_keys, back_values, back_turned = attend_back(
        first, query, query.T, keys, turned, keys_t, turned_t, values, back_out.T, back_out, out_wide, bias, lse, heads
    )
    back_query_n = after(back_query_n, (slope_down.came, own_result.came))
    own_result.partner(back_query_n)
    tiles = back_query_r.reshape(-1, 2, 64, count)
    back_turn = jnp.stack(rotate(tiles[:, 0], tiles[:, 1], cos_tile, -sin_tile), axis=1).reshape(-1, count)
    back_raw = jnp.concatenate([back_query_n, back_turn], axis=0).astype(bf)
    query_part = multiply(wide_query_up, back_raw)
    latent_back = against(up_keys, back_keys) + against(up_values, back_values)
    turned_back = jnp.sum(back_turned.T.reshape(2, 4, half, blocks * count), axis=1).reshape(DR, blocks * count)
    far = jnp.concatenate([latent_back, turned_back], axis=0)
    to_send = jnp.concatenate(
        [query_part] + [far[:, b * count : (b + 1) * count] for b in range(blocks)], axis=0
    )
    to_send = after(to_send, slope_up.came)
    slope_up.far(to_send)
    slope_down, away = slope_down.halves()
    summed, came = fold(to_send, COLS, 3, 8, lanes=True, cargo=away)
    slope_down = in_pair_order(slope_down, came, 0)
    slope_gate.came = after(slope_gate.came, summed)
    own_result = middle + RES * features_in_order(own_result.result())
    back_query_in = summed[:QR]
    wide_far = KR + DR
    parts = [summed[QR + b * wide_far : QR + (b + 1) * wide_far] for b in range(blocks)]
    back_key = parts[reach]
    for step in range(1, reach + 1):
        back_key = back_key + from_behind(parts[reach - step], -step)

    own_latents = pick(quarters(latents, 1))
    own_query, own_latent = own_latents[:QR], own_latents[QR : QR + KR]
    back_query_latent, query_gain_part = norm_back(
        own_query, inverse_of(own_query, 0), query_scale, back_query_in, 0
    )
    back_latent, latent_gain_part = norm_back(
        own_latent, inverse_of(own_latent, 0), latent_scale, back_key[:KR], 0
    )
    own_cosine, own_sine = pick(quarters(cosine, 1)), pick(quarters(sine, 1))
    back_front, back_behind = rotate(back_key[KR : KR + half], back_key[KR + half :], own_cosine, -own_sine)
    back_latents = jnp.concatenate([back_query_latent, back_latent, back_front, back_behind], axis=0).astype(bf)
    back_latents = spread(back_latents, COLS, 3, 9, lanes=True)
    back_slice = lax.dynamic_slice_in_dim(back_latents, column * slice_width, slice_width, 0)
    back_first = fold(dot(back_slice, wide_down, ((0,), (1,))), COLS, 4, 10)
    back_norm_first, gain_first_part = norm_back(own_residual, inverse_of(own_residual, 1), gain_one, back_first, 1)
    own_back = back_middle + back_norm_first

    packed = jnp.concatenate(
        [part.reshape(rows, -1) for part in (gain_first_part, gain_second_part, query_gain_part, latent_gain_part)],
        axis=1,
    )
    packed = jnp.pad(packed, ((0, 0), (0, -packed.shape[1] % 256))).reshape(-1, 128)
    back_slice_n = jnp.pad(back_slice.T, ((0, 0), (0, -slice_width % 128)))
    slope_up.came = after(slope_up.came, back_first)
    halves = [flow.halves() for flow in (slope_gate, slope_up)]
    away = jnp.stack([gone for _, gone in halves])
    (slope_output, slope_query_up, slope_latent_up, slope_down_slice, packed), came, (result, back_tokens) = ring_scatter((
        over_rows(back_branch, out).astype(bf),
        against(query_in, back_raw).astype(bf),
        multiply(latent_all, jnp.concatenate([back_keys, back_values], axis=1)).astype(bf),
        over_rows(first_in, back_slice_n).astype(bf),
        packed,
    ), away, (own_result, own_back))
    slope_gate, slope_up = (in_pair_order(mine, got, 0) for (mine, _), got in zip(halves, came))
    slope_both = spread(slope_down_slice.astype(bf), COLS, 2, 11, lanes=True)
    slope_both = jnp.concatenate([piece[:, :slice_width] for piece in quarters(slope_both, 1)], axis=1).astype(f32)
    packed = packed.reshape(-1)
    bit = 1
    while bit < cols:
        packed = packed + swap_col(packed, bit)
        bit *= 2
    n = gain_first.shape[0]
    m = query_gain.shape[0]
    k = latent_gain.shape[0]

    exact = functools.partial(
        lax.dot_general,
        dimension_numbers=(((1,), (1,)), ((), ())),
        precision=lax.Precision.HIGHEST,
        preferred_element_type=f32,
    )
    return (
        result,
        back_tokens,
        packed[:n],
        slope_both[:, :QR],
        packed[2 * n : 2 * n + m],
        slope_both[:, QR:],
        packed[2 * n + m : 2 * n + m + k],
        exact(slope_query_up, query_one.astype(f32)),
        exact(slope_latent_up, latent_one.astype(f32)),
        slope_output.T,
        packed[n : 2 * n],
        slope_gate.T.astype(f32),
        slope_up.T.astype(f32),
        slope_down.astype(f32),
    )


def solution(mesh):
    placed = (
        P("row", "col"), P(), P("row"), P("row", None), P("row"), P("row", None), P("row"), P("row", "col"),
        P("row", "col"), P("col", "row"), P("row"), P("row", "col"), P("row", "col"), P("col", "row"),
        P("row", "col"),
    )
    outs = (
        P("row", "col"), P("row", "col"), P("row"), P("row", None), P("row"), P("row", None), P("row"),
        P("row", "col"), P("row", "col"), P("col", "row"), P("row"), P("row", "col"), P("row", "col"),
        P("col", "row"),
    )
    return jax.shard_map(shards, mesh=mesh, in_specs=placed, out_specs=outs, check_vma=False)
```

```python
import functools
import math

import jax
import jax.numpy as jnp
from jax import lax
from jax.experimental import pallas as pl
from jax.experimental.pallas import tpu as pltpu
from jax.sharding import PartitionSpec as P

DN = 64
DR = 32
DV = 64
QR = 768
KR = 256
SEQ_LEN = 4096
DOC_MOST = 2000
EPS = 1e-05
RES = 1.4 / math.sqrt(62.0)
THETA = 10000.0
NEG = -1e30
LOG2E = math.log2(math.e)
SCALE = (DN + DR) ** (-0.5)
VMEM_LIMIT = 56 << 20
MESH = pl.DeviceIdType.MESH
PAIR = 2
bf = jnp.bfloat16
f32 = jnp.float32


def ring_place(row, rows):
    return row // 2 + (row % 2) * (rows - 1 - 2 * (row // 2))


def ring_row(place, rows):
    side = place // (rows // 2)
    return 2 * (place + side * (rows - 1 - 2 * place)) + side


def flip(value, bit):
    return value + bit * (1 - 2 * ((value // bit) % 2))


def ring_barrier(others):
    barrier = pltpu.get_barrier_semaphore()
    for other in others:
        pl.semaphore_signal(barrier, inc=1, device_id=other, device_id_type=MESH)
    pl.semaphore_wait(barrier, len(others))


def col_peers(column, cols):
    return [flip(flip(column, 1) if k & 1 else column, 2) if k & 2 else flip(column, 1) for k in range(1, cols)]


def ring_gather_kernel(rows, n, *refs):
    blocks, (tokens_ref, back_ref, away_ref), refs = refs[:n], refs[n : n + 3], refs[n + 3 :]
    wholes, (features_ref, own_back_ref, came_ref), refs = refs[:n], refs[n : n + 3], refs[n + 3 :]
    own_sem, send_sem, recv_sem, col_send, col_recv = refs
    row, column = lax.axis_index("row"), lax.axis_index("col")
    place = ring_place(row, rows)
    ends = (ring_row((place + 1) % rows, rows), ring_row((place + rows - 1) % rows, rows))
    cols = features_ref.shape[1] // tokens_ref.shape[1]
    quarter = back_ref.shape[0] // cols
    peers = col_peers(column, cols)
    partner = (flip(row, PAIR), column)
    ring_barrier([(ends[0], column), (ends[1], column), partner] + [(row, peer) for peer in peers])
    lanes = pl.ds(pl.multiple_of(column * tokens_ref.shape[1], 128), tokens_ref.shape[1])

    def to_col(k, target):
        part = back_ref.at[pl.ds(pl.multiple_of(target * quarter, 128), quarter)]
        return [(tokens_ref, features_ref.at[:, lanes]), (part, own_back_ref.at[:, lanes])]

    crossing = []
    for k, peer in enumerate(peers):
        for which, (source, there) in enumerate(to_col(k, peer)):
            crossing.append(
                pltpu.make_async_remote_copy(
                    src_ref=source,
                    dst_ref=there,
                    send_sem=col_send.at[which, k],
                    recv_sem=col_recv.at[which, k],
                    device_id=(row, peer),
                    device_id_type=MESH,
                )
            )
    crossing.append(
        pltpu.make_async_remote_copy(
            src_ref=away_ref,
            dst_ref=came_ref,
            send_sem=col_send.at[2, 0],
            recv_sem=col_recv.at[2, 0],
            device_id=partner,
            device_id_type=MESH,
        )
    )
    staying = [
        pltpu.make_async_copy(source, there, own_sem.at[n + which])
        for which, (source, there) in enumerate(to_col(-1, column))
    ]

    def own(k):
        return pltpu.make_async_copy(blocks[k], wholes[k].at[row], own_sem.at[k])

    def hop(step, side, k):
        origin = ring_row((place + (step if side else rows - step)) % rows, rows)
        return pltpu.make_async_remote_copy(
            src_ref=wholes[k].at[origin, side],
            dst_ref=wholes[k].at[origin, side],
            send_sem=send_sem.at[step, side, k],
            recv_sem=recv_sem.at[step, side, k],
            device_id=(ends[side], column),
            device_id_type=MESH,
        )

    for k in range(n):
        own(k).start()
    for k in range(n):
        own(k).wait()
        for side in (0, 1):
            hop(0, side, k).start()
    for copy in crossing + staying:
        copy.start()

    def advance(step, carry):
        for k in range(n):
            for side in (0, 1):
                hop(step - 1, side, k).wait_recv()
                hop(step, side, k).start()
        return carry

    lax.fori_loop(1, rows - 1, advance, 0)
    for k in range(n):
        for side in (0, 1):
            hop(rows - 2, side, k).wait_recv()

    def drain(step, carry):
        for k in range(n):
            for side in (0, 1):
                hop(step, side, k).wait_send()
        return carry

    lax.fori_loop(0, rows - 1, drain, 0)
    for copy in crossing + staying:
        copy.wait()


def ring_gather(blocks, tokens, back, away):
    rows, cols, n = lax.axis_size("row"), lax.axis_size("col"), len(blocks)
    halves = [block.reshape(2, block.shape[0] // 2, block.shape[1]) for block in blocks]
    anywhere = pl.BlockSpec(memory_space=pl.ANY)
    *wholes, features, own_back, came = pl.pallas_call(
        functools.partial(ring_gather_kernel, rows, n),
        out_shape=[jax.ShapeDtypeStruct((rows,) + half.shape, half.dtype) for half in halves]
        + [
            jax.ShapeDtypeStruct((tokens.shape[0], cols * tokens.shape[1]), tokens.dtype),
            jax.ShapeDtypeStruct((back.shape[0] // cols, cols * back.shape[1]), back.dtype),
            jax.ShapeDtypeStruct(away.shape, away.dtype),
        ],
        in_specs=[anywhere] * (n + 3),
        out_specs=[anywhere] * (n + 3),
        scratch_shapes=[
            pltpu.SemaphoreType.DMA((n + 2,)),
            pltpu.SemaphoreType.DMA((rows - 1, 2, n)),
            pltpu.SemaphoreType.DMA((rows - 1, 2, n)),
            pltpu.SemaphoreType.DMA((3, cols - 1)),
            pltpu.SemaphoreType.DMA((3, cols - 1)),
        ],
        compiler_params=pltpu.CompilerParams(collective_id=0, has_side_effects=True),
        name="ring_gather",
    )(*halves, tokens, back, away)
    wholes = [whole.reshape(rows * block.shape[0], block.shape[1]) for whole, block in zip(wholes, blocks)]
    return wholes, features, own_back, came


def ring_scatter_kernel(rows, n, extra, *refs):
    terms, away_ref, leaving, refs = refs[:n], refs[n], refs[n + 1 : n + 1 + extra], refs[n + 1 + extra :]
    sums, came_ref, arriving, refs = refs[:n], refs[n], refs[n + 1 : n + 1 + extra], refs[n + 1 + extra :]
    slots, refs = refs[:n], refs[n:]
    send_sem, recv_sem, swap_send, swap_recv, own_sem, col_send, col_recv = refs
    row, column = lax.axis_index("row"), lax.axis_index("col")
    place = ring_place(row, rows)
    ends = (ring_row((place + 1) % rows, rows), ring_row((place + rows - 1) % rows, rows))
    partner = (flip(row, PAIR), column)
    cols = lax.axis_size("col")
    peers = col_peers(column, cols)
    ring_barrier([(ends[0], column), (ends[1], column), partner] + [(row, peer) for peer in peers])
    crossing = []
    for e in range(extra):
        quarter, width = leaving[e].shape[0], leaving[e].shape[1] // cols
        place_there = arriving[e].at[pl.ds(pl.multiple_of(column * quarter, 128), quarter)]

        def features(target):
            return leaving[e].at[:, pl.ds(pl.multiple_of(target * width, 128), width)]

        crossing.append(pltpu.make_async_copy(features(column), place_there, own_sem.at[e]))
        for k, peer in enumerate(peers):
            crossing.append(
                pltpu.make_async_remote_copy(
                    src_ref=features(peer),
                    dst_ref=place_there,
                    send_sem=col_send.at[e, k],
                    recv_sem=col_recv.at[e, k],
                    device_id=(row, peer),
                    device_id_type=MESH,
                )
            )
    swap = pltpu.make_async_remote_copy(
        src_ref=away_ref,
        dst_ref=came_ref,
        send_sem=swap_send,
        recv_sem=swap_recv,
        device_id=partner,
        device_id_type=MESH,
    )

    def target(step, side):
        return ring_row((place + (1 + step if side else 2 * rows - 1 - step)) % rows, rows)

    def hop(step, side, k, source):
        return pltpu.make_async_remote_copy(
            src_ref=source,
            dst_ref=slots[k].at[step, side],
            send_sem=send_sem.at[step, side, k],
            recv_sem=recv_sem.at[step, side, k],
            device_id=(ends[side], column),
            device_id_type=MESH,
        )

    def first(side, k):
        return hop(0, side, k, terms[k].at[target(0, side), side])

    def later(step, side, k):
        return hop(step, side, k, slots[k].at[step - 1, side])

    for k in range(n):
        for side in (0, 1):
            first(side, k).start()
    swap.start()
    for copy in crossing:
        copy.start()

    def arrive(step, side, k):
        return hop(step, side, k, slots[k].at[step, side])

    def advance(step, carry):
        for k in range(n):
            for side in (0, 1):
                arrive(step - 1, side, k).wait_recv()
                total = slots[k][step - 1, side].astype(f32) + terms[k][target(step, side), side].astype(f32)
                slots[k][step - 1, side] = total.astype(slots[k].dtype)
                later(step, side, k).start()
        return carry

    lax.fori_loop(1, rows - 1, advance, 0)
    for k in range(n):
        for side in (0, 1):
            arrive(rows - 2, side, k).wait_recv()
            sums[k][side] = slots[k][rows - 2, side].astype(f32) + terms[k][row, side].astype(f32)

    def drain(step, carry):
        for k in range(n):
            for side in (0, 1):
                arrive(step, side, k).wait_send()
        return carry

    lax.fori_loop(0, rows - 1, drain, 0)
    swap.wait()
    for copy in crossing:
        copy.wait()


def ring_scatter(terms, away, leaving):
    rows, n = lax.axis_size("row"), len(terms)
    split = [term.reshape(rows, 2, term.shape[0] // rows // 2, term.shape[1]) for term in terms]
    anywhere = pl.BlockSpec(memory_space=pl.ANY)
    cols, extra = lax.axis_size("col"), len(leaving)
    *sums, came, first, second = pl.pallas_call(
        functools.partial(ring_scatter_kernel, rows, n, extra),
        out_shape=[jax.ShapeDtypeStruct(term.shape[1:], f32) for term in split]
        + [jax.ShapeDtypeStruct(away.shape, away.dtype)]
        + [jax.ShapeDtypeStruct((v.shape[0] * cols, v.shape[1] // cols), v.dtype) for v in leaving],
        in_specs=[pl.BlockSpec(memory_space=pltpu.VMEM)] * n + [anywhere] * (1 + extra),
        out_specs=[pl.BlockSpec(memory_space=pltpu.VMEM)] * n + [anywhere] * (1 + extra),
        scratch_shapes=[pltpu.VMEM((rows - 1,) + term.shape[1:], term.dtype) for term in split]
        + [pltpu.SemaphoreType.DMA((rows - 1, 2, n)), pltpu.SemaphoreType.DMA((rows - 1, 2, n))]
        + [pltpu.SemaphoreType.DMA, pltpu.SemaphoreType.DMA, pltpu.SemaphoreType.DMA((extra,))]
        + [pltpu.SemaphoreType.DMA((extra, cols - 1)), pltpu.SemaphoreType.DMA((extra, cols - 1))],
        compiler_params=pltpu.CompilerParams(
            collective_id=1, has_side_effects=True, vmem_limit_bytes=VMEM_LIMIT
        ),
        name="ring_scatter",
    )(*split, away, *leaving)
    return [total.reshape(total.shape[0] * total.shape[1], total.shape[2]) for total in sums], came, (first, second)


def from_behind(value, steps):
    count = lax.axis_size("row")
    initial, last = (max(0, -steps), min(count, count - steps))
    return lax.ppermute(value, "row", [(source, source + steps) for source in range(initial, last)])


def swap_col(value, bit):
    return lax.ppermute(value, "col", [(c, c ^ bit) for c in range(lax.axis_size("col"))])


def by_owner(pieces, own=None):
    own = lax.axis_index("col") if own is None else own
    bit = 1
    pieces = list(pieces)
    while bit < len(pieces):
        odd = (own // bit) % 2 == 1
        pieces = [jnp.where(odd, pieces[k ^ bit], pieces[k]) for k in range(len(pieces))]
        bit *= 2
    return pieces


def pick(pieces):
    return by_owner(pieces)[0]


def col_gather(own):
    across = swap_col(own, 2)
    beside = swap_col(own, 1)
    return by_owner([own, beside, across, swap_col(across, 1)])


def col_scatter(pieces):
    mine = by_owner(pieces)
    low = [piece.astype(bf) for piece in mine]
    across = mine[2].astype(f32) + swap_col(low[3], 1).astype(f32)
    beside = mine[0].astype(f32) + swap_col(low[1], 1).astype(f32)
    return beside + swap_col(across.astype(bf), 2).astype(f32)


def quarters(value, axis):
    return jnp.split(value, lax.axis_size("col"), axis=axis)


def group_row(group, side):
    return (group // 2) * 4 + side * PAIR + group % 2


def own_group():
    row = lax.axis_index("row")
    return ((row // 4) * 2 + row % 2, (row // PAIR) % 2)


def swap_row(value, mask):
    return lax.ppermute(value, "row", [(r, r ^ mask) for r in range(lax.axis_size("row"))])


def group_masks():
    bits = (lax.axis_size("row") // 2).bit_length() - 1
    return [(1 << b, group_row(1 << b, 0)) for b in reversed(range(bits))]


def after(value, other):
    return lax.optimization_barrier((value, other))[0]


def features_by_group(value):
    rows = lax.axis_size("row")
    chunks = jnp.split(value, rows, axis=1)
    groups = [
        jnp.concatenate([chunks[group_row(g, side)] for side in (0, 1)], axis=1) for g in range(rows // 2)
    ]
    return jnp.concatenate(by_owner(groups, own_group()[0]), axis=1)


def features_in_order(value):
    rows = lax.axis_size("row")
    groups = by_owner(jnp.split(value, rows // 2, axis=1), own_group()[0])
    chunks = [None] * rows
    for g, group in enumerate(groups):
        for side, chunk in enumerate(jnp.split(group, 2, axis=1)):
            chunks[group_row(g, side)] = chunk
    return jnp.concatenate(chunks, axis=1)


class GroupScatter:
    def __init__(self, value):
        x = jnp.split(value, 2 * lax.axis_size("col"), axis=0)
        self.kept = (x[0], x[2], x[4], x[6])
        self.came = swap_col(jnp.concatenate([x[1], x[3], x[5], x[7]], axis=0).astype(bf), 1)

    def add(self, mark):
        self.came = after(self.came, mark)
        return [a + b.astype(f32) for a, b in zip(self.kept, jnp.split(self.came, len(self.kept), axis=0))]

    def across(self, mark):
        y = self.add(mark)
        self.kept = (y[0], y[2])
        self.came = swap_col(jnp.concatenate([y[1], y[3]], axis=0).astype(bf), 2)

    def partner(self, mark):
        z = self.add(mark)
        self.kept = (z[0],)
        self.came = swap_row(z[1].astype(bf), PAIR)

    def result(self):
        return self.kept[0] + self.came.astype(f32)


def pair_halves(value, axis):
    low, high = jnp.split(value, 2, axis=axis)
    upper = own_group()[1] == 1
    return (jnp.where(upper, high, low), jnp.where(upper, low, high))


def in_pair_order(mine, came, axis):
    upper = own_group()[1] == 1
    return jnp.concatenate([jnp.where(upper, came, mine), jnp.where(upper, mine, came)], axis=axis)


class HiddenGather:
    def __init__(self, blocks):
        self.mine, self.away = pair_halves(blocks, 1)
        self.pieces = [{} for _ in range(blocks.shape[0])]

    def arrived(self, came, first, last):
        own = in_pair_order(self.mine[first:last], came, 2)
        for which in range(first, last):
            self.pieces[which][0] = (own, which - first)
        return own

    def near_own(self, own, first, last, mark):
        beside = swap_row(after(own, mark), group_masks()[-1][1])
        for which in range(first, last):
            self.pieces[which][1] = (beside, which - first)
        return beside

    def far(self, which, mark):
        own, index = self.pieces[which][0]
        moved = {0: after(own[index : index + 1], mark)}
        for bit, mask in group_masks()[:-1]:
            for k in list(moved):
                moved[k ^ bit] = swap_row(moved[k], mask)
        self.pieces[which].update((k, (piece, 0)) for k, piece in moved.items() if k)
        return [piece for k, piece in moved.items() if k]

    def near(self, which, mark):
        pieces = self.pieces[which]
        for k in [k for k in pieces if k > 1]:
            pieces[k ^ 1] = (swap_row(after(pieces[k][0], mark), group_masks()[-1][1]), 0)
        return [pieces[k] for k in range(len(pieces))]


class HiddenScatter:
    def __init__(self, left, right):
        groups = lax.axis_size("row") // 2
        chunks = jnp.split(right, groups, axis=1)
        self.kept = [k for k in range(groups) if not k & 1]
        self.away = over_rows(left, jnp.concatenate([chunks[k | 1] for k in self.kept], axis=1)).astype(bf)
        self.total = over_rows(left, jnp.concatenate([chunks[k] for k in self.kept], axis=1))

    def near(self, mark):
        self.came = swap_row(after(self.away, mark), group_masks()[-1][1])

    def add(self):
        pieces = jnp.split(self.total + self.came.astype(f32), len(self.kept), axis=1)
        return dict(zip(self.kept, pieces))

    def far(self, mark):
        for bit, mask in reversed(group_masks()[:-1]):
            self.came = after(self.came, mark)
            pieces = self.add()
            away = [k for k in self.kept if k & bit]
            self.kept = [k for k in self.kept if not k & bit]
            self.total = jnp.concatenate([pieces[k] for k in self.kept], axis=1)
            self.came = swap_row(jnp.concatenate([pieces[k] for k in away], axis=1).astype(bf), mask)

    def halves(self):
        return pair_halves(self.add()[0].astype(bf), 1)


COLS = (("col", 1), ("col", 2))
GROUP = COLS + (("row", PAIR),)


class Cube:
    def __init__(self, dims, parts):
        self.dims, self.parts = dims, parts
        self.row, self.column = lax.axis_index("row"), lax.axis_index("col")
        self.masks = range(1, 1 << len(dims))

    def device(self, mask):
        row, column = self.row, self.column
        for k, (axis, bit) in enumerate(self.dims):
            if mask >> k & 1:
                row, column = (flip(row, bit), column) if axis == "row" else (row, flip(column, bit))
        return (row, column)

    def partner(self):
        return (flip(self.row, PAIR), self.column)

    def greet(self, cargo):
        others = [self.device(1 << k) for k in range(len(self.dims))] + [self.partner()] * cargo
        barrier = pltpu.get_barrier_semaphore()
        for other in others:
            pl.semaphore_signal(barrier, inc=1, device_id=other, device_id_type=MESH)
        pl.semaphore_wait(barrier, len(others))

    def ship(self, cargo):
        return [
            pltpu.make_async_remote_copy(
                src_ref=cargo[0],
                dst_ref=cargo[1],
                send_sem=cargo[2],
                recv_sem=cargo[3],
                device_id=self.partner(),
                device_id_type=MESH,
            )
        ] if cargo else []

    def order(self, part):
        slow = list(range(1, len(self.dims)))
        return [0] + (slow[::-1] if part % 2 else slow)


def cut(ref, index, rows, width):
    if width is None:
        return ref.at[index, rows]
    return ref.at[rows, pl.ds(pl.multiple_of(index * width, 128), width)]


def unpack(cargo, refs, inputs, outputs):
    if not cargo:
        return (refs, ())
    own, swapped = refs[inputs], refs[inputs + 1 + outputs]
    rest = refs[:inputs] + refs[inputs + 1 : inputs + 1 + outputs] + refs[inputs + outputs + 2 : -2]
    return (rest, (own, swapped) + tuple(refs[-2:]))


def spread_kernel(dims, parts, lanes, relative, cargo, *refs):
    (own_ref, all_ref, own_sem, send_sem, recv_sem), cargo = unpack(cargo, refs, 1, 1)
    cube = Cube(dims, parts)
    cube.greet(len(cargo) > 0)
    ship = cube.ship(cargo)
    for copy in ship:
        copy.start()
    height, width = own_ref.shape
    size = height // parts
    width = width if lanes else None

    def index(mask):
        return mask if relative else cube.device(mask)[1]

    def rows(part):
        return pl.ds(part * size, size)

    own = pltpu.make_async_copy(own_ref, cut(all_ref, index(0), pl.ds(0, height), width), own_sem)
    own.start()

    def hop(part, mask, k):
        there = mask | 1 << k
        target = there if relative else index(mask)
        source = cut(all_ref, index(mask), rows(part), width) if mask else own_ref.at[rows(part)]
        return pltpu.make_async_remote_copy(
            src_ref=source,
            dst_ref=cut(all_ref, target, rows(part), width),
            send_sem=send_sem.at[part, there],
            recv_sem=recv_sem.at[part, there],
            device_id=cube.device(1 << k),
            device_id_type=MESH,
        )

    def arrival(part, mask):
        view = cut(all_ref, index(mask), rows(part), width)
        return pltpu.make_async_remote_copy(
            src_ref=view,
            dst_ref=view,
            send_sem=send_sem.at[part, mask],
            recv_sem=recv_sem.at[part, mask],
            device_id=cube.device(1),
            device_id_type=MESH,
        )

    sent = []
    for part in range(parts):
        for k in cube.order(part)[::-1]:
            sent.append(hop(part, 0, k))
            sent[-1].start()
    last = []
    for bits in range(1, len(dims)):
        for part in range(parts):
            order = cube.order(part)[::-1]
            for mask in cube.masks:
                if bin(mask).count("1") != bits:
                    continue
                further = order[max(order.index(k) for k in range(len(dims)) if mask >> k & 1) + 1 :]
                if not further:
                    last.append((part, mask))
                    continue
                arrival(part, mask).wait_recv()
                for k in further:
                    sent.append(hop(part, mask, k))
                    sent[-1].start()
    last += [(part, cube.masks[-1]) for part in range(parts)]
    for part, mask in last:
        arrival(part, mask).wait_recv()
    for copy in sent:
        copy.wait_send()
    own.wait()
    for copy in ship:
        copy.wait()


def cargo_parts(cargo):
    if cargo is None:
        return ([], [], [])
    anywhere = pl.BlockSpec(memory_space=pl.ANY)
    return ([anywhere], [jax.ShapeDtypeStruct(cargo.shape, cargo.dtype)], [pltpu.SemaphoreType.DMA] * 2)


def spread(own, dims, parts, number, lanes=False, relative=False, cargo=None):
    specs, shapes, semaphores = cargo_parts(cargo)
    count = 1 << len(dims)
    shape = (own.shape[0], count * own.shape[1]) if lanes else (count,) + own.shape
    whole, *swapped = pl.pallas_call(
        functools.partial(spread_kernel, dims, parts, lanes, relative, cargo is not None),
        out_shape=[jax.ShapeDtypeStruct(shape, own.dtype)] + shapes,
        in_specs=[pl.BlockSpec(memory_space=pl.ANY)] + specs,
        out_specs=[pl.BlockSpec(memory_space=pl.ANY)] + specs,
        scratch_shapes=[
            pltpu.SemaphoreType.DMA,
            pltpu.SemaphoreType.DMA((parts, count)),
            pltpu.SemaphoreType.DMA((parts, count)),
        ]
        + semaphores,
        compiler_params=pltpu.CompilerParams(collective_id=number, has_side_effects=True),
        name=f"spread{number}",
    )(*([own] if cargo is None else [own, cargo]))
    whole = whole if lanes else whole.reshape(count * own.shape[0], own.shape[1])
    return (whole, swapped[0]) if swapped else whole


def behind_kernel(reach, key_ref, all_ref, own_sem, send_sem, recv_sem):
    rows, cols = lax.axis_size("row"), lax.axis_size("col")
    row, column = lax.axis_index("row"), lax.axis_index("col")
    count = key_ref.shape[1]
    quarter = count // cols
    beside, across = (row, flip(column, 1)), (row, flip(column, 2))
    ring_barrier([((row + rows - k) % rows, column) for k in range(1, reach + 1)] + [beside, across])
    own = pltpu.make_async_copy(key_ref, all_ref.at[:, pl.ds(reach * count, count)], own_sem)
    own.start()

    def view(k, mask):
        owner = flip(flip(column, 1) if mask & 1 else column, 2) if mask & 2 else (flip(column, 1) if mask else column)
        return all_ref.at[:, pl.ds(pl.multiple_of((reach - k) * count + owner * quarter, 128), quarter)]

    def hop(k, mask, target, there, source=None):
        return pltpu.make_async_remote_copy(
            src_ref=view(k, mask) if source is None else source,
            dst_ref=view(k, mask),
            send_sem=send_sem.at[k - 1, there],
            recv_sem=recv_sem.at[k - 1, there],
            device_id=target,
            device_id_type=MESH,
        )

    mine = key_ref.at[:, pl.ds(pl.multiple_of(column * quarter, 128), quarter)]
    sent = []
    for k in range(1, reach + 1):
        sent.append(hop(k, 0, ((row + k) % rows, column), 0, mine))
        sent[-1].start()
    for k in range(1, reach + 1):
        hop(k, 0, beside, 0).wait_recv()
        sent += [hop(k, 0, across, 2), hop(k, 0, beside, 1)]
        sent[-2].start()
        sent[-1].start()
    for k in range(1, reach + 1):
        hop(k, 2, across, 2).wait_recv()
        sent.append(hop(k, 2, beside, 3))
        sent[-1].start()
    for k in range(1, reach + 1):
        hop(k, 1, beside, 1).wait_recv()
        hop(k, 3, beside, 3).wait_recv()
    for copy in sent:
        copy.wait_send()
    own.wait()


def gather_behind(key, reach):
    height, count = key.shape
    return pl.pallas_call(
        functools.partial(behind_kernel, reach),
        out_shape=jax.ShapeDtypeStruct((height, (reach + 1) * count), key.dtype),
        in_specs=[pl.BlockSpec(memory_space=pl.ANY)],
        out_specs=pl.BlockSpec(memory_space=pl.ANY),
        scratch_shapes=[
            pltpu.SemaphoreType.DMA,
            pltpu.SemaphoreType.DMA((reach, 4)),
            pltpu.SemaphoreType.DMA((reach, 4)),
        ],
        compiler_params=pltpu.CompilerParams(collective_id=2, has_side_effects=True),
        name="gather_behind",
    )(key)


def fold_kernel(dims, parts, lanes, relative, cargo, *refs):
    (terms_ref, sum_ref, arrive_ref, leave_ref, send_sem, recv_sem), cargo = unpack(cargo, refs, 1, 1)
    cube = Cube(dims, parts)
    cube.greet(len(cargo) > 0)
    ship = cube.ship(cargo)
    for copy in ship:
        copy.start()
    height, width = sum_ref.shape
    size = height // parts
    width = width if lanes else None

    def term(part, mask):
        return cut(terms_ref, mask if relative else cube.device(mask)[1], pl.ds(part * size, size), width)

    def hop(part, mask, k, source):
        return pltpu.make_async_remote_copy(
            src_ref=source,
            dst_ref=arrive_ref.at[mask, pl.ds(part * size, size)],
            send_sem=send_sem.at[part, mask],
            recv_sem=recv_sem.at[part, mask],
            device_id=cube.device(1 << k),
            device_id_type=MESH,
        )

    sent = []
    for stage in range(len(dims) + 1):
        for part in range(parts):
            rows = pl.ds(part * size, size)
            order = cube.order(part)
            done = sum(1 << k for k in order[:stage])
            if stage:
                for mask in range(1 << len(dims)):
                    if not mask & done:
                        there = mask | 1 << order[stage - 1]
                        hop(part, there, order[stage - 1], arrive_ref.at[there, rows]).wait_recv()
            going = [0] if stage == len(dims) else [m for m in cube.masks if not m & done and m >> order[stage] & 1]
            for mask in going:
                source = term(part, mask)
                if stage:
                    total = source[...].astype(f32)
                    for k in order[:stage]:
                        total = total + arrive_ref[mask | 1 << k, rows].astype(f32)
                    if mask == 0:
                        sum_ref[rows] = total
                        continue
                    leave_ref[mask, rows] = total.astype(bf)
                    source = leave_ref.at[mask, rows]
                sent.append(hop(part, mask, order[stage], source))
                sent[-1].start()
    for copy in sent:
        copy.wait_send()
    for copy in ship:
        copy.wait()


def fold(terms, dims, parts, number, lanes=False, relative=False, cargo=None):
    count = 1 << len(dims)
    terms = terms.astype(bf)
    if lanes:
        shape = (terms.shape[0], terms.shape[1] // count)
    else:
        shape = (terms.shape[0] // count, terms.shape[1])
        terms = terms.reshape((count,) + shape)
    specs, shapes, semaphores = cargo_parts(cargo)
    total, *swapped = pl.pallas_call(
        functools.partial(fold_kernel, dims, parts, lanes, relative, cargo is not None),
        out_shape=[jax.ShapeDtypeStruct(shape, f32)] + shapes,
        in_specs=[pl.BlockSpec(memory_space=pltpu.VMEM)] + specs,
        out_specs=[pl.BlockSpec(memory_space=pltpu.VMEM)] + specs,
        scratch_shapes=[
            pltpu.VMEM((count,) + shape, bf),
            pltpu.VMEM((count,) + shape, bf),
            pltpu.SemaphoreType.DMA((parts, count)),
            pltpu.SemaphoreType.DMA((parts, count)),
        ]
        + semaphores,
        compiler_params=pltpu.CompilerParams(
            collective_id=number, has_side_effects=True, vmem_limit_bytes=VMEM_LIMIT
        ),
        name=f"fold{number}",
    )(*([terms] if cargo is None else [terms, cargo]))
    return (total, swapped[0]) if swapped else total


def dot(left, right, dims):
    return lax.dot_general(left, right, (dims, ((), ())), preferred_element_type=f32)


def multiply(left, right):
    return dot(left, right, ((1,), (0,)))


def against(left, right):
    return dot(left, right, ((1,), (1,)))


def over_rows(left, right):
    return dot(left, right, ((0,), (0,)))


def inverse_of(value, axis):
    return lax.rsqrt(jnp.mean(value * value, axis=axis, keepdims=True) + EPS)


def norm_back(value, inverse, gain, upstream, axis):
    unit = value * inverse
    scaled = upstream * gain
    inward = inverse * (scaled - unit * jnp.mean(scaled * unit, axis=axis, keepdims=True))
    return (inward, jnp.sum(upstream * unit, axis=1 - axis))


def angles(start, count):
    place = ((start + jnp.arange(count, dtype=jnp.int32)) % SEQ_LEN).astype(f32)
    half = DR // 2
    freq = jnp.exp(jnp.arange(half, dtype=f32) * (-math.log(THETA) / half))
    turn = freq[:, None] * place[None, :]
    return (jnp.cos(turn), jnp.sin(turn))


def rotate(front, behind, cosine, sine):
    return (front * cosine - behind * sine, behind * cosine + front * sine)


def query_columns(heads):
    tiles = -(-heads // 4)
    column = lax.iota(jnp.int32, heads * DN + tiles * 128)
    plain = (column // DN) * (DN + DR) + column % DN
    rest = column - heads * DN
    head = (rest // 128) * 4 + (rest % 64) // 16
    turned = head * (DN + DR) + DN + ((rest % 128) // 64) * 16 + rest % 16
    turned = jnp.where(head < heads, turned, -1)
    return jnp.where(column < heads * DN, plain, turned)


def latent_columns(heads):
    column = lax.iota(jnp.int32, heads * (DN + DV))
    rest = column % (heads * DN)
    return (rest // DN) * (DN + DV) + rest % DN + (column // (heads * DN)) * DN


def chosen(origin, width):
    return lax.broadcasted_iota(jnp.int32, (width, origin.shape[0]), 0) == origin[None, :]


BLOCK = 512


def head_rows(step, side, shape, axis):
    place = lax.broadcasted_iota(jnp.int32, shape, axis)
    plain = (place // DN == side).astype(f32).astype(bf)
    turned = ((place % 64) // 16 == 2 * (step % 2) + side).astype(f32).astype(bf)
    return (plain, turned)


def attend_kernel(
    blocks, first_ref, qn_ref, qr_ref, k_ref, kr_ref, vt_ref, bias_ref, o_ref, wide_ref, lse_ref, s_ref
):
    step = pl.program_id(0)
    first = first_ref[0]
    count = qn_ref.shape[1]
    sides = (0, 1)
    rights = []
    for side in sides:
        plain, turned = head_rows(step, side, qn_ref.shape, 0)
        rights.append(jnp.concatenate([qn_ref[...] * plain, qr_ref[...] * turned], axis=0))

    def score(j, tops):
        rows = pl.ds(pl.multiple_of(j * BLOCK, BLOCK), BLOCK)
        left = jnp.concatenate([k_ref[rows, :], kr_ref[rows, :]], axis=1)
        new = []
        for side in sides:
            s = multiply(left, rights[side]) * (SCALE * LOG2E) + bias_ref[rows, :]
            s_ref[side, rows, :] = s
            new.append(jnp.maximum(tops[side], jnp.max(s, axis=0, keepdims=True)))
        return tuple(new)

    tops = lax.fori_loop(first, blocks, score, (jnp.full((1, count), NEG, f32),) * 2)

    def gather(j, carry):
        rows = pl.ds(pl.multiple_of(j * BLOCK, BLOCK), BLOCK)
        new = []
        for side in sides:
            total, out = carry[side]
            chance = jnp.exp2(s_ref[side, rows, :] - tops[side])
            total = total + jnp.sum(chance, axis=0, keepdims=True)
            out = out + multiply(vt_ref[side * DV : (side + 1) * DV, rows], chance.astype(bf))
            new.append((total, out))
        return tuple(new)

    start = (jnp.zeros((1, count), f32), jnp.zeros((DV, count), f32))
    sums = lax.fori_loop(first, blocks, gather, (start, start))
    for side in sides:
        total, out = sums[side]
        out = out / total
        o_ref[side * DV : (side + 1) * DV, :] = out.astype(bf)
        wide_ref[side * DV : (side + 1) * DV, :] = out
        lse_ref[0, side : side + 1, :] = tops[side] + jnp.log2(total)


def attend(first, query, keys, turned_keys, values_t, bias, heads):
    count, kl = query.shape[1], keys.shape[0]
    pairs, base = heads // 2, heads * DN // 128
    grid = pltpu.PrefetchScalarGridSpec(
        num_scalar_prefetch=1,
        grid=(pairs,),
        in_specs=[
            pl.BlockSpec((128, count), lambda p, s: (p, 0)),
            pl.BlockSpec((128, count), lambda p, s: (base + p // 2, 0)),
            pl.BlockSpec((kl, 128), lambda p, s: (0, p)),
            pl.BlockSpec((kl, 128), lambda p, s: (0, 0)),
            pl.BlockSpec((128, kl), lambda p, s: (p, 0)),
            pl.BlockSpec((kl, count), lambda p, s: (0, 0)),
        ],
        out_specs=[
            pl.BlockSpec((128, count), lambda p, s: (p, 0)),
            pl.BlockSpec((128, count), lambda p, s: (p, 0)),
            pl.BlockSpec((1, 2, count), lambda p, s: (p, 0, 0)),
        ],
        scratch_shapes=[pltpu.VMEM((2, kl, count), f32)],
    )
    return pl.pallas_call(
        functools.partial(attend_kernel, kl // BLOCK),
        grid_spec=grid,
        out_shape=[
            jax.ShapeDtypeStruct((heads * DV, count), bf),
            jax.ShapeDtypeStruct((heads * DV, count), f32),
            jax.ShapeDtypeStruct((pairs, 2, count), f32),
        ],
        compiler_params=pltpu.CompilerParams(vmem_limit_bytes=VMEM_LIMIT),
        name="attend",
    )(first, query, query, keys, turned_keys, values_t, bias)


def attend_back_kernel(
    blocks, first_ref, qn_ref, qr_ref, qnn_ref, qrn_ref, k_ref, kr_ref, kt_ref, krt_ref, v_ref, dot_ref, do_ref, o_ref,
    bias_ref, lse_ref, dqn_ref, dqr_ref, dk_ref, dv_ref, dkr_ref,
):
    step = pl.program_id(0)
    first = first_ref[0]
    count = qn_ref.shape[1]
    sides = (0, 1)

    @pl.when(step == 0)
    def _():
        dkr_ref[...] = jnp.zeros_like(dkr_ref)

    @pl.when(step % 2 == 0)
    def _():
        dqr_ref[...] = jnp.zeros_like(dqr_ref)

    dk_ref[...] = jnp.zeros_like(dk_ref)
    dv_ref[...] = jnp.zeros_like(dv_ref)
    rights, out_rights, query_rights, value_rights, lses, deltas = [], [], [], [], [], []
    for side in sides:
        plain, turned = head_rows(step, side, qn_ref.shape, 0)
        rights.append(jnp.concatenate([qn_ref[...] * plain, qr_ref[...] * turned], axis=0))
        out_rights.append(dot_ref[...] * plain)
        plain_l, turned_l = head_rows(step, side, qnn_ref.shape, 1)
        query_rights.append(jnp.concatenate([qnn_ref[...] * plain_l, qrn_ref[...] * turned_l], axis=1))
        value_rights.append(do_ref[...] * plain_l)
        lses.append(lse_ref[0, side : side + 1, :])
        rows = slice(side * DV, (side + 1) * DV)
        deltas.append(jnp.sum(dot_ref[rows, :].astype(f32) * o_ref[rows, :], axis=0, keepdims=True))

    def block(j, dqs):
        rows = pl.ds(pl.multiple_of(j * BLOCK, BLOCK), BLOCK)
        left = jnp.concatenate([k_ref[rows, :], kr_ref[rows, :]], axis=1)
        left_t = jnp.concatenate([kt_ref[:, rows], krt_ref[:, rows]], axis=0)
        new, dk, dv = [], 0.0, 0.0
        for side in sides:
            s = multiply(left, rights[side]) * (SCALE * LOG2E) + bias_ref[rows, :]
            chance = jnp.exp2(s - lses[side])
            back = multiply(v_ref[rows, :], out_rights[side])
            ds = (chance * (back - deltas[side])).astype(bf)
            new.append(dqs[side] + multiply(left_t, ds))
            dk = dk + multiply(ds, query_rights[side])
            dv = dv + multiply(chance.astype(bf), value_rights[side])
        dk_ref[rows, :] = (dk[:, :128] * SCALE).astype(bf)
        dkr_ref[rows, :] += dk[:, 128:] * SCALE
        dv_ref[rows, :] = dv.astype(bf)
        return tuple(new)

    dqs = lax.fori_loop(first, blocks, block, (jnp.zeros((256, count), f32),) * 2)
    place = lax.broadcasted_iota(jnp.int32, (128, count), 0)
    for side in sides:
        dq = dqs[side] * SCALE
        dqn_ref[side * DN : (side + 1) * DN, :] = dq[side * DN : (side + 1) * DN]
        dqr_ref[...] += jnp.where((place % 64) // 16 == 2 * (step % 2) + side, dq[128:], 0.0)


def attend_back(
    first, query, query_n, keys, turned_keys, keys_t, turned_keys_t, values, do_t, do, out, bias, lse, heads
):
    count, kl = query.shape[1], keys.shape[0]
    pairs, base, tiles = heads // 2, heads * DN // 128, -(-heads // 4)
    across = lambda p, s: (0, p)
    along = lambda p, s: (p, 0)
    fixed = lambda p, s: (0, 0)
    grid = pltpu.PrefetchScalarGridSpec(
        num_scalar_prefetch=1,
        grid=(pairs,),
        in_specs=[
            pl.BlockSpec((128, count), along),
            pl.BlockSpec((128, count), lambda p, s: (base + p // 2, 0)),
            pl.BlockSpec((count, 128), across),
            pl.BlockSpec((count, 128), lambda p, s: (0, base + p // 2)),
            pl.BlockSpec((kl, 128), across),
            pl.BlockSpec((kl, 128), fixed),
            pl.BlockSpec((128, kl), along),
            pl.BlockSpec((128, kl), fixed),
            pl.BlockSpec((kl, 128), across),
            pl.BlockSpec((128, count), along),
            pl.BlockSpec((count, 128), across),
            pl.BlockSpec((128, count), along),
            pl.BlockSpec((kl, count), fixed),
            pl.BlockSpec((1, 2, count), lambda p, s: (p, 0, 0)),
        ],
        out_specs=[
            pl.BlockSpec((128, count), along),
            pl.BlockSpec((128, count), lambda p, s: (p // 2, 0)),
            pl.BlockSpec((kl, 128), across),
            pl.BlockSpec((kl, 128), across),
            pl.BlockSpec((kl, 128), fixed),
        ],
    )
    return pl.pallas_call(
        functools.partial(attend_back_kernel, kl // BLOCK),
        grid_spec=grid,
        out_shape=[
            jax.ShapeDtypeStruct((heads * DN, count), f32),
            jax.ShapeDtypeStruct((tiles * 128, count), f32),
            jax.ShapeDtypeStruct((kl, heads * DN), bf),
            jax.ShapeDtypeStruct((kl, heads * DV), bf),
            jax.ShapeDtypeStruct((kl, 128), f32),
        ],
        compiler_params=pltpu.CompilerParams(vmem_limit_bytes=VMEM_LIMIT),
        name="attend_back",
    )(first, query, query, query_n, query_n, keys, turned_keys, keys_t, turned_keys_t, values, do_t, do, out, bias, lse)


TOKENS = 256


def dot_pieces(left, pieces):
    width = pieces[0].shape[2]
    total = None
    for k, piece in enumerate(pieces):
        term = against(left[:, k * width : (k + 1) * width], piece[0])
        total = term if total is None else total + term
    return total


def ffn_kernel(n, x_ref, *refs):
    gate = dot_pieces(x_ref, refs[:n])
    upward = dot_pieces(x_ref, refs[n : 2 * n])
    gate_ref, up_ref, hidden_ref = refs[2 * n :]
    gate_ref[...] = gate
    up_ref[...] = upward
    hidden_ref[...] = (gate / (1.0 + jnp.exp(-gate)) * upward).astype(bf)


def piece_specs(pieces):
    def spec(array, index):
        return pl.BlockSpec((1,) + array.shape[1:], lambda i: (index, 0, 0), pipeline_mode=pl.Buffered(1))

    return [spec(array, index) for array, index in pieces]


def ffn(x, gate, up):
    tokens, hidden = x.shape[0], gate[0][0].shape[1]
    tile = lambda width: pl.BlockSpec((TOKENS, width), lambda i: (i, 0))
    return pl.pallas_call(
        functools.partial(ffn_kernel, len(gate)),
        grid=(tokens // TOKENS,),
        out_shape=[
            jax.ShapeDtypeStruct((tokens, hidden), f32),
            jax.ShapeDtypeStruct((tokens, hidden), f32),
            jax.ShapeDtypeStruct((tokens, hidden), bf),
        ],
        in_specs=[tile(x.shape[1])] + piece_specs(gate + up),
        out_specs=[tile(hidden)] * 3,
        compiler_params=pltpu.CompilerParams(vmem_limit_bytes=VMEM_LIMIT),
        name="ffn",
    )(x, *[array for array, _ in gate + up])


def ffn_back_kernel(n, dm_ref, gate_ref, up_ref, hidden_ref, *refs):
    gates, ups, down = refs[:n], refs[n : 2 * n], refs[2 * n : 3 * n]
    dgate_ref, dup_ref, dx_ref, out_ref = refs[3 * n :]
    width = down[0].shape[2]
    back_hidden = dot_pieces(dm_ref, down)
    gate, upward = gate_ref[...], up_ref[...]
    sigma = 1.0 / (1.0 + jnp.exp(-gate))
    dgate_ref[...] = (back_hidden * upward * sigma * (1.0 + gate * (1.0 - sigma))).astype(bf)
    dup_ref[...] = (back_hidden * gate * sigma).astype(bf)
    for k in range(n):
        lanes = slice(k * width, (k + 1) * width)
        dx_ref[:, lanes] = (multiply(dgate_ref[...], gates[k][0]) + multiply(dup_ref[...], ups[k][0])).astype(bf)
        out_ref[:, lanes] = multiply(hidden_ref[...], down[k][0]).astype(bf)


def ffn_back(dm, gate, upward, hidden, pieces, n):
    tokens, units = gate.shape
    tile = lambda width: pl.BlockSpec((TOKENS, width), lambda i: (i, 0))
    return pl.pallas_call(
        functools.partial(ffn_back_kernel, n),
        grid=(tokens // TOKENS,),
        out_shape=[
            jax.ShapeDtypeStruct((tokens, units), bf),
            jax.ShapeDtypeStruct((tokens, units), bf),
            jax.ShapeDtypeStruct(dm.shape, bf),
            jax.ShapeDtypeStruct(dm.shape, bf),
        ],
        in_specs=[tile(dm.shape[1]), tile(units), tile(units), tile(units)] + piece_specs(pieces),
        out_specs=[tile(units), tile(units), tile(dm.shape[1]), tile(dm.shape[1])],
        compiler_params=pltpu.CompilerParams(vmem_limit_bytes=VMEM_LIMIT),
        name="ffn_back",
    )(dm, gate, upward, hidden, *[array for array, _ in pieces])


def shards(
    tokens, document_ids, gain_first, query_down, query_gain, latent_down, latent_gain, query_up, latent_up,
    output_weight, gain_second, gate_weight, up_weight, down_weight, cotangent,
):
    count, own_width = tokens.shape
    rows, cols = lax.axis_size("row"), lax.axis_size("col")
    row, column = lax.axis_index("row"), lax.axis_index("col")
    start = row * count
    heads = query_up.shape[1] // (DN + DR)
    reach = -(-(DOC_MOST - 1) // count)
    blocks = reach + 1
    wide = heads * DN
    quarter = count // cols
    cosine, sine = angles(start, count)

    both_down = jnp.concatenate([query_down, latent_down], axis=1).astype(bf)
    down_slice = pick(quarters(both_down, 1))
    slice_width = down_slice.shape[1]
    small = jnp.concatenate([query_gain, latent_gain]).astype(bf)
    small = jnp.pad(small, (0, gain_first.shape[0] - small.shape[0]))
    gains = jnp.stack([gain_first.astype(bf), gain_second.astype(bf), small], axis=1)
    query_one = chosen(query_columns(heads), heads * (DN + DR))
    latent_one = chosen(latent_columns(heads), heads * (DN + DV))
    query_up_low = multiply(query_up.astype(bf), query_one.astype(bf)).astype(bf)
    latent_up_low = multiply(latent_up.astype(bf), latent_one.astype(bf)).astype(bf)
    down_block = jnp.concatenate([down_slice, gains], axis=1)
    down_block = jnp.pad(down_block, ((0, 0), (0, -down_block.shape[1] % 128)))
    ffn_weights = HiddenGather(
        jnp.stack([gate_weight.astype(bf).T, up_weight.astype(bf).T, down_weight.astype(bf)])
    )
    (wide_down, wide_query_up, wide_latent_up), features, own_up, came = ring_gather(
        (down_block, query_up_low, latent_up_low), tokens, cotangent, ffn_weights.away[:1]
    )
    first_own = ffn_weights.arrived(came, 0, 1)
    back_down = spread(features_by_group((RES * own_up).astype(bf)), GROUP, 4, 12, relative=True)
    others = swap_row(after(ffn_weights.away[1:], back_down), PAIR)
    early = (ffn_weights.near_own(first_own, 0, 1, back_down), ffn_weights.far(0, back_down), others)
    wide_output = lax.all_gather(after(output_weight, back_down).astype(bf).T, "row", axis=0, tiled=True)
    gain_one = wide_down[:, slice_width].astype(f32)
    gain_two = wide_down[:, slice_width + 1].astype(f32)
    small_gains = wide_down[:, slice_width + 2].reshape(rows, -1).astype(f32)
    own_q = query_gain.shape[0]
    query_scale = small_gains[:, :own_q].reshape(-1)[:, None]
    latent_scale = small_gains[:, own_q : own_q + latent_gain.shape[0]].reshape(-1)[:, None]
    wide_down = wide_down[:, :slice_width]

    residual = features.astype(f32)
    first_in = (residual * inverse_of(residual, 1) * gain_one).astype(bf)
    own_residual = pick(quarters(features, 0)).astype(f32)

    latents = jnp.concatenate(col_gather(dot(wide_down, first_in, ((0,), (1,)))), axis=0)
    query_latent, latent_part = latents[:QR], latents[QR : QR + KR]
    inverse_query, inverse_latent = inverse_of(query_latent, 0), inverse_of(latent_part, 0)
    query_in = (query_latent * inverse_query * query_scale).astype(bf)
    latent_in = (latent_part * inverse_latent * latent_scale).astype(bf)
    half = DR // 2
    key_front, key_back = rotate(latents[QR + KR : QR + KR + half], latents[QR + KR + half :], cosine, sine)
    key_part = jnp.concatenate([latent_in, key_front.astype(bf), key_back.astype(bf)], axis=0)
    key_parts = gather_behind(after(key_part, early), reach)
    other_own = ffn_weights.arrived(others, 1, 3)
    beside = ffn_weights.near_own(other_own, 1, 3, key_parts)
    far_up, far_down = ffn_weights.far(1, key_parts), ffn_weights.far(2, key_parts)
    latent_all = key_parts[:KR]
    turned_t = jnp.concatenate([key_parts[KR : KR + half]] * 4 + [key_parts[KR + half :]] * 4, axis=0)
    turned = turned_t.T

    key_place = start - reach * count + jnp.arange(blocks * count, dtype=jnp.int32)
    place = start + jnp.arange(count, dtype=jnp.int32)
    key_doc = lax.dynamic_slice_in_dim(jnp.pad(document_ids, (reach * count, 0)), start, blocks * count)
    doc = lax.dynamic_slice_in_dim(document_ids, start, count)
    allowed = (key_doc[:, None] == doc[None, :]) & (key_place[:, None] <= place[None, :])
    allowed = allowed & (key_place[:, None] >= (place // SEQ_LEN * SEQ_LEN)[None, :])
    bias = jnp.where(allowed, 0.0, NEG).astype(f32)
    doc_start = jnp.sum((document_ids < doc[0]).astype(jnp.int32))
    first = jnp.clip((doc_start - (start - reach * count)) // BLOCK, 0, reach).reshape(1)

    raw = over_rows(wide_query_up, query_in)
    tiles = raw[wide:].reshape(-1, 2, 64, count)
    cos_tile, sin_tile = jnp.tile(cosine, (4, 1)), jnp.tile(sine, (4, 1))
    query_turned = jnp.stack(rotate(tiles[:, 0], tiles[:, 1], cos_tile, sin_tile), axis=1).reshape(-1, count)
    query = jnp.concatenate([raw[:wide], query_turned], axis=0).astype(bf)
    up_keys, up_values = wide_latent_up[:, :wide], wide_latent_up[:, wide:]
    keys = over_rows(latent_all, up_keys).astype(bf)
    values_t = over_rows(up_values, latent_all).astype(bf)
    out_t, out_wide, lse = attend(first, query, keys, turned, values_t, bias, heads)

    gate_pieces = ffn_weights.near(0, out_t)
    out_t = after(out_t, beside)
    branch = dot(out_t, wide_output, ((0,), (1,)))
    middle = own_residual + RES * fold(branch, COLS, 8, 4)
    middle = after(middle, far_up)
    up_pieces = ffn_weights.near(1, middle)
    middle = after(middle, far_down)
    down_pieces = ffn_weights.near(2, middle)
    inverse_second = inverse_of(middle, 1)
    second_in = features_by_group((middle * inverse_second * gain_two).astype(bf))
    second_in = spread(second_in, GROUP, 8, 5, relative=True)

    gate, upward, hidden = ffn(second_in, gate_pieces, up_pieces)
    slope_down = HiddenScatter(hidden, back_down)
    slope_down.near(hidden)
    gate = after(gate, slope_down.away)
    back_gate, back_upward, back_second, out_part = ffn_back(
        back_down, gate, upward, hidden, gate_pieces + up_pieces + down_pieces, len(gate_pieces)
    )
    slope_gate = HiddenScatter(back_gate, second_in)
    slope_gate.near(back_gate)
    back_second = after(back_second, slope_gate.away)
    back_second = features_in_order(fold(back_second, GROUP, 8, 6, relative=True))
    slope_up = HiddenScatter(back_upward, second_in)
    own_result = GroupScatter(out_part)
    back_norm, gain_second_part = norm_back(middle, inverse_second, gain_two, back_second, 1)
    back_middle = own_up + back_norm
    back_branch = after((RES * back_middle).astype(bf), (slope_down.came, own_result.came, slope_up.away))
    slope_up.near(back_branch)
    slope_down.far(back_branch)
    back_branch = spread(back_branch, COLS, 8, 7)
    own_result.across(back_branch)

    out = out_t.T
    back_out = multiply(back_branch, wide_output).astype(bf)
    slope_gate.far(back_out)
    keys_t = over_rows(up_keys, latent_all).astype(bf)
    values = over_rows(latent_all, up_values).astype(bf)
    back_query_n, back_query_r, back_keys, back_values, back_turned = attend_back(
        first, query, query.T, keys, turned, keys_t, turned_t, values, back_out.T, back_out, out_wide, bias, lse, heads
    )
    back_query_n = after(back_query_n, (slope_down.came, slope_gate.came, slope_up.came, own_result.came))
    slope_up.far(back_query_n)
    own_result.partner(back_query_n)
    tiles = back_query_r.reshape(-1, 2, 64, count)
    back_turn = jnp.stack(rotate(tiles[:, 0], tiles[:, 1], cos_tile, -sin_tile), axis=1).reshape(-1, count)
    back_raw = jnp.concatenate([back_query_n, back_turn], axis=0).astype(bf)
    query_part = multiply(wide_query_up, back_raw)
    latent_back = against(up_keys, back_keys) + against(up_values, back_values)
    turned_back = jnp.sum(back_turned.T.reshape(2, 4, half, blocks * count), axis=1).reshape(DR, blocks * count)
    far = jnp.concatenate([latent_back, turned_back], axis=0)
    to_send = jnp.concatenate(
        [query_part] + [far[:, b * count : (b + 1) * count] for b in range(blocks)], axis=0
    )
    summed = after(fold(to_send, COLS, 3, 8, lanes=True), slope_up.came)
    slope_down.came, slope_gate.came = after((slope_down.came, slope_gate.came), summed)
    own_result = middle + RES * features_in_order(own_result.result())
    back_query_in = summed[:QR]
    wide_far = KR + DR
    parts = [summed[QR + b * wide_far : QR + (b + 1) * wide_far] for b in range(blocks)]
    back_key = parts[reach]
    for step in range(1, reach + 1):
        back_key = back_key + from_behind(parts[reach - step], -step)

    own_latents = pick(quarters(latents, 1))
    own_query, own_latent = own_latents[:QR], own_latents[QR : QR + KR]
    back_query_latent, query_gain_part = norm_back(
        own_query, inverse_of(own_query, 0), query_scale, back_query_in, 0
    )
    back_latent, latent_gain_part = norm_back(
        own_latent, inverse_of(own_latent, 0), latent_scale, back_key[:KR], 0
    )
    own_cosine, own_sine = pick(quarters(cosine, 1)), pick(quarters(sine, 1))
    back_front, back_behind = rotate(back_key[KR : KR + half], back_key[KR + half :], own_cosine, -own_sine)
    back_latents = jnp.concatenate([back_query_latent, back_latent, back_front, back_behind], axis=0).astype(bf)
    back_latents = spread(back_latents, COLS, 3, 9, lanes=True)
    back_slice = lax.dynamic_slice_in_dim(back_latents, column * slice_width, slice_width, 0)
    halves = [flow.halves() for flow in (slope_down, slope_gate)]
    away = jnp.stack([gone for _, gone in halves])
    back_first, came = fold(dot(back_slice, wide_down, ((0,), (1,))), COLS, 8, 10, cargo=away)
    slope_down, slope_gate = (in_pair_order(mine, got, 0) for (mine, _), got in zip(halves, came))
    back_norm_first, gain_first_part = norm_back(own_residual, inverse_of(own_residual, 1), gain_one, back_first, 1)
    own_back = back_middle + back_norm_first

    packed = jnp.concatenate(
        [part.reshape(rows, -1) for part in (gain_first_part, gain_second_part, query_gain_part, latent_gain_part)],
        axis=1,
    )
    packed = jnp.pad(packed, ((0, 0), (0, -packed.shape[1] % 256))).reshape(-1, 128)
    back_slice_n = jnp.pad(back_slice.T, ((0, 0), (0, -slice_width % 128)))
    slope_up.came = after(slope_up.came, back_first)
    slope_up, away = slope_up.halves()
    (slope_output, slope_query_up, slope_latent_up, slope_down_slice, packed), came, (result, back_tokens) = ring_scatter((
        over_rows(back_branch, out).astype(bf),
        against(query_in, back_raw).astype(bf),
        multiply(latent_all, jnp.concatenate([back_keys, back_values], axis=1)).astype(bf),
        over_rows(first_in, back_slice_n).astype(bf),
        packed,
    ), away, (own_result, own_back))
    slope_up = in_pair_order(slope_up, came, 0)
    n, m, k = gain_first.shape[0], query_gain.shape[0], latent_gain.shape[0]
    packed = packed.reshape(-1)[: 2 * n + m + k]
    packed = jnp.pad(packed, (0, n - m - k)).reshape(3, n).T
    block = jnp.concatenate([slope_down_slice[:, :slice_width], packed], axis=1).astype(bf)
    block = jnp.pad(block, ((0, 0), (0, -block.shape[1] % 128)))
    blocks = quarters(spread(block, COLS, 2, 11, lanes=True), 1)
    slope_both = jnp.concatenate([piece[:, :slice_width] for piece in blocks], axis=1).astype(f32)
    packed = sum(piece[:, slice_width : slice_width + 3].astype(f32) for piece in blocks).T.reshape(-1)

    exact = functools.partial(
        lax.dot_general,
        dimension_numbers=(((1,), (1,)), ((), ())),
        precision=lax.Precision.HIGHEST,
        preferred_element_type=f32,
    )
    return (
        result,
        back_tokens,
        packed[:n],
        slope_both[:, :QR],
        packed[2 * n : 2 * n + m],
        slope_both[:, QR:],
        packed[2 * n + m : 2 * n + m + k],
        exact(slope_query_up, query_one.astype(f32)),
        exact(slope_latent_up, latent_one.astype(f32)),
        slope_output.T,
        packed[n : 2 * n],
        slope_gate.T.astype(f32),
        slope_up.T.astype(f32),
        slope_down.astype(f32),
    )


def solution(mesh):
    placed = (
        P("row", "col"), P(), P("row"), P("row", None), P("row"), P("row", None), P("row"), P("row", "col"),
        P("row", "col"), P("col", "row"), P("row"), P("row", "col"), P("row", "col"), P("col", "row"),
        P("row", "col"),
    )
    outs = (
        P("row", "col"), P("row", "col"), P("row"), P("row", None), P("row"), P("row", None), P("row"),
        P("row", "col"), P("row", "col"), P("col", "row"), P("row"), P("row", "col"), P("row", "col"),
        P("col", "row"),
    )
    return jax.shard_map(shards, mesh=mesh, in_specs=placed, out_specs=outs, check_vma=False)
```

```python
import functools
import math

import jax
import jax.numpy as jnp
from jax import lax
from jax.experimental import pallas as pl
from jax.experimental.pallas import tpu as pltpu
from jax.sharding import PartitionSpec as P

DN = 64
DR = 32
DV = 64
QR = 768
KR = 256
SEQ_LEN = 4096
DOC_MOST = 2000
EPS = 1e-05
RES = 1.4 / math.sqrt(62.0)
THETA = 10000.0
NEG = -1e30
LOG2E = math.log2(math.e)
SCALE = (DN + DR) ** (-0.5)
VMEM_LIMIT = 56 << 20
MESH = pl.DeviceIdType.MESH
PAIR = 2
bf = jnp.bfloat16
f32 = jnp.float32


def ring_place(row, rows):
    return row // 2 + (row % 2) * (rows - 1 - 2 * (row // 2))


def ring_row(place, rows):
    side = place // (rows // 2)
    return 2 * (place + side * (rows - 1 - 2 * place)) + side


def flip(value, bit):
    return value + bit * (1 - 2 * ((value // bit) % 2))


def ring_barrier(others):
    barrier = pltpu.get_barrier_semaphore()
    for other in others:
        pl.semaphore_signal(barrier, inc=1, device_id=other, device_id_type=MESH)
    pl.semaphore_wait(barrier, len(others))


def col_peers(column, cols):
    return [flip(flip(column, 1) if k & 1 else column, 2) if k & 2 else flip(column, 1) for k in range(1, cols)]


def ring_gather_kernel(rows, n, *refs):
    blocks, (tokens_ref, back_ref, away_ref), refs = refs[:n], refs[n : n + 3], refs[n + 3 :]
    wholes, (features_ref, own_back_ref, came_ref), refs = refs[:n], refs[n : n + 3], refs[n + 3 :]
    own_sem, send_sem, recv_sem, col_send, col_recv = refs
    row, column = lax.axis_index("row"), lax.axis_index("col")
    place = ring_place(row, rows)
    ends = (ring_row((place + 1) % rows, rows), ring_row((place + rows - 1) % rows, rows))
    cols = features_ref.shape[1] // tokens_ref.shape[1]
    quarter = back_ref.shape[0] // cols
    peers = col_peers(column, cols)
    partner = (flip(row, PAIR), column)
    ring_barrier([(ends[0], column), (ends[1], column), partner] + [(row, peer) for peer in peers])
    lanes = pl.ds(pl.multiple_of(column * tokens_ref.shape[1], 128), tokens_ref.shape[1])

    def to_col(k, target):
        part = back_ref.at[pl.ds(pl.multiple_of(target * quarter, 128), quarter)]
        return [(tokens_ref, features_ref.at[:, lanes]), (part, own_back_ref.at[:, lanes])]

    crossing = []
    for k, peer in enumerate(peers):
        for which, (source, there) in enumerate(to_col(k, peer)):
            crossing.append(
                pltpu.make_async_remote_copy(
                    src_ref=source,
                    dst_ref=there,
                    send_sem=col_send.at[which, k],
                    recv_sem=col_recv.at[which, k],
                    device_id=(row, peer),
                    device_id_type=MESH,
                )
            )
    crossing.append(
        pltpu.make_async_remote_copy(
            src_ref=away_ref,
            dst_ref=came_ref,
            send_sem=col_send.at[2, 0],
            recv_sem=col_recv.at[2, 0],
            device_id=partner,
            device_id_type=MESH,
        )
    )
    staying = [
        pltpu.make_async_copy(source, there, own_sem.at[n + which])
        for which, (source, there) in enumerate(to_col(-1, column))
    ]

    def own(k):
        return pltpu.make_async_copy(blocks[k], wholes[k].at[row], own_sem.at[k])

    def hop(step, side, k):
        origin = ring_row((place + (step if side else rows - step)) % rows, rows)
        return pltpu.make_async_remote_copy(
            src_ref=wholes[k].at[origin, side],
            dst_ref=wholes[k].at[origin, side],
            send_sem=send_sem.at[step, side, k],
            recv_sem=recv_sem.at[step, side, k],
            device_id=(ends[side], column),
            device_id_type=MESH,
        )

    for k in range(n):
        own(k).start()
    for k in range(n):
        own(k).wait()
        for side in (0, 1):
            hop(0, side, k).start()
    for copy in crossing + staying:
        copy.start()

    def advance(step, carry):
        for k in range(n):
            for side in (0, 1):
                hop(step - 1, side, k).wait_recv()
                hop(step, side, k).start()
        return carry

    lax.fori_loop(1, rows - 1, advance, 0)
    for k in range(n):
        for side in (0, 1):
            hop(rows - 2, side, k).wait_recv()

    def drain(step, carry):
        for k in range(n):
            for side in (0, 1):
                hop(step, side, k).wait_send()
        return carry

    lax.fori_loop(0, rows - 1, drain, 0)
    for copy in crossing + staying:
        copy.wait()


def ring_gather(blocks, tokens, back, away):
    rows, cols, n = lax.axis_size("row"), lax.axis_size("col"), len(blocks)
    halves = [block.reshape(2, block.shape[0] // 2, block.shape[1]) for block in blocks]
    anywhere = pl.BlockSpec(memory_space=pl.ANY)
    *wholes, features, own_back, came = pl.pallas_call(
        functools.partial(ring_gather_kernel, rows, n),
        out_shape=[jax.ShapeDtypeStruct((rows,) + half.shape, half.dtype) for half in halves]
        + [
            jax.ShapeDtypeStruct((tokens.shape[0], cols * tokens.shape[1]), tokens.dtype),
            jax.ShapeDtypeStruct((back.shape[0] // cols, cols * back.shape[1]), back.dtype),
            jax.ShapeDtypeStruct(away.shape, away.dtype),
        ],
        in_specs=[anywhere] * (n + 3),
        out_specs=[anywhere] * (n + 3),
        scratch_shapes=[
            pltpu.SemaphoreType.DMA((n + 2,)),
            pltpu.SemaphoreType.DMA((rows - 1, 2, n)),
            pltpu.SemaphoreType.DMA((rows - 1, 2, n)),
            pltpu.SemaphoreType.DMA((3, cols - 1)),
            pltpu.SemaphoreType.DMA((3, cols - 1)),
        ],
        compiler_params=pltpu.CompilerParams(collective_id=0, has_side_effects=True),
        name="ring_gather",
    )(*halves, tokens, back, away)
    wholes = [whole.reshape(rows * block.shape[0], block.shape[1]) for whole, block in zip(wholes, blocks)]
    return wholes, features, own_back, came


def ring_scatter_kernel(rows, n, extra, *refs):
    terms, away_ref, leaving, refs = refs[:n], refs[n], refs[n + 1 : n + 1 + extra], refs[n + 1 + extra :]
    sums, came_ref, arriving, refs = refs[:n], refs[n], refs[n + 1 : n + 1 + extra], refs[n + 1 + extra :]
    slots, refs = refs[:n], refs[n:]
    send_sem, recv_sem, swap_send, swap_recv, own_sem, col_send, col_recv = refs
    row, column = lax.axis_index("row"), lax.axis_index("col")
    place = ring_place(row, rows)
    ends = (ring_row((place + 1) % rows, rows), ring_row((place + rows - 1) % rows, rows))
    partner = (flip(row, PAIR), column)
    cols = lax.axis_size("col")
    peers = col_peers(column, cols)
    ring_barrier([(ends[0], column), (ends[1], column), partner] + [(row, peer) for peer in peers])
    crossing = []
    for e in range(extra):
        quarter, width = leaving[e].shape[0], leaving[e].shape[1] // cols
        place_there = arriving[e].at[pl.ds(pl.multiple_of(column * quarter, 128), quarter)]

        def features(target):
            return leaving[e].at[:, pl.ds(pl.multiple_of(target * width, 128), width)]

        crossing.append(pltpu.make_async_copy(features(column), place_there, own_sem.at[e]))
        for k, peer in enumerate(peers):
            crossing.append(
                pltpu.make_async_remote_copy(
                    src_ref=features(peer),
                    dst_ref=place_there,
                    send_sem=col_send.at[e, k],
                    recv_sem=col_recv.at[e, k],
                    device_id=(row, peer),
                    device_id_type=MESH,
                )
            )
    swap = pltpu.make_async_remote_copy(
        src_ref=away_ref,
        dst_ref=came_ref,
        send_sem=swap_send,
        recv_sem=swap_recv,
        device_id=partner,
        device_id_type=MESH,
    )

    def target(step, side):
        return ring_row((place + (1 + step if side else 2 * rows - 1 - step)) % rows, rows)

    def hop(step, side, k, source):
        return pltpu.make_async_remote_copy(
            src_ref=source,
            dst_ref=slots[k].at[step, side],
            send_sem=send_sem.at[step, side, k],
            recv_sem=recv_sem.at[step, side, k],
            device_id=(ends[side], column),
            device_id_type=MESH,
        )

    def first(side, k):
        return hop(0, side, k, terms[k].at[target(0, side), side])

    def later(step, side, k):
        return hop(step, side, k, slots[k].at[step - 1, side])

    for k in range(n):
        for side in (0, 1):
            first(side, k).start()
    swap.start()
    for copy in crossing:
        copy.start()

    def arrive(step, side, k):
        return hop(step, side, k, slots[k].at[step, side])

    def advance(step, carry):
        for k in range(n):
            for side in (0, 1):
                arrive(step - 1, side, k).wait_recv()
                total = slots[k][step - 1, side].astype(f32) + terms[k][target(step, side), side].astype(f32)
                slots[k][step - 1, side] = total.astype(slots[k].dtype)
                later(step, side, k).start()
        return carry

    lax.fori_loop(1, rows - 1, advance, 0)
    for k in range(n):
        for side in (0, 1):
            arrive(rows - 2, side, k).wait_recv()
            sums[k][side] = slots[k][rows - 2, side].astype(f32) + terms[k][row, side].astype(f32)

    def drain(step, carry):
        for k in range(n):
            for side in (0, 1):
                arrive(step, side, k).wait_send()
        return carry

    lax.fori_loop(0, rows - 1, drain, 0)
    swap.wait()
    for copy in crossing:
        copy.wait()


def ring_scatter(terms, away, leaving):
    rows, n = lax.axis_size("row"), len(terms)
    split = [term.reshape(rows, 2, term.shape[0] // rows // 2, term.shape[1]) for term in terms]
    anywhere = pl.BlockSpec(memory_space=pl.ANY)
    cols, extra = lax.axis_size("col"), len(leaving)
    *sums, came, first, second = pl.pallas_call(
        functools.partial(ring_scatter_kernel, rows, n, extra),
        out_shape=[jax.ShapeDtypeStruct(term.shape[1:], f32) for term in split]
        + [jax.ShapeDtypeStruct(away.shape, away.dtype)]
        + [jax.ShapeDtypeStruct((v.shape[0] * cols, v.shape[1] // cols), v.dtype) for v in leaving],
        in_specs=[pl.BlockSpec(memory_space=pltpu.VMEM)] * n + [anywhere] * (1 + extra),
        out_specs=[pl.BlockSpec(memory_space=pltpu.VMEM)] * n + [anywhere] * (1 + extra),
        scratch_shapes=[pltpu.VMEM((rows - 1,) + term.shape[1:], term.dtype) for term in split]
        + [pltpu.SemaphoreType.DMA((rows - 1, 2, n)), pltpu.SemaphoreType.DMA((rows - 1, 2, n))]
        + [pltpu.SemaphoreType.DMA, pltpu.SemaphoreType.DMA, pltpu.SemaphoreType.DMA((extra,))]
        + [pltpu.SemaphoreType.DMA((extra, cols - 1)), pltpu.SemaphoreType.DMA((extra, cols - 1))],
        compiler_params=pltpu.CompilerParams(
            collective_id=1, has_side_effects=True, vmem_limit_bytes=VMEM_LIMIT
        ),
        name="ring_scatter",
    )(*split, away, *leaving)
    return [total.reshape(total.shape[0] * total.shape[1], total.shape[2]) for total in sums], came, (first, second)


def from_behind(value, steps):
    count = lax.axis_size("row")
    initial, last = (max(0, -steps), min(count, count - steps))
    return lax.ppermute(value, "row", [(source, source + steps) for source in range(initial, last)])


def swap_col(value, bit):
    return lax.ppermute(value, "col", [(c, c ^ bit) for c in range(lax.axis_size("col"))])


def by_owner(pieces, own=None):
    own = lax.axis_index("col") if own is None else own
    bit = 1
    pieces = list(pieces)
    while bit < len(pieces):
        odd = (own // bit) % 2 == 1
        pieces = [jnp.where(odd, pieces[k ^ bit], pieces[k]) for k in range(len(pieces))]
        bit *= 2
    return pieces


def pick(pieces):
    return by_owner(pieces)[0]


def col_gather(own):
    across = swap_col(own, 2)
    beside = swap_col(own, 1)
    return by_owner([own, beside, across, swap_col(across, 1)])


def col_scatter(pieces):
    mine = by_owner(pieces)
    low = [piece.astype(bf) for piece in mine]
    across = mine[2].astype(f32) + swap_col(low[3], 1).astype(f32)
    beside = mine[0].astype(f32) + swap_col(low[1], 1).astype(f32)
    return beside + swap_col(across.astype(bf), 2).astype(f32)


def quarters(value, axis):
    return jnp.split(value, lax.axis_size("col"), axis=axis)


def group_row(group, side):
    return (group // 2) * 4 + side * PAIR + group % 2


def own_group():
    row = lax.axis_index("row")
    return ((row // 4) * 2 + row % 2, (row // PAIR) % 2)


def swap_row(value, mask):
    return lax.ppermute(value, "row", [(r, r ^ mask) for r in range(lax.axis_size("row"))])


def group_masks():
    bits = (lax.axis_size("row") // 2).bit_length() - 1
    return [(1 << b, group_row(1 << b, 0)) for b in reversed(range(bits))]


def after(value, other):
    return lax.optimization_barrier((value, other))[0]


def features_by_group(value):
    rows = lax.axis_size("row")
    chunks = jnp.split(value, rows, axis=1)
    groups = [
        jnp.concatenate([chunks[group_row(g, side)] for side in (0, 1)], axis=1) for g in range(rows // 2)
    ]
    return jnp.concatenate(by_owner(groups, own_group()[0]), axis=1)


def features_in_order(value):
    rows = lax.axis_size("row")
    groups = by_owner(jnp.split(value, rows // 2, axis=1), own_group()[0])
    chunks = [None] * rows
    for g, group in enumerate(groups):
        for side, chunk in enumerate(jnp.split(group, 2, axis=1)):
            chunks[group_row(g, side)] = chunk
    return jnp.concatenate(chunks, axis=1)


def group_gather(own, other):
    both = jnp.concatenate([own, other], axis=0)
    across = swap_col(both, 2)
    pieces = [both, swap_col(both, 1), across, swap_col(across, 1)]
    return jnp.concatenate([p for half in zip(*(jnp.split(piece, 2, axis=0) for piece in pieces)) for p in half], axis=0)


class GroupScatter:
    def __init__(self, value):
        x = jnp.split(value, 2 * lax.axis_size("col"), axis=0)
        self.kept = (x[0], x[2], x[4], x[6])
        self.came = swap_col(jnp.concatenate([x[1], x[3], x[5], x[7]], axis=0).astype(bf), 1)

    def add(self, mark):
        self.came = after(self.came, mark)
        return [a + b.astype(f32) for a, b in zip(self.kept, jnp.split(self.came, len(self.kept), axis=0))]

    def across(self, mark):
        y = self.add(mark)
        self.kept = (y[0], y[2])
        self.came = swap_col(jnp.concatenate([y[1], y[3]], axis=0).astype(bf), 2)

    def partner(self, mark):
        z = self.add(mark)
        self.kept = (z[0],)
        self.came = swap_row(z[1].astype(bf), PAIR)

    def result(self):
        return self.kept[0] + self.came.astype(f32)


def pair_halves(value, axis):
    low, high = jnp.split(value, 2, axis=axis)
    upper = own_group()[1] == 1
    return (jnp.where(upper, high, low), jnp.where(upper, low, high))


def in_pair_order(mine, came, axis):
    upper = own_group()[1] == 1
    return jnp.concatenate([jnp.where(upper, came, mine), jnp.where(upper, mine, came)], axis=axis)


class HiddenGather:
    def __init__(self, blocks):
        self.mine, self.away = pair_halves(blocks, 1)
        self.pieces = [{} for _ in range(blocks.shape[0])]

    def arrived(self, came, first, last):
        own = in_pair_order(self.mine[first:last], came, 2)
        for which in range(first, last):
            self.pieces[which][0] = (own, which - first)
        return own

    def near_own(self, own, first, last, mark):
        beside = swap_row(after(own, mark), group_masks()[-1][1])
        for which in range(first, last):
            self.pieces[which][1] = (beside, which - first)
        return beside

    def far(self, which, mark):
        own, index = self.pieces[which][0]
        moved = {0: after(own[index : index + 1], mark)}
        for bit, mask in group_masks()[:-1]:
            for k in list(moved):
                moved[k ^ bit] = swap_row(moved[k], mask)
        self.pieces[which].update((k, (piece, 0)) for k, piece in moved.items() if k)
        return [piece for k, piece in moved.items() if k]

    def near(self, which, mark):
        pieces = self.pieces[which]
        for k in [k for k in pieces if k > 1]:
            pieces[k ^ 1] = (swap_row(after(pieces[k][0], mark), group_masks()[-1][1]), 0)
        return [pieces[k] for k in range(len(pieces))]


class HiddenScatter:
    def __init__(self, left, right):
        groups = lax.axis_size("row") // 2
        chunks = jnp.split(right, groups, axis=1)
        self.kept = [k for k in range(groups) if not k & 1]
        self.away = over_rows(left, jnp.concatenate([chunks[k | 1] for k in self.kept], axis=1)).astype(bf)
        self.total = over_rows(left, jnp.concatenate([chunks[k] for k in self.kept], axis=1))

    def near(self, mark):
        self.came = swap_row(after(self.away, mark), group_masks()[-1][1])

    def add(self):
        pieces = jnp.split(self.total + self.came.astype(f32), len(self.kept), axis=1)
        return dict(zip(self.kept, pieces))

    def far(self, mark):
        for bit, mask in reversed(group_masks()[:-1]):
            self.came = after(self.came, mark)
            pieces = self.add()
            away = [k for k in self.kept if k & bit]
            self.kept = [k for k in self.kept if not k & bit]
            self.total = jnp.concatenate([pieces[k] for k in self.kept], axis=1)
            self.came = swap_row(jnp.concatenate([pieces[k] for k in away], axis=1).astype(bf), mask)

    def halves(self):
        return pair_halves(self.add()[0].astype(bf), 1)


COLS = (("col", 1), ("col", 2))
GROUP = COLS + (("row", PAIR),)


class Cube:
    def __init__(self, dims, parts):
        self.dims, self.parts = dims, parts
        self.row, self.column = lax.axis_index("row"), lax.axis_index("col")
        self.masks = range(1, 1 << len(dims))

    def device(self, mask):
        row, column = self.row, self.column
        for k, (axis, bit) in enumerate(self.dims):
            if mask >> k & 1:
                row, column = (flip(row, bit), column) if axis == "row" else (row, flip(column, bit))
        return (row, column)

    def partner(self):
        return (flip(self.row, PAIR), self.column)

    def greet(self, cargo):
        others = [self.device(1 << k) for k in range(len(self.dims))] + [self.partner()] * cargo
        barrier = pltpu.get_barrier_semaphore()
        for other in others:
            pl.semaphore_signal(barrier, inc=1, device_id=other, device_id_type=MESH)
        pl.semaphore_wait(barrier, len(others))

    def ship(self, cargo):
        return [
            pltpu.make_async_remote_copy(
                src_ref=cargo[0],
                dst_ref=cargo[1],
                send_sem=cargo[2],
                recv_sem=cargo[3],
                device_id=self.partner(),
                device_id_type=MESH,
            )
        ] if cargo else []

    def order(self, part):
        slow = list(range(1, len(self.dims)))
        return [0] + (slow[::-1] if part % 2 else slow)


def cut(ref, index, rows, width):
    if width is None:
        return ref.at[index, rows]
    return ref.at[rows, pl.ds(pl.multiple_of(index * width, 128), width)]


def unpack(cargo, refs, inputs, outputs):
    if not cargo:
        return (refs, ())
    own, swapped = refs[inputs], refs[inputs + 1 + outputs]
    rest = refs[:inputs] + refs[inputs + 1 : inputs + 1 + outputs] + refs[inputs + outputs + 2 : -2]
    return (rest, (own, swapped) + tuple(refs[-2:]))


def spread_kernel(dims, parts, lanes, relative, cargo, *refs):
    (own_ref, all_ref, own_sem, send_sem, recv_sem), cargo = unpack(cargo, refs, 1, 1)
    cube = Cube(dims, parts)
    cube.greet(len(cargo) > 0)
    ship = cube.ship(cargo)
    for copy in ship:
        copy.start()
    height, width = own_ref.shape
    size = height // parts
    width = width if lanes else None

    def index(mask):
        return mask if relative else cube.device(mask)[1]

    def rows(part):
        return pl.ds(part * size, size)

    own = pltpu.make_async_copy(own_ref, cut(all_ref, index(0), pl.ds(0, height), width), own_sem)
    own.start()

    def hop(part, mask, k):
        there = mask | 1 << k
        target = there if relative else index(mask)
        source = cut(all_ref, index(mask), rows(part), width) if mask else own_ref.at[rows(part)]
        return pltpu.make_async_remote_copy(
            src_ref=source,
            dst_ref=cut(all_ref, target, rows(part), width),
            send_sem=send_sem.at[part, there],
            recv_sem=recv_sem.at[part, there],
            device_id=cube.device(1 << k),
            device_id_type=MESH,
        )

    def arrival(part, mask):
        view = cut(all_ref, index(mask), rows(part), width)
        return pltpu.make_async_remote_copy(
            src_ref=view,
            dst_ref=view,
            send_sem=send_sem.at[part, mask],
            recv_sem=recv_sem.at[part, mask],
            device_id=cube.device(1),
            device_id_type=MESH,
        )

    sent = []
    for part in range(parts):
        for k in cube.order(part)[::-1]:
            sent.append(hop(part, 0, k))
            sent[-1].start()
    last = []
    for bits in range(1, len(dims)):
        for part in range(parts):
            order = cube.order(part)[::-1]
            for mask in cube.masks:
                if bin(mask).count("1") != bits:
                    continue
                further = order[max(order.index(k) for k in range(len(dims)) if mask >> k & 1) + 1 :]
                if not further:
                    last.append((part, mask))
                    continue
                arrival(part, mask).wait_recv()
                for k in further:
                    sent.append(hop(part, mask, k))
                    sent[-1].start()
    last += [(part, cube.masks[-1]) for part in range(parts)]
    for part, mask in last:
        arrival(part, mask).wait_recv()
    for copy in sent:
        copy.wait_send()
    own.wait()
    for copy in ship:
        copy.wait()


def cargo_parts(cargo):
    if cargo is None:
        return ([], [], [])
    anywhere = pl.BlockSpec(memory_space=pl.ANY)
    return ([anywhere], [jax.ShapeDtypeStruct(cargo.shape, cargo.dtype)], [pltpu.SemaphoreType.DMA] * 2)


def spread(own, dims, parts, number, lanes=False, relative=False, cargo=None):
    specs, shapes, semaphores = cargo_parts(cargo)
    count = 1 << len(dims)
    shape = (own.shape[0], count * own.shape[1]) if lanes else (count,) + own.shape
    whole, *swapped = pl.pallas_call(
        functools.partial(spread_kernel, dims, parts, lanes, relative, cargo is not None),
        out_shape=[jax.ShapeDtypeStruct(shape, own.dtype)] + shapes,
        in_specs=[pl.BlockSpec(memory_space=pl.ANY)] + specs,
        out_specs=[pl.BlockSpec(memory_space=pl.ANY)] + specs,
        scratch_shapes=[
            pltpu.SemaphoreType.DMA,
            pltpu.SemaphoreType.DMA((parts, count)),
            pltpu.SemaphoreType.DMA((parts, count)),
        ]
        + semaphores,
        compiler_params=pltpu.CompilerParams(collective_id=number, has_side_effects=True),
        name=f"spread{number}",
    )(*([own] if cargo is None else [own, cargo]))
    whole = whole if lanes else whole.reshape(count * own.shape[0], own.shape[1])
    return (whole, swapped[0]) if swapped else whole


def behind_kernel(reach, key_ref, all_ref, own_sem, send_sem, recv_sem):
    rows, cols = lax.axis_size("row"), lax.axis_size("col")
    row, column = lax.axis_index("row"), lax.axis_index("col")
    count = key_ref.shape[1]
    quarter = count // cols
    beside, across = (row, flip(column, 1)), (row, flip(column, 2))
    ring_barrier([((row + rows - k) % rows, column) for k in range(1, reach + 1)] + [beside, across])
    own = pltpu.make_async_copy(key_ref, all_ref.at[:, pl.ds(reach * count, count)], own_sem)
    own.start()

    def view(k, mask):
        owner = flip(flip(column, 1) if mask & 1 else column, 2) if mask & 2 else (flip(column, 1) if mask else column)
        return all_ref.at[:, pl.ds(pl.multiple_of((reach - k) * count + owner * quarter, 128), quarter)]

    def hop(k, mask, target, there, source=None):
        return pltpu.make_async_remote_copy(
            src_ref=view(k, mask) if source is None else source,
            dst_ref=view(k, mask),
            send_sem=send_sem.at[k - 1, there],
            recv_sem=recv_sem.at[k - 1, there],
            device_id=target,
            device_id_type=MESH,
        )

    mine = key_ref.at[:, pl.ds(pl.multiple_of(column * quarter, 128), quarter)]
    sent = []
    for k in range(1, reach + 1):
        sent.append(hop(k, 0, ((row + k) % rows, column), 0, mine))
        sent[-1].start()
    for k in range(1, reach + 1):
        hop(k, 0, beside, 0).wait_recv()
        sent += [hop(k, 0, across, 2), hop(k, 0, beside, 1)]
        sent[-2].start()
        sent[-1].start()
    for k in range(1, reach + 1):
        hop(k, 2, across, 2).wait_recv()
        sent.append(hop(k, 2, beside, 3))
        sent[-1].start()
    for k in range(1, reach + 1):
        hop(k, 1, beside, 1).wait_recv()
        hop(k, 3, beside, 3).wait_recv()
    for copy in sent:
        copy.wait_send()
    own.wait()


def gather_behind(key, reach):
    height, count = key.shape
    return pl.pallas_call(
        functools.partial(behind_kernel, reach),
        out_shape=jax.ShapeDtypeStruct((height, (reach + 1) * count), key.dtype),
        in_specs=[pl.BlockSpec(memory_space=pl.ANY)],
        out_specs=pl.BlockSpec(memory_space=pl.ANY),
        scratch_shapes=[
            pltpu.SemaphoreType.DMA,
            pltpu.SemaphoreType.DMA((reach, 4)),
            pltpu.SemaphoreType.DMA((reach, 4)),
        ],
        compiler_params=pltpu.CompilerParams(collective_id=2, has_side_effects=True),
        name="gather_behind",
    )(key)


def fold_kernel(dims, parts, lanes, relative, cargo, *refs):
    (terms_ref, sum_ref, arrive_ref, leave_ref, send_sem, recv_sem), cargo = unpack(cargo, refs, 1, 1)
    cube = Cube(dims, parts)
    cube.greet(len(cargo) > 0)
    ship = cube.ship(cargo)
    for copy in ship:
        copy.start()
    height, width = sum_ref.shape
    size = height // parts
    width = width if lanes else None

    def term(part, mask):
        return cut(terms_ref, mask if relative else cube.device(mask)[1], pl.ds(part * size, size), width)

    def hop(part, mask, k, source):
        return pltpu.make_async_remote_copy(
            src_ref=source,
            dst_ref=arrive_ref.at[mask, pl.ds(part * size, size)],
            send_sem=send_sem.at[part, mask],
            recv_sem=recv_sem.at[part, mask],
            device_id=cube.device(1 << k),
            device_id_type=MESH,
        )

    sent = []
    for stage in range(len(dims) + 1):
        for part in range(parts):
            rows = pl.ds(part * size, size)
            order = cube.order(part)
            done = sum(1 << k for k in order[:stage])
            if stage:
                for mask in range(1 << len(dims)):
                    if not mask & done:
                        there = mask | 1 << order[stage - 1]
                        hop(part, there, order[stage - 1], arrive_ref.at[there, rows]).wait_recv()
            going = [0] if stage == len(dims) else [m for m in cube.masks if not m & done and m >> order[stage] & 1]
            for mask in going:
                source = term(part, mask)
                if stage:
                    total = source[...].astype(f32)
                    for k in order[:stage]:
                        total = total + arrive_ref[mask | 1 << k, rows].astype(f32)
                    if mask == 0:
                        sum_ref[rows] = total
                        continue
                    leave_ref[mask, rows] = total.astype(bf)
                    source = leave_ref.at[mask, rows]
                sent.append(hop(part, mask, order[stage], source))
                sent[-1].start()
    for copy in sent:
        copy.wait_send()
    for copy in ship:
        copy.wait()


def fold(terms, dims, parts, number, lanes=False, relative=False, cargo=None):
    count = 1 << len(dims)
    terms = terms.astype(bf)
    if lanes:
        shape = (terms.shape[0], terms.shape[1] // count)
    else:
        shape = (terms.shape[0] // count, terms.shape[1])
        terms = terms.reshape((count,) + shape)
    specs, shapes, semaphores = cargo_parts(cargo)
    total, *swapped = pl.pallas_call(
        functools.partial(fold_kernel, dims, parts, lanes, relative, cargo is not None),
        out_shape=[jax.ShapeDtypeStruct(shape, f32)] + shapes,
        in_specs=[pl.BlockSpec(memory_space=pltpu.VMEM)] + specs,
        out_specs=[pl.BlockSpec(memory_space=pltpu.VMEM)] + specs,
        scratch_shapes=[
            pltpu.VMEM((count,) + shape, bf),
            pltpu.VMEM((count,) + shape, bf),
            pltpu.SemaphoreType.DMA((parts, count)),
            pltpu.SemaphoreType.DMA((parts, count)),
        ]
        + semaphores,
        compiler_params=pltpu.CompilerParams(
            collective_id=number, has_side_effects=True, vmem_limit_bytes=VMEM_LIMIT
        ),
        name=f"fold{number}",
    )(*([terms] if cargo is None else [terms, cargo]))
    return (total, swapped[0]) if swapped else total


def dot(left, right, dims):
    return lax.dot_general(left, right, (dims, ((), ())), preferred_element_type=f32)


def multiply(left, right):
    return dot(left, right, ((1,), (0,)))


def against(left, right):
    return dot(left, right, ((1,), (1,)))


def over_rows(left, right):
    return dot(left, right, ((0,), (0,)))


def inverse_of(value, axis):
    return lax.rsqrt(jnp.mean(value * value, axis=axis, keepdims=True) + EPS)


def norm_back(value, inverse, gain, upstream, axis):
    unit = value * inverse
    scaled = upstream * gain
    inward = inverse * (scaled - unit * jnp.mean(scaled * unit, axis=axis, keepdims=True))
    return (inward, jnp.sum(upstream * unit, axis=1 - axis))


def angles(start, count):
    place = ((start + jnp.arange(count, dtype=jnp.int32)) % SEQ_LEN).astype(f32)
    half = DR // 2
    freq = jnp.exp(jnp.arange(half, dtype=f32) * (-math.log(THETA) / half))
    turn = freq[:, None] * place[None, :]
    return (jnp.cos(turn), jnp.sin(turn))


def rotate(front, behind, cosine, sine):
    return (front * cosine - behind * sine, behind * cosine + front * sine)


def query_columns(heads):
    tiles = -(-heads // 4)
    column = lax.iota(jnp.int32, heads * DN + tiles * 128)
    plain = (column // DN) * (DN + DR) + column % DN
    rest = column - heads * DN
    head = (rest // 128) * 4 + (rest % 64) // 16
    turned = head * (DN + DR) + DN + ((rest % 128) // 64) * 16 + rest % 16
    turned = jnp.where(head < heads, turned, -1)
    return jnp.where(column < heads * DN, plain, turned)


def latent_columns(heads):
    column = lax.iota(jnp.int32, heads * (DN + DV))
    rest = column % (heads * DN)
    return (rest // DN) * (DN + DV) + rest % DN + (column // (heads * DN)) * DN


def chosen(origin, width):
    return lax.broadcasted_iota(jnp.int32, (width, origin.shape[0]), 0) == origin[None, :]


BLOCK = 512


def head_rows(step, side, shape, axis):
    place = lax.broadcasted_iota(jnp.int32, shape, axis)
    plain = (place // DN == side).astype(f32).astype(bf)
    turned = ((place % 64) // 16 == 2 * (step % 2) + side).astype(f32).astype(bf)
    return (plain, turned)


def attend_kernel(
    blocks, first_ref, qn_ref, qr_ref, k_ref, kr_ref, vt_ref, bias_ref, o_ref, wide_ref, lse_ref, s_ref
):
    step = pl.program_id(0)
    first = first_ref[0]
    count = qn_ref.shape[1]
    sides = (0, 1)
    rights = []
    for side in sides:
        plain, turned = head_rows(step, side, qn_ref.shape, 0)
        rights.append(jnp.concatenate([qn_ref[...] * plain, qr_ref[...] * turned], axis=0))

    def score(j, tops):
        rows = pl.ds(pl.multiple_of(j * BLOCK, BLOCK), BLOCK)
        left = jnp.concatenate([k_ref[rows, :], kr_ref[rows, :]], axis=1)
        new = []
        for side in sides:
            s = multiply(left, rights[side]) * (SCALE * LOG2E) + bias_ref[rows, :]
            s_ref[side, rows, :] = s
            new.append(jnp.maximum(tops[side], jnp.max(s, axis=0, keepdims=True)))
        return tuple(new)

    tops = lax.fori_loop(first, blocks, score, (jnp.full((1, count), NEG, f32),) * 2)

    def gather(j, carry):
        rows = pl.ds(pl.multiple_of(j * BLOCK, BLOCK), BLOCK)
        new = []
        for side in sides:
            total, out = carry[side]
            chance = jnp.exp2(s_ref[side, rows, :] - tops[side])
            total = total + jnp.sum(chance, axis=0, keepdims=True)
            out = out + multiply(vt_ref[side * DV : (side + 1) * DV, rows], chance.astype(bf))
            new.append((total, out))
        return tuple(new)

    start = (jnp.zeros((1, count), f32), jnp.zeros((DV, count), f32))
    sums = lax.fori_loop(first, blocks, gather, (start, start))
    for side in sides:
        total, out = sums[side]
        out = out / total
        o_ref[side * DV : (side + 1) * DV, :] = out.astype(bf)
        wide_ref[side * DV : (side + 1) * DV, :] = out
        lse_ref[0, side : side + 1, :] = tops[side] + jnp.log2(total)


def attend(first, query, keys, turned_keys, values_t, bias, heads):
    count, kl = query.shape[1], keys.shape[0]
    pairs, base = heads // 2, heads * DN // 128
    grid = pltpu.PrefetchScalarGridSpec(
        num_scalar_prefetch=1,
        grid=(pairs,),
        in_specs=[
            pl.BlockSpec((128, count), lambda p, s: (p, 0)),
            pl.BlockSpec((128, count), lambda p, s: (base + p // 2, 0)),
            pl.BlockSpec((kl, 128), lambda p, s: (0, p)),
            pl.BlockSpec((kl, 128), lambda p, s: (0, 0)),
            pl.BlockSpec((128, kl), lambda p, s: (p, 0)),
            pl.BlockSpec((kl, count), lambda p, s: (0, 0)),
        ],
        out_specs=[
            pl.BlockSpec((128, count), lambda p, s: (p, 0)),
            pl.BlockSpec((128, count), lambda p, s: (p, 0)),
            pl.BlockSpec((1, 2, count), lambda p, s: (p, 0, 0)),
        ],
        scratch_shapes=[pltpu.VMEM((2, kl, count), f32)],
    )
    return pl.pallas_call(
        functools.partial(attend_kernel, kl // BLOCK),
        grid_spec=grid,
        out_shape=[
            jax.ShapeDtypeStruct((heads * DV, count), bf),
            jax.ShapeDtypeStruct((heads * DV, count), f32),
            jax.ShapeDtypeStruct((pairs, 2, count), f32),
        ],
        compiler_params=pltpu.CompilerParams(vmem_limit_bytes=VMEM_LIMIT),
        name="attend",
    )(first, query, query, keys, turned_keys, values_t, bias)


def attend_back_kernel(
    blocks, first_ref, qn_ref, qr_ref, qnn_ref, qrn_ref, k_ref, kr_ref, kt_ref, krt_ref, v_ref, dot_ref, do_ref, o_ref,
    bias_ref, lse_ref, dqn_ref, dqr_ref, dk_ref, dv_ref, dkr_ref,
):
    step = pl.program_id(0)
    first = first_ref[0]
    count = qn_ref.shape[1]
    sides = (0, 1)

    @pl.when(step == 0)
    def _():
        dkr_ref[...] = jnp.zeros_like(dkr_ref)

    @pl.when(step % 2 == 0)
    def _():
        dqr_ref[...] = jnp.zeros_like(dqr_ref)

    dk_ref[...] = jnp.zeros_like(dk_ref)
    dv_ref[...] = jnp.zeros_like(dv_ref)
    rights, out_rights, query_rights, value_rights, lses, deltas = [], [], [], [], [], []
    for side in sides:
        plain, turned = head_rows(step, side, qn_ref.shape, 0)
        rights.append(jnp.concatenate([qn_ref[...] * plain, qr_ref[...] * turned], axis=0))
        out_rights.append(dot_ref[...] * plain)
        plain_l, turned_l = head_rows(step, side, qnn_ref.shape, 1)
        query_rights.append(jnp.concatenate([qnn_ref[...] * plain_l, qrn_ref[...] * turned_l], axis=1))
        value_rights.append(do_ref[...] * plain_l)
        lses.append(lse_ref[0, side : side + 1, :])
        rows = slice(side * DV, (side + 1) * DV)
        deltas.append(jnp.sum(dot_ref[rows, :].astype(f32) * o_ref[rows, :], axis=0, keepdims=True))

    def block(j, dqs):
        rows = pl.ds(pl.multiple_of(j * BLOCK, BLOCK), BLOCK)
        left = jnp.concatenate([k_ref[rows, :], kr_ref[rows, :]], axis=1)
        left_t = jnp.concatenate([kt_ref[:, rows], krt_ref[:, rows]], axis=0)
        new, dk, dv = [], 0.0, 0.0
        for side in sides:
            s = multiply(left, rights[side]) * (SCALE * LOG2E) + bias_ref[rows, :]
            chance = jnp.exp2(s - lses[side])
            back = multiply(v_ref[rows, :], out_rights[side])
            ds = (chance * (back - deltas[side])).astype(bf)
            new.append(dqs[side] + multiply(left_t, ds))
            dk = dk + multiply(ds, query_rights[side])
            dv = dv + multiply(chance.astype(bf), value_rights[side])
        dk_ref[rows, :] = (dk[:, :128] * SCALE).astype(bf)
        dkr_ref[rows, :] += dk[:, 128:] * SCALE
        dv_ref[rows, :] = dv.astype(bf)
        return tuple(new)

    dqs = lax.fori_loop(first, blocks, block, (jnp.zeros((256, count), f32),) * 2)
    place = lax.broadcasted_iota(jnp.int32, (128, count), 0)
    for side in sides:
        dq = dqs[side] * SCALE
        dqn_ref[side * DN : (side + 1) * DN, :] = dq[side * DN : (side + 1) * DN]
        dqr_ref[...] += jnp.where((place % 64) // 16 == 2 * (step % 2) + side, dq[128:], 0.0)


def attend_back(
    first, query, query_n, keys, turned_keys, keys_t, turned_keys_t, values, do_t, do, out, bias, lse, heads
):
    count, kl = query.shape[1], keys.shape[0]
    pairs, base, tiles = heads // 2, heads * DN // 128, -(-heads // 4)
    across = lambda p, s: (0, p)
    along = lambda p, s: (p, 0)
    fixed = lambda p, s: (0, 0)
    grid = pltpu.PrefetchScalarGridSpec(
        num_scalar_prefetch=1,
        grid=(pairs,),
        in_specs=[
            pl.BlockSpec((128, count), along),
            pl.BlockSpec((128, count), lambda p, s: (base + p // 2, 0)),
            pl.BlockSpec((count, 128), across),
            pl.BlockSpec((count, 128), lambda p, s: (0, base + p // 2)),
            pl.BlockSpec((kl, 128), across),
            pl.BlockSpec((kl, 128), fixed),
            pl.BlockSpec((128, kl), along),
            pl.BlockSpec((128, kl), fixed),
            pl.BlockSpec((kl, 128), across),
            pl.BlockSpec((128, count), along),
            pl.BlockSpec((count, 128), across),
            pl.BlockSpec((128, count), along),
            pl.BlockSpec((kl, count), fixed),
            pl.BlockSpec((1, 2, count), lambda p, s: (p, 0, 0)),
        ],
        out_specs=[
            pl.BlockSpec((128, count), along),
            pl.BlockSpec((128, count), lambda p, s: (p // 2, 0)),
            pl.BlockSpec((kl, 128), across),
            pl.BlockSpec((kl, 128), across),
            pl.BlockSpec((kl, 128), fixed),
        ],
    )
    return pl.pallas_call(
        functools.partial(attend_back_kernel, kl // BLOCK),
        grid_spec=grid,
        out_shape=[
            jax.ShapeDtypeStruct((heads * DN, count), f32),
            jax.ShapeDtypeStruct((tiles * 128, count), f32),
            jax.ShapeDtypeStruct((kl, heads * DN), bf),
            jax.ShapeDtypeStruct((kl, heads * DV), bf),
            jax.ShapeDtypeStruct((kl, 128), f32),
        ],
        compiler_params=pltpu.CompilerParams(vmem_limit_bytes=VMEM_LIMIT),
        name="attend_back",
    )(first, query, query, query_n, query_n, keys, turned_keys, keys_t, turned_keys_t, values, do_t, do, out, bias, lse)


TOKENS = 256


def dot_pieces(left, pieces):
    width = pieces[0].shape[2]
    total = None
    for k, piece in enumerate(pieces):
        term = against(left[:, k * width : (k + 1) * width], piece[0])
        total = term if total is None else total + term
    return total


def ffn_kernel(n, x_ref, *refs):
    gate = dot_pieces(x_ref, refs[:n])
    upward = dot_pieces(x_ref, refs[n : 2 * n])
    gate_ref, up_ref, hidden_ref = refs[2 * n :]
    gate_ref[...] = gate
    up_ref[...] = upward
    hidden_ref[...] = (gate / (1.0 + jnp.exp(-gate)) * upward).astype(bf)


def piece_specs(pieces):
    def spec(array, index):
        return pl.BlockSpec((1,) + array.shape[1:], lambda i: (index, 0, 0), pipeline_mode=pl.Buffered(1))

    return [spec(array, index) for array, index in pieces]


def ffn(x, gate, up):
    tokens, hidden = x.shape[0], gate[0][0].shape[1]
    tile = lambda width: pl.BlockSpec((TOKENS, width), lambda i: (i, 0))
    return pl.pallas_call(
        functools.partial(ffn_kernel, len(gate)),
        grid=(tokens // TOKENS,),
        out_shape=[
            jax.ShapeDtypeStruct((tokens, hidden), f32),
            jax.ShapeDtypeStruct((tokens, hidden), f32),
            jax.ShapeDtypeStruct((tokens, hidden), bf),
        ],
        in_specs=[tile(x.shape[1])] + piece_specs(gate + up),
        out_specs=[tile(hidden)] * 3,
        compiler_params=pltpu.CompilerParams(vmem_limit_bytes=VMEM_LIMIT),
        name="ffn",
    )(x, *[array for array, _ in gate + up])


def ffn_back_kernel(n, dm_ref, gate_ref, up_ref, hidden_ref, *refs):
    gates, ups, down = refs[:n], refs[n : 2 * n], refs[2 * n : 3 * n]
    dgate_ref, dup_ref, dx_ref, out_ref = refs[3 * n :]
    width = down[0].shape[2]
    back_hidden = dot_pieces(dm_ref, down)
    gate, upward = gate_ref[...], up_ref[...]
    sigma = 1.0 / (1.0 + jnp.exp(-gate))
    dgate_ref[...] = (back_hidden * upward * sigma * (1.0 + gate * (1.0 - sigma))).astype(bf)
    dup_ref[...] = (back_hidden * gate * sigma).astype(bf)
    for k in range(n):
        lanes = slice(k * width, (k + 1) * width)
        dx_ref[:, lanes] = (multiply(dgate_ref[...], gates[k][0]) + multiply(dup_ref[...], ups[k][0])).astype(bf)
        out_ref[:, lanes] = multiply(hidden_ref[...], down[k][0]).astype(bf)


def ffn_back(dm, gate, upward, hidden, pieces, n):
    tokens, units = gate.shape
    tile = lambda width: pl.BlockSpec((TOKENS, width), lambda i: (i, 0))
    return pl.pallas_call(
        functools.partial(ffn_back_kernel, n),
        grid=(tokens // TOKENS,),
        out_shape=[
            jax.ShapeDtypeStruct((tokens, units), bf),
            jax.ShapeDtypeStruct((tokens, units), bf),
            jax.ShapeDtypeStruct(dm.shape, bf),
            jax.ShapeDtypeStruct(dm.shape, bf),
        ],
        in_specs=[tile(dm.shape[1]), tile(units), tile(units), tile(units)] + piece_specs(pieces),
        out_specs=[tile(units), tile(units), tile(dm.shape[1]), tile(dm.shape[1])],
        compiler_params=pltpu.CompilerParams(vmem_limit_bytes=VMEM_LIMIT),
        name="ffn_back",
    )(dm, gate, upward, hidden, *[array for array, _ in pieces])


def shards(
    tokens, document_ids, gain_first, query_down, query_gain, latent_down, latent_gain, query_up, latent_up,
    output_weight, gain_second, gate_weight, up_weight, down_weight, cotangent,
):
    count, own_width = tokens.shape
    rows, cols = lax.axis_size("row"), lax.axis_size("col")
    row, column = lax.axis_index("row"), lax.axis_index("col")
    start = row * count
    heads = query_up.shape[1] // (DN + DR)
    reach = -(-(DOC_MOST - 1) // count)
    blocks = reach + 1
    wide = heads * DN
    quarter = count // cols
    cosine, sine = angles(start, count)

    both_down = jnp.concatenate([query_down, latent_down], axis=1).astype(bf)
    down_slice = pick(quarters(both_down, 1))
    slice_width = down_slice.shape[1]
    small = jnp.concatenate([query_gain, latent_gain]).astype(bf)
    small = jnp.pad(small, (0, gain_first.shape[0] - small.shape[0]))
    gains = jnp.stack([gain_first.astype(bf), gain_second.astype(bf), small], axis=1)
    query_one = chosen(query_columns(heads), heads * (DN + DR))
    latent_one = chosen(latent_columns(heads), heads * (DN + DV))
    query_up_low = multiply(query_up.astype(bf), query_one.astype(bf)).astype(bf)
    latent_up_low = multiply(latent_up.astype(bf), latent_one.astype(bf)).astype(bf)
    down_block = jnp.concatenate([down_slice, gains], axis=1)
    down_block = jnp.pad(down_block, ((0, 0), (0, -down_block.shape[1] % 128)))
    ffn_weights = HiddenGather(
        jnp.stack([gate_weight.astype(bf).T, up_weight.astype(bf).T, down_weight.astype(bf)])
    )
    (wide_down, wide_query_up, wide_latent_up), features, own_up, came = ring_gather(
        (down_block, query_up_low, latent_up_low), tokens, cotangent, ffn_weights.away[:1]
    )
    first_own = ffn_weights.arrived(came, 0, 1)
    own_down = features_by_group((RES * own_up).astype(bf))
    other_down = swap_row(own_down, PAIR)
    others = swap_row(after(ffn_weights.away[1:], wide_down), PAIR)
    early = (ffn_weights.near_own(first_own, 0, 1, wide_down), ffn_weights.far(0, wide_down), others, other_down)
    wide_output = lax.all_gather(after(output_weight, wide_down).astype(bf).T, "row", axis=0, tiled=True)
    gain_one = wide_down[:, slice_width].astype(f32)
    gain_two = wide_down[:, slice_width + 1].astype(f32)
    small_gains = wide_down[:, slice_width + 2].reshape(rows, -1).astype(f32)
    own_q = query_gain.shape[0]
    query_scale = small_gains[:, :own_q].reshape(-1)[:, None]
    latent_scale = small_gains[:, own_q : own_q + latent_gain.shape[0]].reshape(-1)[:, None]
    wide_down = wide_down[:, :slice_width]

    residual = features.astype(f32)
    first_in = (residual * inverse_of(residual, 1) * gain_one).astype(bf)
    own_residual = pick(quarters(features, 0)).astype(f32)

    latents = spread(dot(wide_down, first_in, ((0,), (1,))), COLS, 3, 3)
    query_latent, latent_part = latents[:QR], latents[QR : QR + KR]
    inverse_query, inverse_latent = inverse_of(query_latent, 0), inverse_of(latent_part, 0)
    query_in = (query_latent * inverse_query * query_scale).astype(bf)
    latent_in = (latent_part * inverse_latent * latent_scale).astype(bf)
    half = DR // 2
    key_front, key_back = rotate(latents[QR + KR : QR + KR + half], latents[QR + KR + half :], cosine, sine)
    key_part = jnp.concatenate([latent_in, key_front.astype(bf), key_back.astype(bf)], axis=0)
    key_parts = gather_behind(after(key_part, early), reach)
    other_own = ffn_weights.arrived(others, 1, 3)
    beside = ffn_weights.near_own(other_own, 1, 3, key_parts)
    far_up, far_down = ffn_weights.far(1, key_parts), ffn_weights.far(2, key_parts)
    back_down = group_gather(*after((own_down, other_down), key_parts))
    latent_all = key_parts[:KR]
    turned_t = jnp.concatenate([key_parts[KR : KR + half]] * 4 + [key_parts[KR + half :]] * 4, axis=0)
    turned = turned_t.T

    key_place = start - reach * count + jnp.arange(blocks * count, dtype=jnp.int32)
    place = start + jnp.arange(count, dtype=jnp.int32)
    key_doc = lax.dynamic_slice_in_dim(jnp.pad(document_ids, (reach * count, 0)), start, blocks * count)
    doc = lax.dynamic_slice_in_dim(document_ids, start, count)
    allowed = (key_doc[:, None] == doc[None, :]) & (key_place[:, None] <= place[None, :])
    allowed = allowed & (key_place[:, None] >= (place // SEQ_LEN * SEQ_LEN)[None, :])
    bias = jnp.where(allowed, 0.0, NEG).astype(f32)
    doc_start = jnp.sum((document_ids < doc[0]).astype(jnp.int32))
    first = jnp.clip((doc_start - (start - reach * count)) // BLOCK, 0, reach).reshape(1)

    raw = over_rows(wide_query_up, query_in)
    tiles = raw[wide:].reshape(-1, 2, 64, count)
    cos_tile, sin_tile = jnp.tile(cosine, (4, 1)), jnp.tile(sine, (4, 1))
    query_turned = jnp.stack(rotate(tiles[:, 0], tiles[:, 1], cos_tile, sin_tile), axis=1).reshape(-1, count)
    query = jnp.concatenate([raw[:wide], query_turned], axis=0).astype(bf)
    up_keys, up_values = wide_latent_up[:, :wide], wide_latent_up[:, wide:]
    keys = over_rows(latent_all, up_keys).astype(bf)
    values_t = over_rows(up_values, latent_all).astype(bf)
    out_t, out_wide, lse = attend(first, query, keys, turned, values_t, bias, heads)

    gate_pieces = ffn_weights.near(0, out_t)
    out_t = after(out_t, beside)
    branch = after(dot(out_t, wide_output, ((0,), (1,))), back_down)
    middle = own_residual + RES * fold(branch, COLS, 8, 4)
    middle = after(middle, far_up)
    up_pieces = ffn_weights.near(1, middle)
    middle = after(middle, far_down)
    down_pieces = ffn_weights.near(2, middle)
    inverse_second = inverse_of(middle, 1)
    second_in = features_by_group((middle * inverse_second * gain_two).astype(bf))
    second_in = spread(second_in, GROUP, 8, 5, relative=True)

    gate, upward, hidden = ffn(second_in, gate_pieces, up_pieces)
    slope_down = HiddenScatter(hidden, back_down)
    slope_down.near(hidden)
    gate = after(gate, slope_down.away)
    back_gate, back_upward, back_second, out_part = ffn_back(
        back_down, gate, upward, hidden, gate_pieces + up_pieces + down_pieces, len(gate_pieces)
    )
    slope_gate = HiddenScatter(back_gate, second_in)
    slope_gate.near(back_gate)
    back_second = after(back_second, slope_gate.away)
    back_second = features_in_order(fold(back_second, GROUP, 8, 6, relative=True))
    slope_up = HiddenScatter(back_upward, second_in)
    own_result = GroupScatter(out_part)
    back_norm, gain_second_part = norm_back(middle, inverse_second, gain_two, back_second, 1)
    back_middle = own_up + back_norm
    back_branch = after((RES * back_middle).astype(bf), (slope_down.came, own_result.came, slope_up.away))
    slope_up.near(back_branch)
    slope_down.far(back_branch)
    back_branch = spread(back_branch, COLS, 8, 7)
    own_result.across(back_branch)

    out = out_t.T
    back_out = multiply(back_branch, wide_output).astype(bf)
    slope_gate.far(back_out)
    keys_t = over_rows(up_keys, latent_all).astype(bf)
    values = over_rows(latent_all, up_values).astype(bf)
    back_query_n, back_query_r, back_keys, back_values, back_turned = attend_back(
        first, query, query.T, keys, turned, keys_t, turned_t, values, back_out.T, back_out, out_wide, bias, lse, heads
    )
    back_query_n = after(back_query_n, (slope_down.came, slope_gate.came, slope_up.came, own_result.came))
    slope_up.far(back_query_n)
    own_result.partner(back_query_n)
    tiles = back_query_r.reshape(-1, 2, 64, count)
    back_turn = jnp.stack(rotate(tiles[:, 0], tiles[:, 1], cos_tile, -sin_tile), axis=1).reshape(-1, count)
    back_raw = jnp.concatenate([back_query_n, back_turn], axis=0).astype(bf)
    query_part = multiply(wide_query_up, back_raw)
    latent_back = against(up_keys, back_keys) + against(up_values, back_values)
    turned_back = jnp.sum(back_turned.T.reshape(2, 4, half, blocks * count), axis=1).reshape(DR, blocks * count)
    far = jnp.concatenate([latent_back, turned_back], axis=0)
    to_send = jnp.concatenate(
        [query_part] + [far[:, b * count : (b + 1) * count] for b in range(blocks)], axis=0
    )
    summed = after(fold(to_send, COLS, 3, 8, lanes=True), slope_up.came)
    slope_down.came, slope_gate.came = after((slope_down.came, slope_gate.came), summed)
    own_result = middle + RES * features_in_order(own_result.result())
    back_query_in = summed[:QR]
    wide_far = KR + DR
    parts = [summed[QR + b * wide_far : QR + (b + 1) * wide_far] for b in range(blocks)]
    back_key = parts[reach]
    for step in range(1, reach + 1):
        back_key = back_key + from_behind(parts[reach - step], -step)

    own_latents = pick(quarters(latents, 1))
    own_query, own_latent = own_latents[:QR], own_latents[QR : QR + KR]
    back_query_latent, query_gain_part = norm_back(
        own_query, inverse_of(own_query, 0), query_scale, back_query_in, 0
    )
    back_latent, latent_gain_part = norm_back(
        own_latent, inverse_of(own_latent, 0), latent_scale, back_key[:KR], 0
    )
    own_cosine, own_sine = pick(quarters(cosine, 1)), pick(quarters(sine, 1))
    back_front, back_behind = rotate(back_key[KR : KR + half], back_key[KR + half :], own_cosine, -own_sine)
    back_latents = jnp.concatenate([back_query_latent, back_latent, back_front, back_behind], axis=0).astype(bf)
    back_latents = spread(back_latents, COLS, 3, 9, lanes=True)
    back_slice = lax.dynamic_slice_in_dim(back_latents, column * slice_width, slice_width, 0)
    halves = [flow.halves() for flow in (slope_down, slope_gate)]
    away = jnp.stack([gone for _, gone in halves])
    back_first, came = fold(dot(back_slice, wide_down, ((0,), (1,))), COLS, 8, 10, cargo=away)
    slope_down, slope_gate = (in_pair_order(mine, got, 0) for (mine, _), got in zip(halves, came))
    back_norm_first, gain_first_part = norm_back(own_residual, inverse_of(own_residual, 1), gain_one, back_first, 1)
    own_back = back_middle + back_norm_first

    packed = jnp.concatenate(
        [part.reshape(rows, -1) for part in (gain_first_part, gain_second_part, query_gain_part, latent_gain_part)],
        axis=1,
    )
    packed = jnp.pad(packed, ((0, 0), (0, -packed.shape[1] % 256))).reshape(-1, 128)
    back_slice_n = jnp.pad(back_slice.T, ((0, 0), (0, -slice_width % 128)))
    slope_up.came = after(slope_up.came, back_first)
    slope_up, away = slope_up.halves()
    (slope_output, slope_query_up, slope_latent_up, slope_down_slice, packed), came, (result, back_tokens) = ring_scatter((
        over_rows(back_branch, out).astype(bf),
        against(query_in, back_raw).astype(bf),
        multiply(latent_all, jnp.concatenate([back_keys, back_values], axis=1)).astype(bf),
        over_rows(first_in, back_slice_n).astype(bf),
        packed,
    ), away, (own_result, own_back))
    slope_up = in_pair_order(slope_up, came, 0)
    n, m, k = gain_first.shape[0], query_gain.shape[0], latent_gain.shape[0]
    packed = packed.reshape(-1)[: 2 * n + m + k]
    packed = jnp.pad(packed, (0, n - m - k)).reshape(3, n).T
    block = jnp.concatenate([slope_down_slice[:, :slice_width], packed], axis=1).astype(bf)
    block = jnp.pad(block, ((0, 0), (0, -block.shape[1] % 128)))
    blocks = quarters(spread(block, COLS, 2, 11, lanes=True), 1)
    slope_both = jnp.concatenate([piece[:, :slice_width] for piece in blocks], axis=1).astype(f32)
    packed = sum(piece[:, slice_width : slice_width + 3].astype(f32) for piece in blocks).T.reshape(-1)

    exact = functools.partial(
        lax.dot_general,
        dimension_numbers=(((1,), (1,)), ((), ())),
        precision=lax.Precision.HIGHEST,
        preferred_element_type=f32,
    )
    return (
        result,
        back_tokens,
        packed[:n],
        slope_both[:, :QR],
        packed[2 * n : 2 * n + m],
        slope_both[:, QR:],
        packed[2 * n + m : 2 * n + m + k],
        exact(slope_query_up, query_one.astype(f32)),
        exact(slope_latent_up, latent_one.astype(f32)),
        slope_output.T,
        packed[n : 2 * n],
        slope_gate.T.astype(f32),
        slope_up.T.astype(f32),
        slope_down.astype(f32),
    )


def solution(mesh):
    placed = (
        P("row", "col"), P(), P("row"), P("row", None), P("row"), P("row", None), P("row"), P("row", "col"),
        P("row", "col"), P("col", "row"), P("row"), P("row", "col"), P("row", "col"), P("col", "row"),
        P("row", "col"),
    )
    outs = (
        P("row", "col"), P("row", "col"), P("row"), P("row", None), P("row"), P("row", None), P("row"),
        P("row", "col"), P("row", "col"), P("col", "row"), P("row"), P("row", "col"), P("row", "col"),
        P("col", "row"),
    )
    return jax.shard_map(shards, mesh=mesh, in_specs=placed, out_specs=outs, check_vma=False)
```

```python
import functools
import math

import jax
import jax.numpy as jnp
from jax import lax
from jax.experimental import pallas as pl
from jax.experimental.pallas import tpu as pltpu
from jax.sharding import PartitionSpec as P

DN = 64
DR = 32
DV = 64
QR = 768
KR = 256
SEQ_LEN = 4096
DOC_MOST = 2000
EPS = 1e-05
RES = 1.4 / math.sqrt(62.0)
THETA = 10000.0
NEG = -1e30
LOG2E = math.log2(math.e)
SCALE = (DN + DR) ** (-0.5)
VMEM_LIMIT = 56 << 20
MESH = pl.DeviceIdType.MESH
PAIR = 2
bf = jnp.bfloat16
f32 = jnp.float32


def ring_place(row, rows):
    return row // 2 + (row % 2) * (rows - 1 - 2 * (row // 2))


def ring_row(place, rows):
    side = place // (rows // 2)
    return 2 * (place + side * (rows - 1 - 2 * place)) + side


def flip(value, bit):
    return value + bit * (1 - 2 * ((value // bit) % 2))


def ring_barrier(others):
    barrier = pltpu.get_barrier_semaphore()
    for other in others:
        pl.semaphore_signal(barrier, inc=1, device_id=other, device_id_type=MESH)
    pl.semaphore_wait(barrier, len(others))


def col_peers(column, cols):
    return [flip(flip(column, 1) if k & 1 else column, 2) if k & 2 else flip(column, 1) for k in range(1, cols)]


def ring_gather_kernel(rows, n, *refs):
    blocks, (tokens_ref, back_ref, away_ref), refs = refs[:n], refs[n : n + 3], refs[n + 3 :]
    wholes, (features_ref, own_back_ref, came_ref), refs = refs[:n], refs[n : n + 3], refs[n + 3 :]
    own_sem, send_sem, recv_sem, col_send, col_recv = refs
    row, column = lax.axis_index("row"), lax.axis_index("col")
    place = ring_place(row, rows)
    ends = (ring_row((place + 1) % rows, rows), ring_row((place + rows - 1) % rows, rows))
    cols = features_ref.shape[1] // tokens_ref.shape[1]
    quarter = back_ref.shape[0] // cols
    peers = col_peers(column, cols)
    partner = (flip(row, PAIR), column)
    ring_barrier([(ends[0], column), (ends[1], column), partner] + [(row, peer) for peer in peers])
    lanes = pl.ds(pl.multiple_of(column * tokens_ref.shape[1], 128), tokens_ref.shape[1])

    def to_col(k, target):
        part = back_ref.at[pl.ds(pl.multiple_of(target * quarter, 128), quarter)]
        return [(tokens_ref, features_ref.at[:, lanes]), (part, own_back_ref.at[:, lanes])]

    crossing = []
    for k, peer in enumerate(peers):
        for which, (source, there) in enumerate(to_col(k, peer)):
            crossing.append(
                pltpu.make_async_remote_copy(
                    src_ref=source,
                    dst_ref=there,
                    send_sem=col_send.at[which, k],
                    recv_sem=col_recv.at[which, k],
                    device_id=(row, peer),
                    device_id_type=MESH,
                )
            )
    crossing.append(
        pltpu.make_async_remote_copy(
            src_ref=away_ref,
            dst_ref=came_ref,
            send_sem=col_send.at[2, 0],
            recv_sem=col_recv.at[2, 0],
            device_id=partner,
            device_id_type=MESH,
        )
    )
    staying = [
        pltpu.make_async_copy(source, there, own_sem.at[n + which])
        for which, (source, there) in enumerate(to_col(-1, column))
    ]

    def own(k):
        return pltpu.make_async_copy(blocks[k], wholes[k].at[row], own_sem.at[k])

    def hop(step, side, k):
        origin = ring_row((place + (step if side else rows - step)) % rows, rows)
        return pltpu.make_async_remote_copy(
            src_ref=wholes[k].at[origin, side],
            dst_ref=wholes[k].at[origin, side],
            send_sem=send_sem.at[step, side, k],
            recv_sem=recv_sem.at[step, side, k],
            device_id=(ends[side], column),
            device_id_type=MESH,
        )

    for k in range(n):
        own(k).start()
    for k in range(n):
        own(k).wait()
        for side in (0, 1):
            hop(0, side, k).start()
    for copy in crossing + staying:
        copy.start()

    def advance(step, carry):
        for k in range(n):
            for side in (0, 1):
                hop(step - 1, side, k).wait_recv()
                hop(step, side, k).start()
        return carry

    lax.fori_loop(1, rows - 1, advance, 0)
    for k in range(n):
        for side in (0, 1):
            hop(rows - 2, side, k).wait_recv()

    def drain(step, carry):
        for k in range(n):
            for side in (0, 1):
                hop(step, side, k).wait_send()
        return carry

    lax.fori_loop(0, rows - 1, drain, 0)
    for copy in crossing + staying:
        copy.wait()


def ring_gather(blocks, tokens, back, away):
    rows, cols, n = lax.axis_size("row"), lax.axis_size("col"), len(blocks)
    halves = [block.reshape(2, block.shape[0] // 2, block.shape[1]) for block in blocks]
    anywhere = pl.BlockSpec(memory_space=pl.ANY)
    *wholes, features, own_back, came = pl.pallas_call(
        functools.partial(ring_gather_kernel, rows, n),
        out_shape=[jax.ShapeDtypeStruct((rows,) + half.shape, half.dtype) for half in halves]
        + [
            jax.ShapeDtypeStruct((tokens.shape[0], cols * tokens.shape[1]), tokens.dtype),
            jax.ShapeDtypeStruct((back.shape[0] // cols, cols * back.shape[1]), back.dtype),
            jax.ShapeDtypeStruct(away.shape, away.dtype),
        ],
        in_specs=[anywhere] * (n + 3),
        out_specs=[anywhere] * (n + 3),
        scratch_shapes=[
            pltpu.SemaphoreType.DMA((n + 2,)),
            pltpu.SemaphoreType.DMA((rows - 1, 2, n)),
            pltpu.SemaphoreType.DMA((rows - 1, 2, n)),
            pltpu.SemaphoreType.DMA((3, cols - 1)),
            pltpu.SemaphoreType.DMA((3, cols - 1)),
        ],
        compiler_params=pltpu.CompilerParams(collective_id=0, has_side_effects=True),
        name="ring_gather",
    )(*halves, tokens, back, away)
    wholes = [whole.reshape(rows * block.shape[0], block.shape[1]) for whole, block in zip(wholes, blocks)]
    return wholes, features, own_back, came


def ring_scatter_kernel(rows, n, extra, *refs):
    terms, away_ref, leaving, refs = refs[:n], refs[n], refs[n + 1 : n + 1 + extra], refs[n + 1 + extra :]
    sums, came_ref, arriving, refs = refs[:n], refs[n], refs[n + 1 : n + 1 + extra], refs[n + 1 + extra :]
    slots, refs = refs[:n], refs[n:]
    send_sem, recv_sem, swap_send, swap_recv, own_sem, col_send, col_recv = refs
    row, column = lax.axis_index("row"), lax.axis_index("col")
    place = ring_place(row, rows)
    ends = (ring_row((place + 1) % rows, rows), ring_row((place + rows - 1) % rows, rows))
    partner = (flip(row, PAIR), column)
    cols = lax.axis_size("col")
    peers = col_peers(column, cols)
    ring_barrier([(ends[0], column), (ends[1], column), partner] + [(row, peer) for peer in peers])
    crossing = []
    for e in range(extra):
        quarter, width = leaving[e].shape[0], leaving[e].shape[1] // cols
        place_there = arriving[e].at[pl.ds(pl.multiple_of(column * quarter, 128), quarter)]

        def features(target):
            return leaving[e].at[:, pl.ds(pl.multiple_of(target * width, 128), width)]

        crossing.append(pltpu.make_async_copy(features(column), place_there, own_sem.at[e]))
        for k, peer in enumerate(peers):
            crossing.append(
                pltpu.make_async_remote_copy(
                    src_ref=features(peer),
                    dst_ref=place_there,
                    send_sem=col_send.at[e, k],
                    recv_sem=col_recv.at[e, k],
                    device_id=(row, peer),
                    device_id_type=MESH,
                )
            )
    swap = pltpu.make_async_remote_copy(
        src_ref=away_ref,
        dst_ref=came_ref,
        send_sem=swap_send,
        recv_sem=swap_recv,
        device_id=partner,
        device_id_type=MESH,
    )

    def target(step, side):
        return ring_row((place + (1 + step if side else 2 * rows - 1 - step)) % rows, rows)

    def hop(step, side, k, source):
        return pltpu.make_async_remote_copy(
            src_ref=source,
            dst_ref=slots[k].at[step, side],
            send_sem=send_sem.at[step, side, k],
            recv_sem=recv_sem.at[step, side, k],
            device_id=(ends[side], column),
            device_id_type=MESH,
        )

    def first(side, k):
        return hop(0, side, k, terms[k].at[target(0, side), side])

    def later(step, side, k):
        return hop(step, side, k, slots[k].at[step - 1, side])

    for k in range(n):
        for side in (0, 1):
            first(side, k).start()
    swap.start()
    for copy in crossing:
        copy.start()

    def arrive(step, side, k):
        return hop(step, side, k, slots[k].at[step, side])

    def advance(step, carry):
        for k in range(n):
            for side in (0, 1):
                arrive(step - 1, side, k).wait_recv()
                total = slots[k][step - 1, side].astype(f32) + terms[k][target(step, side), side].astype(f32)
                slots[k][step - 1, side] = total.astype(slots[k].dtype)
                later(step, side, k).start()
        return carry

    lax.fori_loop(1, rows - 1, advance, 0)
    for k in range(n):
        for side in (0, 1):
            arrive(rows - 2, side, k).wait_recv()
            sums[k][side] = slots[k][rows - 2, side].astype(f32) + terms[k][row, side].astype(f32)

    def drain(step, carry):
        for k in range(n):
            for side in (0, 1):
                arrive(step, side, k).wait_send()
        return carry

    lax.fori_loop(0, rows - 1, drain, 0)
    swap.wait()
    for copy in crossing:
        copy.wait()


def ring_scatter(terms, away, leaving):
    rows, n = lax.axis_size("row"), len(terms)
    split = [term.reshape(rows, 2, term.shape[0] // rows // 2, term.shape[1]) for term in terms]
    anywhere = pl.BlockSpec(memory_space=pl.ANY)
    cols, extra = lax.axis_size("col"), len(leaving)
    *sums, came, first, second = pl.pallas_call(
        functools.partial(ring_scatter_kernel, rows, n, extra),
        out_shape=[jax.ShapeDtypeStruct(term.shape[1:], f32) for term in split]
        + [jax.ShapeDtypeStruct(away.shape, away.dtype)]
        + [jax.ShapeDtypeStruct((v.shape[0] * cols, v.shape[1] // cols), v.dtype) for v in leaving],
        in_specs=[pl.BlockSpec(memory_space=pltpu.VMEM)] * n + [anywhere] * (1 + extra),
        out_specs=[pl.BlockSpec(memory_space=pltpu.VMEM)] * n + [anywhere] * (1 + extra),
        scratch_shapes=[pltpu.VMEM((rows - 1,) + term.shape[1:], term.dtype) for term in split]
        + [pltpu.SemaphoreType.DMA((rows - 1, 2, n)), pltpu.SemaphoreType.DMA((rows - 1, 2, n))]
        + [pltpu.SemaphoreType.DMA, pltpu.SemaphoreType.DMA, pltpu.SemaphoreType.DMA((extra,))]
        + [pltpu.SemaphoreType.DMA((extra, cols - 1)), pltpu.SemaphoreType.DMA((extra, cols - 1))],
        compiler_params=pltpu.CompilerParams(
            collective_id=1, has_side_effects=True, vmem_limit_bytes=VMEM_LIMIT
        ),
        name="ring_scatter",
    )(*split, away, *leaving)
    return [total.reshape(total.shape[0] * total.shape[1], total.shape[2]) for total in sums], came, (first, second)


def from_behind(value, steps):
    count = lax.axis_size("row")
    initial, last = (max(0, -steps), min(count, count - steps))
    return lax.ppermute(value, "row", [(source, source + steps) for source in range(initial, last)])


def swap_col(value, bit):
    return lax.ppermute(value, "col", [(c, c ^ bit) for c in range(lax.axis_size("col"))])


def by_owner(pieces, own=None):
    own = lax.axis_index("col") if own is None else own
    bit = 1
    pieces = list(pieces)
    while bit < len(pieces):
        odd = (own // bit) % 2 == 1
        pieces = [jnp.where(odd, pieces[k ^ bit], pieces[k]) for k in range(len(pieces))]
        bit *= 2
    return pieces


def pick(pieces):
    return by_owner(pieces)[0]


def col_gather(own):
    across = swap_col(own, 2)
    beside = swap_col(own, 1)
    return by_owner([own, beside, across, swap_col(across, 1)])


def col_scatter(pieces):
    mine = by_owner(pieces)
    low = [piece.astype(bf) for piece in mine]
    across = mine[2].astype(f32) + swap_col(low[3], 1).astype(f32)
    beside = mine[0].astype(f32) + swap_col(low[1], 1).astype(f32)
    return beside + swap_col(across.astype(bf), 2).astype(f32)


def quarters(value, axis):
    return jnp.split(value, lax.axis_size("col"), axis=axis)


def group_row(group, side):
    return (group // 2) * 4 + side * PAIR + group % 2


def own_group():
    row = lax.axis_index("row")
    return ((row // 4) * 2 + row % 2, (row // PAIR) % 2)


def swap_row(value, mask):
    return lax.ppermute(value, "row", [(r, r ^ mask) for r in range(lax.axis_size("row"))])


def group_masks():
    bits = (lax.axis_size("row") // 2).bit_length() - 1
    return [(1 << b, group_row(1 << b, 0)) for b in reversed(range(bits))]


def after(value, other):
    return lax.optimization_barrier((value, other))[0]


def features_by_group(value):
    rows = lax.axis_size("row")
    chunks = jnp.split(value, rows, axis=1)
    groups = [
        jnp.concatenate([chunks[group_row(g, side)] for side in (0, 1)], axis=1) for g in range(rows // 2)
    ]
    return jnp.concatenate(by_owner(groups, own_group()[0]), axis=1)


def features_in_order(value):
    rows = lax.axis_size("row")
    groups = by_owner(jnp.split(value, rows // 2, axis=1), own_group()[0])
    chunks = [None] * rows
    for g, group in enumerate(groups):
        for side, chunk in enumerate(jnp.split(group, 2, axis=1)):
            chunks[group_row(g, side)] = chunk
    return jnp.concatenate(chunks, axis=1)


def group_gather(own, other):
    both = jnp.concatenate([own, other], axis=0)
    across = swap_col(both, 2)
    pieces = [both, swap_col(both, 1), across, swap_col(across, 1)]
    return jnp.concatenate([p for half in zip(*(jnp.split(piece, 2, axis=0) for piece in pieces)) for p in half], axis=0)


class GroupScatter:
    def __init__(self, value):
        x = jnp.split(value, 2 * lax.axis_size("col"), axis=0)
        self.kept = (x[0], x[2], x[4], x[6])
        self.came = swap_col(jnp.concatenate([x[1], x[3], x[5], x[7]], axis=0).astype(bf), 1)

    def add(self, mark):
        self.came = after(self.came, mark)
        return [a + b.astype(f32) for a, b in zip(self.kept, jnp.split(self.came, len(self.kept), axis=0))]

    def across(self, mark):
        y = self.add(mark)
        self.kept = (y[0], y[2])
        self.came = swap_col(jnp.concatenate([y[1], y[3]], axis=0).astype(bf), 2)

    def partner(self, mark):
        z = self.add(mark)
        self.kept = (z[0],)
        self.came = swap_row(z[1].astype(bf), PAIR)

    def result(self):
        return self.kept[0] + self.came.astype(f32)


def pair_halves(value, axis):
    low, high = jnp.split(value, 2, axis=axis)
    upper = own_group()[1] == 1
    return (jnp.where(upper, high, low), jnp.where(upper, low, high))


def in_pair_order(mine, came, axis):
    upper = own_group()[1] == 1
    return jnp.concatenate([jnp.where(upper, came, mine), jnp.where(upper, mine, came)], axis=axis)


class HiddenGather:
    def __init__(self, blocks):
        self.mine, self.away = pair_halves(blocks, 1)
        self.pieces = [{} for _ in range(blocks.shape[0])]

    def arrived(self, came, first, last):
        own = in_pair_order(self.mine[first:last], came, 2)
        for which in range(first, last):
            self.pieces[which][0] = (own, which - first)
        return own

    def near_own(self, own, first, last, mark):
        beside = swap_row(after(own, mark), group_masks()[-1][1])
        for which in range(first, last):
            self.pieces[which][1] = (beside, which - first)
        return beside

    def far(self, which, mark):
        own, index = self.pieces[which][0]
        moved = {0: after(own[index : index + 1], mark)}
        for bit, mask in group_masks()[:-1]:
            for k in list(moved):
                moved[k ^ bit] = swap_row(moved[k], mask)
        self.pieces[which].update((k, (piece, 0)) for k, piece in moved.items() if k)
        return [piece for k, piece in moved.items() if k]

    def near(self, which, mark):
        pieces = self.pieces[which]
        for k in [k for k in pieces if k > 1]:
            pieces[k ^ 1] = (swap_row(after(pieces[k][0], mark), group_masks()[-1][1]), 0)
        return [pieces[k] for k in range(len(pieces))]


class HiddenScatter:
    def __init__(self, left, right):
        groups = lax.axis_size("row") // 2
        chunks = jnp.split(right, groups, axis=1)
        self.kept = [k for k in range(groups) if not k & 1]
        self.away = over_rows(left, jnp.concatenate([chunks[k | 1] for k in self.kept], axis=1)).astype(bf)
        self.total = over_rows(left, jnp.concatenate([chunks[k] for k in self.kept], axis=1))

    def near(self, mark):
        self.came = swap_row(after(self.away, mark), group_masks()[-1][1])

    def add(self):
        pieces = jnp.split(self.total + self.came.astype(f32), len(self.kept), axis=1)
        return dict(zip(self.kept, pieces))

    def far(self, mark):
        for bit, mask in reversed(group_masks()[:-1]):
            self.came = after(self.came, mark)
            pieces = self.add()
            away = [k for k in self.kept if k & bit]
            self.kept = [k for k in self.kept if not k & bit]
            self.total = jnp.concatenate([pieces[k] for k in self.kept], axis=1)
            self.came = swap_row(jnp.concatenate([pieces[k] for k in away], axis=1).astype(bf), mask)

    def halves(self):
        return pair_halves(self.add()[0].astype(bf), 1)


COLS = (("col", 1), ("col", 2))
GROUP = COLS + (("row", PAIR),)


class Cube:
    def __init__(self, dims, parts):
        self.dims, self.parts = dims, parts
        self.row, self.column = lax.axis_index("row"), lax.axis_index("col")
        self.masks = range(1, 1 << len(dims))

    def device(self, mask):
        row, column = self.row, self.column
        for k, (axis, bit) in enumerate(self.dims):
            if mask >> k & 1:
                row, column = (flip(row, bit), column) if axis == "row" else (row, flip(column, bit))
        return (row, column)

    def partner(self):
        return (flip(self.row, PAIR), self.column)

    def greet(self, cargo):
        others = [self.device(1 << k) for k in range(len(self.dims))] + [self.partner()] * cargo
        barrier = pltpu.get_barrier_semaphore()
        for other in others:
            pl.semaphore_signal(barrier, inc=1, device_id=other, device_id_type=MESH)
        pl.semaphore_wait(barrier, len(others))

    def ship(self, cargo):
        return [
            pltpu.make_async_remote_copy(
                src_ref=cargo[0],
                dst_ref=cargo[1],
                send_sem=cargo[2],
                recv_sem=cargo[3],
                device_id=self.partner(),
                device_id_type=MESH,
            )
        ] if cargo else []

    def order(self, part):
        slow = list(range(1, len(self.dims)))
        return [0] + (slow[::-1] if part % 2 else slow)


def cut(ref, index, rows, width):
    if width is None:
        return ref.at[index, rows]
    return ref.at[rows, pl.ds(pl.multiple_of(index * width, 128), width)]


def unpack(cargo, refs, inputs, outputs):
    if not cargo:
        return (refs, ())
    own, swapped = refs[inputs], refs[inputs + 1 + outputs]
    rest = refs[:inputs] + refs[inputs + 1 : inputs + 1 + outputs] + refs[inputs + outputs + 2 : -2]
    return (rest, (own, swapped) + tuple(refs[-2:]))


def spread_kernel(dims, parts, lanes, relative, cargo, *refs):
    (own_ref, all_ref, own_sem, send_sem, recv_sem), cargo = unpack(cargo, refs, 1, 1)
    cube = Cube(dims, parts)
    cube.greet(len(cargo) > 0)
    ship = cube.ship(cargo)
    for copy in ship:
        copy.start()
    height, width = own_ref.shape
    size = height // parts
    width = width if lanes else None

    def index(mask):
        return mask if relative else cube.device(mask)[1]

    def rows(part):
        return pl.ds(part * size, size)

    own = pltpu.make_async_copy(own_ref, cut(all_ref, index(0), pl.ds(0, height), width), own_sem)
    own.start()

    def hop(part, mask, k):
        there = mask | 1 << k
        target = there if relative else index(mask)
        source = cut(all_ref, index(mask), rows(part), width) if mask else own_ref.at[rows(part)]
        return pltpu.make_async_remote_copy(
            src_ref=source,
            dst_ref=cut(all_ref, target, rows(part), width),
            send_sem=send_sem.at[part, there],
            recv_sem=recv_sem.at[part, there],
            device_id=cube.device(1 << k),
            device_id_type=MESH,
        )

    def arrival(part, mask):
        view = cut(all_ref, index(mask), rows(part), width)
        return pltpu.make_async_remote_copy(
            src_ref=view,
            dst_ref=view,
            send_sem=send_sem.at[part, mask],
            recv_sem=recv_sem.at[part, mask],
            device_id=cube.device(1),
            device_id_type=MESH,
        )

    sent = []
    for part in range(parts):
        for k in cube.order(part)[::-1]:
            sent.append(hop(part, 0, k))
            sent[-1].start()
    last = []
    for bits in range(1, len(dims)):
        for part in range(parts):
            order = cube.order(part)[::-1]
            for mask in cube.masks:
                if bin(mask).count("1") != bits:
                    continue
                further = order[max(order.index(k) for k in range(len(dims)) if mask >> k & 1) + 1 :]
                if not further:
                    last.append((part, mask))
                    continue
                arrival(part, mask).wait_recv()
                for k in further:
                    sent.append(hop(part, mask, k))
                    sent[-1].start()
    last += [(part, cube.masks[-1]) for part in range(parts)]
    for part, mask in last:
        arrival(part, mask).wait_recv()
    for copy in sent:
        copy.wait_send()
    own.wait()
    for copy in ship:
        copy.wait()


def cargo_parts(cargo):
    if cargo is None:
        return ([], [], [])
    anywhere = pl.BlockSpec(memory_space=pl.ANY)
    return ([anywhere], [jax.ShapeDtypeStruct(cargo.shape, cargo.dtype)], [pltpu.SemaphoreType.DMA] * 2)


def spread(own, dims, parts, number, lanes=False, relative=False, cargo=None):
    specs, shapes, semaphores = cargo_parts(cargo)
    count = 1 << len(dims)
    shape = (own.shape[0], count * own.shape[1]) if lanes else (count,) + own.shape
    whole, *swapped = pl.pallas_call(
        functools.partial(spread_kernel, dims, parts, lanes, relative, cargo is not None),
        out_shape=[jax.ShapeDtypeStruct(shape, own.dtype)] + shapes,
        in_specs=[pl.BlockSpec(memory_space=pl.ANY)] + specs,
        out_specs=[pl.BlockSpec(memory_space=pl.ANY)] + specs,
        scratch_shapes=[
            pltpu.SemaphoreType.DMA,
            pltpu.SemaphoreType.DMA((parts, count)),
            pltpu.SemaphoreType.DMA((parts, count)),
        ]
        + semaphores,
        compiler_params=pltpu.CompilerParams(collective_id=number, has_side_effects=True),
        name=f"spread{number}",
    )(*([own] if cargo is None else [own, cargo]))
    whole = whole if lanes else whole.reshape(count * own.shape[0], own.shape[1])
    return (whole, swapped[0]) if swapped else whole


def behind_kernel(reach, key_ref, all_ref, own_sem, send_sem, recv_sem):
    rows, cols = lax.axis_size("row"), lax.axis_size("col")
    row, column = lax.axis_index("row"), lax.axis_index("col")
    count = key_ref.shape[1]
    quarter = count // cols
    beside, across = (row, flip(column, 1)), (row, flip(column, 2))
    ring_barrier([((row + rows - k) % rows, column) for k in range(1, reach + 1)] + [beside, across])
    own = pltpu.make_async_copy(key_ref, all_ref.at[:, pl.ds(reach * count, count)], own_sem)
    own.start()

    def view(k, mask):
        owner = flip(flip(column, 1) if mask & 1 else column, 2) if mask & 2 else (flip(column, 1) if mask else column)
        return all_ref.at[:, pl.ds(pl.multiple_of((reach - k) * count + owner * quarter, 128), quarter)]

    def hop(k, mask, target, there, source=None):
        return pltpu.make_async_remote_copy(
            src_ref=view(k, mask) if source is None else source,
            dst_ref=view(k, mask),
            send_sem=send_sem.at[k - 1, there],
            recv_sem=recv_sem.at[k - 1, there],
            device_id=target,
            device_id_type=MESH,
        )

    mine = key_ref.at[:, pl.ds(pl.multiple_of(column * quarter, 128), quarter)]
    sent = []
    for k in range(1, reach + 1):
        sent.append(hop(k, 0, ((row + k) % rows, column), 0, mine))
        sent[-1].start()
    for k in range(1, reach + 1):
        hop(k, 0, beside, 0).wait_recv()
        sent += [hop(k, 0, across, 2), hop(k, 0, beside, 1)]
        sent[-2].start()
        sent[-1].start()
    for k in range(1, reach + 1):
        hop(k, 2, across, 2).wait_recv()
        sent.append(hop(k, 2, beside, 3))
        sent[-1].start()
    for k in range(1, reach + 1):
        hop(k, 1, beside, 1).wait_recv()
        hop(k, 3, beside, 3).wait_recv()
    for copy in sent:
        copy.wait_send()
    own.wait()


def gather_behind(key, reach):
    height, count = key.shape
    return pl.pallas_call(
        functools.partial(behind_kernel, reach),
        out_shape=jax.ShapeDtypeStruct((height, (reach + 1) * count), key.dtype),
        in_specs=[pl.BlockSpec(memory_space=pl.ANY)],
        out_specs=pl.BlockSpec(memory_space=pl.ANY),
        scratch_shapes=[
            pltpu.SemaphoreType.DMA,
            pltpu.SemaphoreType.DMA((reach, 4)),
            pltpu.SemaphoreType.DMA((reach, 4)),
        ],
        compiler_params=pltpu.CompilerParams(collective_id=2, has_side_effects=True),
        name="gather_behind",
    )(key)


def fold_kernel(dims, parts, lanes, relative, cargo, *refs):
    (terms_ref, sum_ref, arrive_ref, leave_ref, send_sem, recv_sem), cargo = unpack(cargo, refs, 1, 1)
    cube = Cube(dims, parts)
    cube.greet(len(cargo) > 0)
    ship = cube.ship(cargo)
    for copy in ship:
        copy.start()
    height, width = sum_ref.shape
    size = height // parts
    width = width if lanes else None

    def term(part, mask):
        return cut(terms_ref, mask if relative else cube.device(mask)[1], pl.ds(part * size, size), width)

    def hop(part, mask, k, source):
        return pltpu.make_async_remote_copy(
            src_ref=source,
            dst_ref=arrive_ref.at[mask, pl.ds(part * size, size)],
            send_sem=send_sem.at[part, mask],
            recv_sem=recv_sem.at[part, mask],
            device_id=cube.device(1 << k),
            device_id_type=MESH,
        )

    sent = []
    for stage in range(len(dims) + 1):
        for part in range(parts):
            rows = pl.ds(part * size, size)
            order = cube.order(part)
            done = sum(1 << k for k in order[:stage])
            if stage:
                for mask in range(1 << len(dims)):
                    if not mask & done:
                        there = mask | 1 << order[stage - 1]
                        hop(part, there, order[stage - 1], arrive_ref.at[there, rows]).wait_recv()
            going = [0] if stage == len(dims) else [m for m in cube.masks if not m & done and m >> order[stage] & 1]
            for mask in going:
                source = term(part, mask)
                if stage:
                    total = source[...].astype(f32)
                    for k in order[:stage]:
                        total = total + arrive_ref[mask | 1 << k, rows].astype(f32)
                    if mask == 0:
                        sum_ref[rows] = total
                        continue
                    leave_ref[mask, rows] = total.astype(bf)
                    source = leave_ref.at[mask, rows]
                sent.append(hop(part, mask, order[stage], source))
                sent[-1].start()
    for copy in sent:
        copy.wait_send()
    for copy in ship:
        copy.wait()


def fold(terms, dims, parts, number, lanes=False, relative=False, cargo=None):
    count = 1 << len(dims)
    terms = terms.astype(bf)
    if lanes:
        shape = (terms.shape[0], terms.shape[1] // count)
    else:
        shape = (terms.shape[0] // count, terms.shape[1])
        terms = terms.reshape((count,) + shape)
    specs, shapes, semaphores = cargo_parts(cargo)
    total, *swapped = pl.pallas_call(
        functools.partial(fold_kernel, dims, parts, lanes, relative, cargo is not None),
        out_shape=[jax.ShapeDtypeStruct(shape, f32)] + shapes,
        in_specs=[pl.BlockSpec(memory_space=pltpu.VMEM)] + specs,
        out_specs=[pl.BlockSpec(memory_space=pltpu.VMEM)] + specs,
        scratch_shapes=[
            pltpu.VMEM((count,) + shape, bf),
            pltpu.VMEM((count,) + shape, bf),
            pltpu.SemaphoreType.DMA((parts, count)),
            pltpu.SemaphoreType.DMA((parts, count)),
        ]
        + semaphores,
        compiler_params=pltpu.CompilerParams(
            collective_id=number, has_side_effects=True, vmem_limit_bytes=VMEM_LIMIT
        ),
        name=f"fold{number}",
    )(*([terms] if cargo is None else [terms, cargo]))
    return (total, swapped[0]) if swapped else total


def dot(left, right, dims):
    return lax.dot_general(left, right, (dims, ((), ())), preferred_element_type=f32)


def multiply(left, right):
    return dot(left, right, ((1,), (0,)))


def against(left, right):
    return dot(left, right, ((1,), (1,)))


def over_rows(left, right):
    return dot(left, right, ((0,), (0,)))


def inverse_of(value, axis):
    return lax.rsqrt(jnp.mean(value * value, axis=axis, keepdims=True) + EPS)


def norm_back(value, inverse, gain, upstream, axis):
    unit = value * inverse
    scaled = upstream * gain
    inward = inverse * (scaled - unit * jnp.mean(scaled * unit, axis=axis, keepdims=True))
    return (inward, jnp.sum(upstream * unit, axis=1 - axis))


def angles(start, count):
    place = ((start + jnp.arange(count, dtype=jnp.int32)) % SEQ_LEN).astype(f32)
    half = DR // 2
    freq = jnp.exp(jnp.arange(half, dtype=f32) * (-math.log(THETA) / half))
    turn = freq[:, None] * place[None, :]
    return (jnp.cos(turn), jnp.sin(turn))


def rotate(front, behind, cosine, sine):
    return (front * cosine - behind * sine, behind * cosine + front * sine)


def query_columns(heads):
    tiles = -(-heads // 4)
    column = lax.iota(jnp.int32, heads * DN + tiles * 128)
    plain = (column // DN) * (DN + DR) + column % DN
    rest = column - heads * DN
    head = (rest // 128) * 4 + (rest % 64) // 16
    turned = head * (DN + DR) + DN + ((rest % 128) // 64) * 16 + rest % 16
    turned = jnp.where(head < heads, turned, -1)
    return jnp.where(column < heads * DN, plain, turned)


def latent_columns(heads):
    column = lax.iota(jnp.int32, heads * (DN + DV))
    rest = column % (heads * DN)
    return (rest // DN) * (DN + DV) + rest % DN + (column // (heads * DN)) * DN


def chosen(origin, width):
    return lax.broadcasted_iota(jnp.int32, (width, origin.shape[0]), 0) == origin[None, :]


BLOCK = 512


def head_rows(step, side, shape, axis):
    place = lax.broadcasted_iota(jnp.int32, shape, axis)
    plain = (place // DN == side).astype(f32).astype(bf)
    turned = ((place % 64) // 16 == 2 * (step % 2) + side).astype(f32).astype(bf)
    return (plain, turned)


def attend_kernel(
    blocks, first_ref, qn_ref, qr_ref, k_ref, kr_ref, vt_ref, bias_ref, o_ref, wide_ref, lse_ref, s_ref
):
    step = pl.program_id(0)
    first = first_ref[0]
    count = qn_ref.shape[1]
    sides = (0, 1)
    rights = []
    for side in sides:
        plain, turned = head_rows(step, side, qn_ref.shape, 0)
        rights.append(jnp.concatenate([qn_ref[...] * plain, qr_ref[...] * turned], axis=0))

    def score(j, tops):
        rows = pl.ds(pl.multiple_of(j * BLOCK, BLOCK), BLOCK)
        left = jnp.concatenate([k_ref[rows, :], kr_ref[rows, :]], axis=1)
        new = []
        for side in sides:
            s = multiply(left, rights[side]) * (SCALE * LOG2E) + bias_ref[rows, :]
            s_ref[side, rows, :] = s
            new.append(jnp.maximum(tops[side], jnp.max(s, axis=0, keepdims=True)))
        return tuple(new)

    tops = lax.fori_loop(first, blocks, score, (jnp.full((1, count), NEG, f32),) * 2)

    def gather(j, carry):
        rows = pl.ds(pl.multiple_of(j * BLOCK, BLOCK), BLOCK)
        new = []
        for side in sides:
            total, out = carry[side]
            chance = jnp.exp2(s_ref[side, rows, :] - tops[side])
            total = total + jnp.sum(chance, axis=0, keepdims=True)
            out = out + multiply(vt_ref[side * DV : (side + 1) * DV, rows], chance.astype(bf))
            new.append((total, out))
        return tuple(new)

    start = (jnp.zeros((1, count), f32), jnp.zeros((DV, count), f32))
    sums = lax.fori_loop(first, blocks, gather, (start, start))
    for side in sides:
        total, out = sums[side]
        out = out / total
        o_ref[side * DV : (side + 1) * DV, :] = out.astype(bf)
        wide_ref[side * DV : (side + 1) * DV, :] = out
        lse_ref[0, side : side + 1, :] = tops[side] + jnp.log2(total)


def attend(first, query, keys, turned_keys, values_t, bias, heads):
    count, kl = query.shape[1], keys.shape[0]
    pairs, base = heads // 2, heads * DN // 128
    grid = pltpu.PrefetchScalarGridSpec(
        num_scalar_prefetch=1,
        grid=(pairs,),
        in_specs=[
            pl.BlockSpec((128, count), lambda p, s: (p, 0)),
            pl.BlockSpec((128, count), lambda p, s: (base + p // 2, 0)),
            pl.BlockSpec((kl, 128), lambda p, s: (0, p)),
            pl.BlockSpec((kl, 128), lambda p, s: (0, 0)),
            pl.BlockSpec((128, kl), lambda p, s: (p, 0)),
            pl.BlockSpec((kl, count), lambda p, s: (0, 0)),
        ],
        out_specs=[
            pl.BlockSpec((128, count), lambda p, s: (p, 0)),
            pl.BlockSpec((128, count), lambda p, s: (p, 0)),
            pl.BlockSpec((1, 2, count), lambda p, s: (p, 0, 0)),
        ],
        scratch_shapes=[pltpu.VMEM((2, kl, count), f32)],
    )
    return pl.pallas_call(
        functools.partial(attend_kernel, kl // BLOCK),
        grid_spec=grid,
        out_shape=[
            jax.ShapeDtypeStruct((heads * DV, count), bf),
            jax.ShapeDtypeStruct((heads * DV, count), f32),
            jax.ShapeDtypeStruct((pairs, 2, count), f32),
        ],
        compiler_params=pltpu.CompilerParams(vmem_limit_bytes=VMEM_LIMIT),
        name="attend",
    )(first, query, query, keys, turned_keys, values_t, bias)


def attend_back_kernel(
    blocks, first_ref, qn_ref, qr_ref, qnn_ref, qrn_ref, k_ref, kr_ref, kt_ref, krt_ref, v_ref, dot_ref, do_ref, o_ref,
    bias_ref, lse_ref, dqn_ref, dqr_ref, dk_ref, dv_ref, dkr_ref,
):
    step = pl.program_id(0)
    first = first_ref[0]
    count = qn_ref.shape[1]
    sides = (0, 1)

    @pl.when(step == 0)
    def _():
        dkr_ref[...] = jnp.zeros_like(dkr_ref)

    @pl.when(step % 2 == 0)
    def _():
        dqr_ref[...] = jnp.zeros_like(dqr_ref)

    dk_ref[...] = jnp.zeros_like(dk_ref)
    dv_ref[...] = jnp.zeros_like(dv_ref)
    rights, out_rights, query_rights, value_rights, lses, deltas = [], [], [], [], [], []
    for side in sides:
        plain, turned = head_rows(step, side, qn_ref.shape, 0)
        rights.append(jnp.concatenate([qn_ref[...] * plain, qr_ref[...] * turned], axis=0))
        out_rights.append(dot_ref[...] * plain)
        plain_l, turned_l = head_rows(step, side, qnn_ref.shape, 1)
        query_rights.append(jnp.concatenate([qnn_ref[...] * plain_l, qrn_ref[...] * turned_l], axis=1))
        value_rights.append(do_ref[...] * plain_l)
        lses.append(lse_ref[0, side : side + 1, :])
        rows = slice(side * DV, (side + 1) * DV)
        deltas.append(jnp.sum(dot_ref[rows, :].astype(f32) * o_ref[rows, :], axis=0, keepdims=True))

    def block(j, dqs):
        rows = pl.ds(pl.multiple_of(j * BLOCK, BLOCK), BLOCK)
        left = jnp.concatenate([k_ref[rows, :], kr_ref[rows, :]], axis=1)
        left_t = jnp.concatenate([kt_ref[:, rows], krt_ref[:, rows]], axis=0)
        new, dk, dv = [], 0.0, 0.0
        for side in sides:
            s = multiply(left, rights[side]) * (SCALE * LOG2E) + bias_ref[rows, :]
            chance = jnp.exp2(s - lses[side])
            back = multiply(v_ref[rows, :], out_rights[side])
            ds = (chance * (back - deltas[side])).astype(bf)
            new.append(dqs[side] + multiply(left_t, ds))
            dk = dk + multiply(ds, query_rights[side])
            dv = dv + multiply(chance.astype(bf), value_rights[side])
        dk_ref[rows, :] = (dk[:, :128] * SCALE).astype(bf)
        dkr_ref[rows, :] += dk[:, 128:] * SCALE
        dv_ref[rows, :] = dv.astype(bf)
        return tuple(new)

    dqs = lax.fori_loop(first, blocks, block, (jnp.zeros((256, count), f32),) * 2)
    place = lax.broadcasted_iota(jnp.int32, (128, count), 0)
    for side in sides:
        dq = dqs[side] * SCALE
        dqn_ref[side * DN : (side + 1) * DN, :] = dq[side * DN : (side + 1) * DN]
        dqr_ref[...] += jnp.where((place % 64) // 16 == 2 * (step % 2) + side, dq[128:], 0.0)


def attend_back(
    first, query, query_n, keys, turned_keys, keys_t, turned_keys_t, values, do_t, do, out, bias, lse, heads
):
    count, kl = query.shape[1], keys.shape[0]
    pairs, base, tiles = heads // 2, heads * DN // 128, -(-heads // 4)
    across = lambda p, s: (0, p)
    along = lambda p, s: (p, 0)
    fixed = lambda p, s: (0, 0)
    grid = pltpu.PrefetchScalarGridSpec(
        num_scalar_prefetch=1,
        grid=(pairs,),
        in_specs=[
            pl.BlockSpec((128, count), along),
            pl.BlockSpec((128, count), lambda p, s: (base + p // 2, 0)),
            pl.BlockSpec((count, 128), across),
            pl.BlockSpec((count, 128), lambda p, s: (0, base + p // 2)),
            pl.BlockSpec((kl, 128), across),
            pl.BlockSpec((kl, 128), fixed),
            pl.BlockSpec((128, kl), along),
            pl.BlockSpec((128, kl), fixed),
            pl.BlockSpec((kl, 128), across),
            pl.BlockSpec((128, count), along),
            pl.BlockSpec((count, 128), across),
            pl.BlockSpec((128, count), along),
            pl.BlockSpec((kl, count), fixed),
            pl.BlockSpec((1, 2, count), lambda p, s: (p, 0, 0)),
        ],
        out_specs=[
            pl.BlockSpec((128, count), along),
            pl.BlockSpec((128, count), lambda p, s: (p // 2, 0)),
            pl.BlockSpec((kl, 128), across),
            pl.BlockSpec((kl, 128), across),
            pl.BlockSpec((kl, 128), fixed),
        ],
    )
    return pl.pallas_call(
        functools.partial(attend_back_kernel, kl // BLOCK),
        grid_spec=grid,
        out_shape=[
            jax.ShapeDtypeStruct((heads * DN, count), f32),
            jax.ShapeDtypeStruct((tiles * 128, count), f32),
            jax.ShapeDtypeStruct((kl, heads * DN), bf),
            jax.ShapeDtypeStruct((kl, heads * DV), bf),
            jax.ShapeDtypeStruct((kl, 128), f32),
        ],
        compiler_params=pltpu.CompilerParams(vmem_limit_bytes=VMEM_LIMIT),
        name="attend_back",
    )(first, query, query, query_n, query_n, keys, turned_keys, keys_t, turned_keys_t, values, do_t, do, out, bias, lse)


TOKENS = 256


def dot_pieces(left, pieces):
    width = pieces[0].shape[2]
    total = None
    for k, piece in enumerate(pieces):
        term = against(left[:, k * width : (k + 1) * width], piece[0])
        total = term if total is None else total + term
    return total


def ffn_kernel(n, x_ref, *refs):
    gate = dot_pieces(x_ref, refs[:n])
    upward = dot_pieces(x_ref, refs[n : 2 * n])
    gate_ref, up_ref, hidden_ref = refs[2 * n :]
    gate_ref[...] = gate
    up_ref[...] = upward
    hidden_ref[...] = (gate / (1.0 + jnp.exp(-gate)) * upward).astype(bf)


def piece_specs(pieces):
    def spec(array, index):
        return pl.BlockSpec((1,) + array.shape[1:], lambda i: (index, 0, 0), pipeline_mode=pl.Buffered(1))

    return [spec(array, index) for array, index in pieces]


def ffn(x, gate, up):
    tokens, hidden = x.shape[0], gate[0][0].shape[1]
    tile = lambda width: pl.BlockSpec((TOKENS, width), lambda i: (i, 0))
    return pl.pallas_call(
        functools.partial(ffn_kernel, len(gate)),
        grid=(tokens // TOKENS,),
        out_shape=[
            jax.ShapeDtypeStruct((tokens, hidden), f32),
            jax.ShapeDtypeStruct((tokens, hidden), f32),
            jax.ShapeDtypeStruct((tokens, hidden), bf),
        ],
        in_specs=[tile(x.shape[1])] + piece_specs(gate + up),
        out_specs=[tile(hidden)] * 3,
        compiler_params=pltpu.CompilerParams(vmem_limit_bytes=VMEM_LIMIT),
        name="ffn",
    )(x, *[array for array, _ in gate + up])


def ffn_back_kernel(n, dm_ref, gate_ref, up_ref, hidden_ref, *refs):
    gates, ups, down = refs[:n], refs[n : 2 * n], refs[2 * n : 3 * n]
    dgate_ref, dup_ref, dx_ref, out_ref = refs[3 * n :]
    width = down[0].shape[2]
    back_hidden = dot_pieces(dm_ref, down)
    gate, upward = gate_ref[...], up_ref[...]
    sigma = 1.0 / (1.0 + jnp.exp(-gate))
    dgate_ref[...] = (back_hidden * upward * sigma * (1.0 + gate * (1.0 - sigma))).astype(bf)
    dup_ref[...] = (back_hidden * gate * sigma).astype(bf)
    for k in range(n):
        lanes = slice(k * width, (k + 1) * width)
        dx_ref[:, lanes] = (multiply(dgate_ref[...], gates[k][0]) + multiply(dup_ref[...], ups[k][0])).astype(bf)
        out_ref[:, lanes] = multiply(hidden_ref[...], down[k][0]).astype(bf)


def ffn_back(dm, gate, upward, hidden, pieces, n):
    tokens, units = gate.shape
    tile = lambda width: pl.BlockSpec((TOKENS, width), lambda i: (i, 0))
    return pl.pallas_call(
        functools.partial(ffn_back_kernel, n),
        grid=(tokens // TOKENS,),
        out_shape=[
            jax.ShapeDtypeStruct((tokens, units), bf),
            jax.ShapeDtypeStruct((tokens, units), bf),
            jax.ShapeDtypeStruct(dm.shape, bf),
            jax.ShapeDtypeStruct(dm.shape, bf),
        ],
        in_specs=[tile(dm.shape[1]), tile(units), tile(units), tile(units)] + piece_specs(pieces),
        out_specs=[tile(units), tile(units), tile(dm.shape[1]), tile(dm.shape[1])],
        compiler_params=pltpu.CompilerParams(vmem_limit_bytes=VMEM_LIMIT),
        name="ffn_back",
    )(dm, gate, upward, hidden, *[array for array, _ in pieces])


def shards(
    tokens, document_ids, gain_first, query_down, query_gain, latent_down, latent_gain, query_up, latent_up,
    output_weight, gain_second, gate_weight, up_weight, down_weight, cotangent,
):
    count, own_width = tokens.shape
    rows, cols = lax.axis_size("row"), lax.axis_size("col")
    row, column = lax.axis_index("row"), lax.axis_index("col")
    start = row * count
    heads = query_up.shape[1] // (DN + DR)
    reach = -(-(DOC_MOST - 1) // count)
    blocks = reach + 1
    wide = heads * DN
    quarter = count // cols
    cosine, sine = angles(start, count)

    both_down = jnp.concatenate([query_down, latent_down], axis=1).astype(bf)
    down_slice = pick(quarters(both_down, 1))
    slice_width = down_slice.shape[1]
    small = jnp.concatenate([query_gain, latent_gain]).astype(bf)
    small = jnp.pad(small, (0, gain_first.shape[0] - small.shape[0]))
    gains = jnp.stack([gain_first.astype(bf), gain_second.astype(bf), small], axis=1)
    query_one = chosen(query_columns(heads), heads * (DN + DR))
    latent_one = chosen(latent_columns(heads), heads * (DN + DV))
    query_up_low = multiply(query_up.astype(bf), query_one.astype(bf)).astype(bf)
    latent_up_low = multiply(latent_up.astype(bf), latent_one.astype(bf)).astype(bf)
    down_block = jnp.concatenate([down_slice, gains], axis=1)
    down_block = jnp.pad(down_block, ((0, 0), (0, -down_block.shape[1] % 128)))
    ffn_weights = HiddenGather(
        jnp.stack([gate_weight.astype(bf).T, up_weight.astype(bf).T, down_weight.astype(bf)])
    )
    (wide_down, wide_query_up, wide_latent_up), features, own_up, came = ring_gather(
        (down_block, query_up_low, latent_up_low), tokens, cotangent, ffn_weights.away[:1]
    )
    first_own = ffn_weights.arrived(came, 0, 1)
    own_down = features_by_group((RES * own_up).astype(bf))
    other_down = swap_row(own_down, PAIR)
    others = swap_row(after(ffn_weights.away[1:], wide_down), PAIR)
    early = (ffn_weights.near_own(first_own, 0, 1, wide_down), ffn_weights.far(0, wide_down), others, other_down)
    wide_output = lax.all_gather(after(output_weight, wide_down).astype(bf).T, "row", axis=0, tiled=True)
    gain_one = wide_down[:, slice_width].astype(f32)
    gain_two = wide_down[:, slice_width + 1].astype(f32)
    small_gains = wide_down[:, slice_width + 2].reshape(rows, -1).astype(f32)
    own_q = query_gain.shape[0]
    query_scale = small_gains[:, :own_q].reshape(-1)[:, None]
    latent_scale = small_gains[:, own_q : own_q + latent_gain.shape[0]].reshape(-1)[:, None]
    wide_down = wide_down[:, :slice_width]

    residual = features.astype(f32)
    first_in = (residual * inverse_of(residual, 1) * gain_one).astype(bf)
    own_residual = pick(quarters(features, 0)).astype(f32)

    latents = spread(dot(wide_down, first_in, ((0,), (1,))), COLS, 3, 3)
    query_latent, latent_part = latents[:QR], latents[QR : QR + KR]
    inverse_query, inverse_latent = inverse_of(query_latent, 0), inverse_of(latent_part, 0)
    query_in = (query_latent * inverse_query * query_scale).astype(bf)
    latent_in = (latent_part * inverse_latent * latent_scale).astype(bf)
    half = DR // 2
    key_front, key_back = rotate(latents[QR + KR : QR + KR + half], latents[QR + KR + half :], cosine, sine)
    key_part = jnp.concatenate([latent_in, key_front.astype(bf), key_back.astype(bf)], axis=0)
    key_parts = gather_behind(after(key_part, early), reach)
    other_own = ffn_weights.arrived(others, 1, 3)
    beside = ffn_weights.near_own(other_own, 1, 3, key_parts)
    far_up, far_down = ffn_weights.far(1, key_parts), ffn_weights.far(2, key_parts)
    back_down = group_gather(*after((own_down, other_down), key_parts))
    latent_all = key_parts[:KR]
    turned_t = jnp.concatenate([key_parts[KR : KR + half]] * 4 + [key_parts[KR + half :]] * 4, axis=0)
    turned = turned_t.T

    key_place = start - reach * count + jnp.arange(blocks * count, dtype=jnp.int32)
    place = start + jnp.arange(count, dtype=jnp.int32)
    key_doc = lax.dynamic_slice_in_dim(jnp.pad(document_ids, (reach * count, 0)), start, blocks * count)
    doc = lax.dynamic_slice_in_dim(document_ids, start, count)
    allowed = (key_doc[:, None] == doc[None, :]) & (key_place[:, None] <= place[None, :])
    allowed = allowed & (key_place[:, None] >= (place // SEQ_LEN * SEQ_LEN)[None, :])
    bias = jnp.where(allowed, 0.0, NEG).astype(f32)
    doc_start = jnp.sum((document_ids < doc[0]).astype(jnp.int32))
    first = jnp.clip((doc_start - (start - reach * count)) // BLOCK, 0, reach).reshape(1)

    raw = over_rows(wide_query_up, query_in)
    tiles = raw[wide:].reshape(-1, 2, 64, count)
    cos_tile, sin_tile = jnp.tile(cosine, (4, 1)), jnp.tile(sine, (4, 1))
    query_turned = jnp.stack(rotate(tiles[:, 0], tiles[:, 1], cos_tile, sin_tile), axis=1).reshape(-1, count)
    query = jnp.concatenate([raw[:wide], query_turned], axis=0).astype(bf)
    up_keys, up_values = wide_latent_up[:, :wide], wide_latent_up[:, wide:]
    keys = over_rows(latent_all, up_keys).astype(bf)
    values_t = over_rows(up_values, latent_all).astype(bf)
    out_t, out_wide, lse = attend(first, query, keys, turned, values_t, bias, heads)

    gate_pieces = ffn_weights.near(0, out_t)
    out_t = after(out_t, beside)
    branch = after(dot(out_t, wide_output, ((0,), (1,))), back_down)
    middle = own_residual + RES * fold(branch, COLS, 8, 4)
    middle = after(middle, far_up)
    up_pieces = ffn_weights.near(1, middle)
    middle = after(middle, far_down)
    down_pieces = ffn_weights.near(2, middle)
    inverse_second = inverse_of(middle, 1)
    second_in = features_by_group((middle * inverse_second * gain_two).astype(bf))
    second_in = spread(second_in, GROUP, 8, 5, relative=True)

    gate, upward, hidden = ffn(second_in, gate_pieces, up_pieces)
    slope_down = HiddenScatter(hidden, back_down)
    slope_down.near(hidden)
    gate = after(gate, slope_down.away)
    back_gate, back_upward, back_second, out_part = ffn_back(
        back_down, gate, upward, hidden, gate_pieces + up_pieces + down_pieces, len(gate_pieces)
    )
    slope_gate = HiddenScatter(back_gate, second_in)
    slope_gate.near(back_gate)
    back_second = after(back_second, slope_gate.away)
    back_second = features_in_order(fold(back_second, GROUP, 8, 6, relative=True))
    slope_up = HiddenScatter(back_upward, second_in)
    own_result = GroupScatter(out_part)
    back_norm, gain_second_part = norm_back(middle, inverse_second, gain_two, back_second, 1)
    back_middle = own_up + back_norm
    back_branch = after((RES * back_middle).astype(bf), (slope_down.came, own_result.came, slope_up.away))
    slope_up.near(back_branch)
    slope_down.far(back_branch)
    back_branch = spread(back_branch, COLS, 8, 7)
    own_result.across(back_branch)

    out = out_t.T
    back_out = multiply(back_branch, wide_output).astype(bf)
    slope_gate.far(back_out)
    keys_t = over_rows(up_keys, latent_all).astype(bf)
    values = over_rows(latent_all, up_values).astype(bf)
    back_query_n, back_query_r, back_keys, back_values, back_turned = attend_back(
        first, query, query.T, keys, turned, keys_t, turned_t, values, back_out.T, back_out, out_wide, bias, lse, heads
    )
    back_query_n = after(back_query_n, (slope_down.came, slope_gate.came, slope_up.came, own_result.came))
    slope_up.far(back_query_n)
    own_result.partner(back_query_n)
    tiles = back_query_r.reshape(-1, 2, 64, count)
    back_turn = jnp.stack(rotate(tiles[:, 0], tiles[:, 1], cos_tile, -sin_tile), axis=1).reshape(-1, count)
    back_raw = jnp.concatenate([back_query_n, back_turn], axis=0).astype(bf)
    query_part = multiply(wide_query_up, back_raw)
    latent_back = against(up_keys, back_keys) + against(up_values, back_values)
    turned_back = jnp.sum(back_turned.T.reshape(2, 4, half, blocks * count), axis=1).reshape(DR, blocks * count)
    far = jnp.concatenate([latent_back, turned_back], axis=0)
    to_send = jnp.concatenate(
        [query_part] + [far[:, b * count : (b + 1) * count] for b in range(blocks)], axis=0
    )
    summed = after(fold(to_send, COLS, 3, 8, lanes=True), slope_up.came)
    slope_down.came, slope_gate.came = after((slope_down.came, slope_gate.came), summed)
    own_result = middle + RES * features_in_order(own_result.result())
    back_query_in = summed[:QR]
    wide_far = KR + DR
    parts = [summed[QR + b * wide_far : QR + (b + 1) * wide_far] for b in range(blocks)]
    back_key = parts[reach]
    for step in range(1, reach + 1):
        back_key = back_key + from_behind(parts[reach - step], -step)

    own_latents = pick(quarters(latents, 1))
    own_query, own_latent = own_latents[:QR], own_latents[QR : QR + KR]
    back_query_latent, query_gain_part = norm_back(
        own_query, inverse_of(own_query, 0), query_scale, back_query_in, 0
    )
    back_latent, latent_gain_part = norm_back(
        own_latent, inverse_of(own_latent, 0), latent_scale, back_key[:KR], 0
    )
    own_cosine, own_sine = pick(quarters(cosine, 1)), pick(quarters(sine, 1))
    back_front, back_behind = rotate(back_key[KR : KR + half], back_key[KR + half :], own_cosine, -own_sine)
    back_latents = jnp.concatenate([back_query_latent, back_latent, back_front, back_behind], axis=0).astype(bf)
    slope_down, away = slope_down.halves()
    back_latents, came = spread(back_latents, COLS, 3, 9, lanes=True, cargo=away)
    slope_down = in_pair_order(slope_down, came, 0)
    back_slice = lax.dynamic_slice_in_dim(back_latents, column * slice_width, slice_width, 0)
    slope_gate, away = slope_gate.halves()
    back_first, came = fold(dot(back_slice, wide_down, ((0,), (1,))), COLS, 8, 10, cargo=away)
    slope_gate = in_pair_order(slope_gate, came, 0)
    back_norm_first, gain_first_part = norm_back(own_residual, inverse_of(own_residual, 1), gain_one, back_first, 1)
    own_back = back_middle + back_norm_first

    packed = jnp.concatenate(
        [part.reshape(rows, -1) for part in (gain_first_part, gain_second_part, query_gain_part, latent_gain_part)],
        axis=1,
    )
    packed = jnp.pad(packed, ((0, 0), (0, -packed.shape[1] % 256))).reshape(-1, 128)
    back_slice_n = jnp.pad(back_slice.T, ((0, 0), (0, -slice_width % 128)))
    slope_up.came = after(slope_up.came, back_first)
    slope_up, away = slope_up.halves()
    (slope_output, slope_query_up, slope_latent_up, slope_down_slice, packed), came, (result, back_tokens) = ring_scatter((
        over_rows(back_branch, out).astype(bf),
        against(query_in, back_raw).astype(bf),
        multiply(latent_all, jnp.concatenate([back_keys, back_values], axis=1)).astype(bf),
        over_rows(first_in, back_slice_n).astype(bf),
        packed,
    ), away, (own_result, own_back))
    slope_up = in_pair_order(slope_up, came, 0)
    n, m, k = gain_first.shape[0], query_gain.shape[0], latent_gain.shape[0]
    packed = packed.reshape(-1)[: 2 * n + m + k]
    packed = jnp.pad(packed, (0, n - m - k)).reshape(3, n).T
    block = jnp.concatenate([slope_down_slice[:, :slice_width], packed], axis=1).astype(bf)
    block = jnp.pad(block, ((0, 0), (0, -block.shape[1] % 128)))
    blocks = quarters(spread(block, COLS, 2, 11, lanes=True), 1)
    slope_both = jnp.concatenate([piece[:, :slice_width] for piece in blocks], axis=1).astype(f32)
    packed = sum(piece[:, slice_width : slice_width + 3].astype(f32) for piece in blocks).T.reshape(-1)

    exact = functools.partial(
        lax.dot_general,
        dimension_numbers=(((1,), (1,)), ((), ())),
        precision=lax.Precision.HIGH,
        preferred_element_type=f32,
    )
    return (
        result,
        back_tokens,
        packed[:n],
        slope_both[:, :QR],
        packed[2 * n : 2 * n + m],
        slope_both[:, QR:],
        packed[2 * n + m : 2 * n + m + k],
        exact(slope_query_up, query_one.astype(f32)),
        exact(slope_latent_up, latent_one.astype(f32)),
        slope_output.T,
        packed[n : 2 * n],
        slope_gate.T.astype(f32),
        slope_up.T.astype(f32),
        slope_down.astype(f32),
    )


def solution(mesh):
    placed = (
        P("row", "col"), P(), P("row"), P("row", None), P("row"), P("row", None), P("row"), P("row", "col"),
        P("row", "col"), P("col", "row"), P("row"), P("row", "col"), P("row", "col"), P("col", "row"),
        P("row", "col"),
    )
    outs = (
        P("row", "col"), P("row", "col"), P("row"), P("row", None), P("row"), P("row", None), P("row"),
        P("row", "col"), P("row", "col"), P("col", "row"), P("row"), P("row", "col"), P("row", "col"),
        P("col", "row"),
    )
    return jax.shard_map(shards, mesh=mesh, in_specs=placed, out_specs=outs, check_vma=False)
```
